32 devices in a mesh: seq: 8 (over z, y), mp: 4 (over x, core).
Axes of the slice: x: 2, y: 2, z: 4, core: 2. Of those that a mesh axis runs over, the one named last changes fastest.
Arguments:
- tokens: bfloat16 [4096, 768], P('seq'), may hold values from -6 to 6
- item_lengths: int32 [8], replicated, may hold values from 1 to 2048, 4096 in all
- w_qkv: bfloat16 [3, 768, 768], P(None, None, 'mp'), may hold values from -2 to 2
- b_qv: float32 [2, 768], P(None, 'mp'), may hold values from -2 to 2
- taps: float32 [12, 33], P('mp'), may hold values from -0.072 to 0.072
- w_out: bfloat16 [768, 768], P('mp'), may hold values from -1.75 to 1.75
- b_out: float32 [768], replicated, may hold values from -3 to 3
- ln1_gain: float32 [768], replicated, may hold values from 0.5 to 1.5
- ln1_bias: float32 [768], replicated, may hold values from -2 to 2
- w_up: bfloat16 [768, 3072], P(None, 'mp'), may hold values from -0.21875 to 0.21875
- b_up: float32 [3072], P('mp'), may hold values from -3 to 3
- w_down: bfloat16 [3072, 768], P('mp'), may hold values from -0.109375 to 0.109375
- b_down: float32 [768], replicated, may hold values from -3 to 3
- ln2_gain: float32 [768], replicated, may hold values from 0.5 to 1.5
- ln2_bias: float32 [768], replicated, may hold values from -2 to 2
- d_out: bfloat16 [4096, 768], P('seq'), may hold values from -6 to 6
Outputs:
- layer_output: bfloat16 [4096, 768], P('seq')
- d_tokens: bfloat16 [4096, 768], P('seq')
- d_w_qkv: float32 [3, 768, 768], P(None, None, 'mp')
- d_b_qv: float32 [2, 768], P(None, 'mp')
- d_taps: float32 [12, 33], P('mp')
- d_w_out: float32 [768, 768], P('mp')
- d_b_out: float32 [768], replicated
- d_ln1_gain: float32 [768], replicated
- d_ln1_bias: float32 [768], replicated
- d_w_up: float32 [768, 3072], P(None, 'mp')
- d_b_up: float32 [3072], P('mp')
- d_w_down: float32 [3072, 768], P('mp')
- d_b_down: float32 [768], replicated
- d_ln2_gain: float32 [768], replicated
- d_ln2_bias: float32 [768], replicated
The draws below stay inside these ranges and needn't reach their ends.
Inputs may be any that keep to these rules, and one draw needn't show every extreme that they name: `item_lengths`: the lengths sum to 4096; the largest is exactly 2048, and no item is longer than 4096.
All inputs are finite; a program needn't handle non-finite values.
Results may differ from the reference program's by a relative error of at most 0.017.
Values may be sent and summed in bfloat16 or wider, within the bound.
No kernel may reach another device: no remote copies, remote signals or barrier semaphores. Data moves between devices by JAX's collectives and lax.ppermute only.
A program may use at most 192 MiB of HBM per device.

```python
import math
import jax
import jax.numpy as jnp
import numpy as np
from jax import lax

D = 768
H = 12
FF = 3072
KW = 33
TOK_DEV = 512
TOKENS = 4096
ITEMS = 8
LONG = 2048


def draw_w_qkv(key, part):
    base_key = jax.random.fold_in(key, 11)
    level_key = jax.random.fold_in(key, 12)
    base = jax.random.truncated_normal(base_key, -4.0, 4.0, (3, D, D), jnp.float32)
    spread = math.log(4.0)
    level = jax.random.uniform(level_key, (D,), jnp.float32, -spread, spread)
    column = jnp.exp(level) * math.sqrt(4.0 * spread / (16.0 - 1.0 / 16.0))
    ones = jnp.ones((D,), jnp.float32)
    scales = jnp.stack([column, column, ones])
    return (base * scales[:, None, :] * D ** (-0.5)).astype(jnp.bfloat16)


def draw_b_qv(key, part):
    raw_key = jax.random.fold_in(key, 21)
    raw = jax.random.truncated_normal(raw_key, -4.0, 4.0, (2, D), jnp.float32)
    rows = jnp.array([0.5, 0.03], jnp.float32)
    return raw * rows[:, None]


def level_of(stream_key, dims, shards, least, high):
    def one(dim, blocks):
        draws = jax.random.uniform(jax.random.fold_in(jax.random.fold_in(stream_key, 6), dim), (blocks,), jnp.float32, least / len(shards), high / len(shards))
        return jnp.repeat(jnp.exp(draws), dims[dim] // blocks).reshape((-1,) + (1,) * (len(dims) - dim - 1))

    level = one(*shards[0])
    for cut in shards[1:]:
        level = level * one(*cut)
    return level


def split_up(count, total, most, lean):
    portions = [(1 << 20) // math.isqrt(grade ** lean) + 1 for grade in range(2, count + 1)]
    spare, counts = total - most - (count - 1), [1] * (count - 1)
    while spare > 0:
        movable = [i for i in range(count - 1) if counts[i] < most]
        mass, left = sum([portions[i] for i in movable]), spare
        for i in movable:
            extra = min(most - counts[i], max(1, left * portions[i] // mass), spare)
            counts[i] = counts[i] + extra
            spare = spare - extra
    return np.array([most] + counts)


def ragged_sizes(key, number_of, total, limit, lean):
    if number_of == 2:
        one = jax.random.randint(key, (), max(1, total - limit), min(limit, total - 1) + 1)
        return jnp.stack([one, total - one])
    tallies = jnp.asarray(split_up(number_of, total, limit, lean), jnp.int32)
    couples = (number_of - 1) // 2
    donor, taker = tallies[1:1 + 2 * couples:2], tallies[2:2 + 2 * couples:2]
    margin = jnp.minimum(donor - 1, limit - taker)
    moved = jax.random.randint(jax.random.fold_in(key, 1), (couples,), 0, 1 << 20) % (margin + 1)
    tallies = tallies.at[1:1 + 2 * couples:2].set(donor - moved).at[2:2 + 2 * couples:2].set(taker + moved)
    return tallies[jax.random.permutation(jax.random.fold_in(key, 2), number_of)]


def gaussian(rng, dims, scale, limit, split=(), held_as=jnp.bfloat16):
    values = jax.random.normal(rng, dims, jnp.float32) * scale
    if len(split) > 0:
        values = level_of(rng, dims, split, -0.22, 0.18) * values
    return jnp.clip(values, min=-limit, max=limit).astype(held_as)


def setup_inputs(seed: int = 0) -> dict:
    streams_of = jax.random.split(jax.random.key(seed), 17)
    return {
        "tokens": gaussian(streams_of[0], (TOKENS, D), 1.0, 6.0, ((0, 8),)),
        "item_lengths": ragged_sizes(streams_of[1], ITEMS, TOKENS, LONG, 2).astype(jnp.int32),
        "w_qkv": draw_w_qkv(jax.random.fold_in(streams_of[16], 71), 0),
        "b_qv": draw_b_qv(jax.random.fold_in(streams_of[16], 71), 0),
        "taps": gaussian(streams_of[4], (H, KW), 0.012, 0.072, ((0, 4),), jnp.float32),
        "w_out": gaussian(streams_of[5], (D, D), H ** -0.5, 1.75, ((0, 4),)),
        "b_out": gaussian(streams_of[6], (D,), 0.5, 3.0, (), jnp.float32),
        "ln1_gain": jnp.clip(1.0 + 0.1 * jax.random.normal(streams_of[7], (D,), jnp.float32), 0.5, 1.5),
        "ln1_bias": gaussian(streams_of[8], (D,), 0.3, 2.0, (), jnp.float32),
        "w_up": gaussian(streams_of[9], (D, FF), D ** -0.5, 0.21875, ((1, 4),)),
        "b_up": gaussian(streams_of[10], (FF,), 0.5, 3.0, ((0, 4),), jnp.float32),
        "w_down": gaussian(streams_of[11], (FF, D), FF ** -0.5, 0.109375, ((0, 4),)),
        "b_down": gaussian(streams_of[12], (D,), 0.5, 3.0, (), jnp.float32),
        "ln2_gain": jnp.clip(1.0 + 0.1 * jax.random.normal(streams_of[13], (D,), jnp.float32), 0.5, 1.5),
        "ln2_bias": gaussian(streams_of[14], (D,), 0.3, 2.0, (), jnp.float32),
        "d_out": gaussian(streams_of[15], (TOKENS, D), 1.0, 6.0, ((0, 8),)),
    }


@jax.custom_vjp
def low(v):
    return lax.optimization_barrier(v.astype(jnp.bfloat16)).astype(jnp.float32)

@jax.custom_vjp
def low_back(v):
    return v

def low_keep(v):
    return (low(v), None)

def low_pass(kept, grad):
    return (grad,)

def back_keep(v):
    return (v, None)

def back_low(kept, grad):
    return (low(grad),)
low.defvjp(low_keep, low_pass)
low_back.defvjp(back_keep, back_low)
SHRINK = 0.95
NORM_EPS = 1e-06
LAYER_EPS = 1e-05
HIGHEST = lax.Precision.HIGHEST

def item_index(positions, ends):
    inside = (positions >= 0) & (positions < ends[-1])
    counted = lax.optimization_barrier(jnp.sum((positions[:, None] >= ends[None, :]).astype(jnp.int32), axis=1))
    return jnp.where(inside, counted, -1).astype(jnp.int32)

def layer_norm(hidden, gain, shift):
    center = hidden - lax.optimization_barrier(jnp.mean(hidden, axis=-1, keepdims=True))
    return center * lax.rsqrt(lax.optimization_barrier(jnp.mean(center * center, axis=-1, keepdims=True)) + LAYER_EPS) * gain + shift

def unit_rows(raw):
    return raw * lax.rsqrt(lax.optimization_barrier(jnp.sum(raw * raw, axis=-1, keepdims=True)) + NORM_EPS)

def attend_block(query_block, block_items, key_low, value_low, items):
    scores = low_back(jnp.einsum('bhe,khe->hbk', query_block, key_low, precision=HIGHEST))
    same = (block_items[:, None] == items[None, :]).astype(jnp.float32)
    closeness = 1.0 - jnp.arccos(SHRINK * scores) / math.pi
    weights = low(same[None] * closeness ** 8)
    return jnp.einsum('hbk,khe->bhe', weights, value_low, precision=HIGHEST)

def reference(tokens, item_lengths, w_qkv, b_qv, taps, w_out, b_out, ln1_gain, ln1_bias, w_up, b_up, w_down, b_down, ln2_gain, ln2_bias, d_out):
    total = tokens.shape[0]
    heads_all = taps.shape[0]
    kernel = taps.shape[1]
    radius = (kernel - 1) // 2
    head_size = w_qkv.shape[2] // heads_all
    ends = jnp.cumsum(item_lengths).astype(jnp.int32)
    items = item_index(jnp.arange(total, dtype=jnp.int32), ends)
    border = jnp.full((radius,), -1, jnp.int32)
    rim_items = jnp.concatenate([border, items, border])
    block = TOK_DEV
    blocks = total // block
    checked = jax.checkpoint(attend_block)

    def forward(x, wq, bq, tp, wo, bo, g1, c1, wu, bu, wd, bd, g2, c2):
        bias_rows = jnp.stack([bq[0], jnp.zeros_like(bq[0]), bq[1]])
        projected = low_back(jnp.einsum('td,ide->ite', x, wq, precision=HIGHEST) + bias_rows[:, None, :])
        heads = projected.reshape(3, total, heads_all, head_size)
        query_low = low(unit_rows(heads[0]))
        key_low = low(unit_rows(heads[1]))
        value_low = low(heads[2])
        attended = lax.map(lambda pair: checked(pair[0], pair[1], key_low, value_low, items), (query_low.reshape(blocks, block, heads_all, head_size), items.reshape(blocks, block)))
        attended = low_back(attended.reshape(total, heads_all, head_size))
        attn_unit = unit_rows(attended).reshape(total, heads_all * head_size)
        value_rim = jnp.pad(value_low.reshape(total, heads_all * head_size), ((radius, radius), (0, 0)))
        tap_columns = jnp.repeat(tp, head_size, axis=0).T
        convolved = jnp.zeros_like(attn_unit)
        for shift_at in range(kernel):
            same_rows = (rim_items[shift_at:shift_at + total] == items).astype(jnp.float32)[:, None]
            convolved = convolved + tap_columns[shift_at] * same_rows * value_rim[shift_at:shift_at + total]
        context = low(low_back(attn_unit + convolved))
        first_sum = x + low_back(jnp.dot(context, wo, precision=HIGHEST)) + bo
        first_out = layer_norm(first_sum, g1, c1)
        inner = low_back(jnp.dot(low(first_out), wu, precision=HIGHEST) + bu)
        activated = low(jax.nn.gelu(inner, approximate=False))
        second_sum = first_out + low_back(jnp.dot(activated, wd, precision=HIGHEST)) + bd
        return layer_norm(second_sum, g2, c2)
    params = tuple((array.astype(jnp.float32) for array in (tokens, w_qkv, b_qv, taps, w_out, b_out, ln1_gain, ln1_bias, w_up, b_up, w_down, b_down, ln2_gain, ln2_bias)))
    result, pull = jax.vjp(forward, *params)
    grads = pull(d_out.astype(jnp.float32))
    return (result.astype(jnp.bfloat16), grads[0].astype(jnp.bfloat16), grads[1], grads[2], grads[3], grads[4], grads[5], grads[6], grads[7], grads[8], grads[9], grads[10], grads[11], grads[12], grads[13])
```

```python
import functools
import math

import jax
import jax.numpy as jnp
from jax import lax
from jax.experimental import pallas as pl
from jax.experimental.pallas import tpu as pltpu
from jax.sharding import PartitionSpec as P

SHRINK = 0.95
NORM_EPS = 1e-06
LAYER_EPS = 1e-05
F32 = jnp.float32
BF16 = jnp.bfloat16
ROWS = 128
KEYS = 256
BAND = 384
VMEM_BYTES = 56 * 1024 * 1024
SQUARE = (
    0.9999936361319989,
    -1.2731008162270503,
    0.4040306859655804,
    -0.20598641392473288,
    0.11615118744625774,
    -0.05772567810293111,
    0.02001158958170149,
    -0.00337422878652264,
)
SLOPE = 4.0 * SHRINK / math.pi


def dot(left, right, left_dim=1, right_dim=0):
    return lax.dot_general(
        left, right, (((left_dim,), (right_dim,)), ((), ())), preferred_element_type=F32
    )


def flips(axis):
    size = lax.axis_size(axis)
    mask = size // 2
    while mask:
        yield [(i, i ^ mask) for i in range(size)]
        mask //= 2


def gathered(cells, axis):
    cells = cells[None]
    for pairs in flips(axis):
        cells = jnp.concatenate([cells, lax.ppermute(cells, axis, pairs)], axis=0)
    return cells


def block_places(axis):
    size = lax.axis_size(axis)
    apart = jnp.arange(size, dtype=jnp.int32) ^ lax.axis_index(axis).astype(jnp.int32)
    place = jnp.zeros_like(apart)
    mask, bit = size // 2, 0
    while mask:
        place = place | (jnp.where((apart & mask) != 0, 1, 0) << bit)
        mask, bit = mask // 2, bit + 1
    return place


def all_sum(cells, axis):
    size = lax.axis_size(axis)
    index = lax.axis_index(axis)
    masks = [1 << bit for bit in range(size.bit_length() - 1)]
    pairs_of = lambda mask: [(i, i ^ mask) for i in range(size)]
    for mask in masks[:-1]:
        half = cells.shape[0] // 2
        upper = (index & mask) != 0
        sent = lax.dynamic_slice_in_dim(cells, jnp.where(upper, 0, half), half)
        kept = lax.dynamic_slice_in_dim(cells, jnp.where(upper, half, 0), half)
        got = lax.ppermute(sent, axis, pairs_of(mask))
        cells = (kept.astype(F32) + got.astype(F32)).astype(BF16)
    got = lax.ppermute(cells, axis, pairs_of(masks[-1]))
    cells = (cells.astype(F32) + got.astype(F32)).astype(BF16)
    for mask in masks[-2::-1]:
        upper = (index & mask) != 0
        got = lax.ppermute(cells, axis, pairs_of(mask))
        cells = jnp.concatenate([jnp.where(upper, got, cells), jnp.where(upper, cells, got)], axis=0)
    return cells


def item_index(positions, ends):
    inside = (positions >= 0) & (positions < ends[-1])
    counted = jnp.sum((positions[:, None] >= ends[None, :]).astype(jnp.int32), axis=1)
    return jnp.where(inside, counted, -1)


def layer_norm(hidden, gain, shift):
    center = hidden - jnp.mean(hidden, axis=-1, keepdims=True)
    scale = lax.rsqrt(jnp.mean(center * center, axis=-1, keepdims=True) + LAYER_EPS)
    normed = center * scale
    return (normed * gain + shift, normed, scale)


def layer_norm_back(grad, normed, scale, gain):
    d_gain = jnp.sum(grad * normed, axis=0)
    d_shift = jnp.sum(grad, axis=0)
    d_normed = grad * gain
    centered = d_normed - jnp.mean(d_normed, axis=-1, keepdims=True)
    d_hidden = scale * (centered - normed * jnp.mean(d_normed * normed, axis=-1, keepdims=True))
    return (d_hidden, d_gain, d_shift)


def call(kernel, out_shape, *args, grid=(), in_specs=None, out_specs=None, scalars=0, flops=0, scratch=()):
    whole = lambda a: pl.BlockSpec(a.shape, lambda *_, n=len(a.shape): (0,) * n)
    ins = [whole(a) if s is None else s for a, s in zip(args[scalars:], in_specs or [None] * 99)]
    outs = [whole(a) if s is None else s for a, s in zip(out_shape, out_specs or [None] * 99)]
    moved = sum(a.size * a.dtype.itemsize for a in (*args, *out_shape))
    return pl.pallas_call(
        kernel,
        out_shape=out_shape,
        grid_spec=pltpu.PrefetchScalarGridSpec(
            num_scalar_prefetch=scalars,
            grid=grid,
            in_specs=ins,
            out_specs=outs,
            scratch_shapes=list(scratch),
        ),
        compiler_params=pltpu.CompilerParams(vmem_limit_bytes=VMEM_BYTES),
        cost_estimate=pl.CostEstimate(flops=flops, bytes_accessed=moved, transcendentals=0),
    )(*args)


def project_kernel(heads, unit, tokens_ref, w_ref, bias_ref, raw_ref, own_ref, turned_ref):
    product = dot(tokens_ref[...], w_ref[...], 1, 1) + bias_ref[...]
    size = product.shape[1] // heads
    rounded = []
    for head in range(heads):
        raw = product[:, head * size : (head + 1) * size]
        if unit:
            raw_ref[head] = raw
            raw = raw * lax.rsqrt(jnp.sum(raw * raw, axis=-1, keepdims=True) + NORM_EPS)
        own_ref[head] = raw.astype(BF16)
        rounded.append(raw)
    turned_ref[...] = jnp.concatenate(rounded, axis=1).T.astype(BF16)


def project(tokens, w, bias, heads, unit):
    rows, columns = tokens.shape[0], w.shape[0]
    size = columns // heads
    shapes = [
        jax.ShapeDtypeStruct((heads, rows, size), F32 if unit else BF16),
        jax.ShapeDtypeStruct((heads, rows, size), BF16),
        jax.ShapeDtypeStruct((columns, rows), BF16),
    ]
    if unit:
        kernel = functools.partial(project_kernel, heads, True)
    else:
        kernel = lambda t, w_, b, own, turned: project_kernel(heads, False, t, w_, b, None, own, turned)
        shapes = shapes[1:]
    return call(kernel, shapes, tokens, w, bias.reshape(1, columns), flops=2 * rows * w.size)


def item_range(lengths_ref, first, last):
    end = jnp.int32(0)
    low = jnp.int32(0)
    high = jnp.int32(0)
    found = jnp.int32(0)
    for item in range(lengths_ref.shape[0]):
        end = end + lengths_ref[item]
        low = jnp.where(end <= first, end, low)
        past = (end > last).astype(jnp.int32)
        high = jnp.where((past == 1) & (found == 0), end, high)
        found = found | past
    return low, high


def square_of(scores):
    half = 0.5 - (0.5 * SHRINK) * scores
    inverse = lax.rsqrt(half)
    root = half * inverse
    square = jnp.full_like(root, SQUARE[-1])
    for factor in SQUARE[-2::-1]:
        square = square * root + factor
    return square, inverse


def slope_of(scores, square, inverse):
    other = lax.rsqrt(0.5 + (0.5 * SHRINK) * scores)
    cube = square * square * square
    return cube * (square * lax.rsqrt(square)) * (inverse * (other * SLOPE))


def band_of(taps_row, flip):
    wide = jnp.broadcast_to(taps_row, (ROWS, BAND))
    return pltpu.roll(wide, 0, 1, stride=1, stride_axis=0)


def split_low(wide):
    high = wide.astype(BF16)
    return high, (wide - high.astype(F32)).astype(BF16)


def near(turned_ref, head_rows, place_ref, tile, width, tiles):
    parts = []
    per = width // ROWS
    for at in (tile - 1, tile, tile + 1):
        at = jnp.clip(at, 0, tiles - 1)
        start = pl.multiple_of((at % per) * ROWS, ROWS)
        parts.append(turned_ref[place_ref[at // per], head_rows, pl.ds(start, ROWS)])
    return jnp.concatenate(parts, axis=1)


def forward_kernel(
    lengths_ref, place_ref, index_ref, mine_ref, items_ref, edge_ref, taps_ref, q_ref, k_ref, v_ref,
    context_ref, raw_ref,
):
    heads, rows, size = q_ref.shape
    blocks, _, width = k_ref.shape
    tile = index_ref[0] * (width // ROWS) + pl.program_id(0)
    first = tile * ROWS
    low, high = item_range(lengths_ref, first, first + rows - 1)
    per = width // KEYS
    mine = mine_ref[...]

    def step(at, sums):
        place = place_ref[at // per]
        start = pl.multiple_of((at % per) * KEYS, KEYS)
        same = mine == items_ref[at // per, :, pl.ds(start, KEYS)]
        out = []
        for head in range(heads):
            group = slice(head * size, (head + 1) * size)
            scores = dot(q_ref[head], k_ref[place, group, pl.ds(start, KEYS)])
            square, _ = square_of(scores)
            fourth = square * square
            weights = jnp.where(same, fourth * fourth, 0.0).astype(BF16)
            out.append(sums[head] + dot(weights, v_ref[place, group, pl.ds(start, KEYS)], 1, 1))
        return tuple(out)

    zero = tuple(jnp.zeros((rows, size), F32) for _ in range(heads))
    sums = lax.fori_loop(low // KEYS, (high + KEYS - 1) // KEYS, step, zero)
    around = mine == edge_ref[pl.ds(pl.program_id(0), 1), :]
    context = []
    for head in range(heads):
        group = slice(head * size, (head + 1) * size)
        raw = sums[head]
        raw_ref[head] = raw
        unit = raw * lax.rsqrt(jnp.sum(raw * raw, axis=-1, keepdims=True) + NORM_EPS)
        values = near(v_ref, group, place_ref, tile, width, blocks * (width // ROWS))
        band = jnp.where(around, band_of(taps_ref[head : head + 1, :], False), 0.0)
        band_high, band_low = split_low(band)
        context.append(unit + (dot(band_high, values, 1, 1) + dot(band_low, values, 1, 1)))
    context_ref[...] = jnp.concatenate(context, axis=1).astype(BF16)


def query_back_kernel(
    lengths_ref, place_ref, index_ref, mine_ref, items_ref, q_ref, da_ref, q_raw_ref, k_ref, v_ref, dq_ref
):
    heads, rows, size = q_ref.shape
    blocks, _, width = k_ref.shape
    first = index_ref[0] * width + pl.program_id(0) * rows
    low, high = item_range(lengths_ref, first, first + rows - 1)
    per = width // KEYS
    mine = mine_ref[...]

    def step(at, sums):
        place = place_ref[at // per]
        start = pl.multiple_of((at % per) * KEYS, KEYS)
        same = mine == items_ref[at // per, :, pl.ds(start, KEYS)]
        out = []
        for head in range(heads):
            group = slice(head * size, (head + 1) * size)
            keys = k_ref[place, group, pl.ds(start, KEYS)]
            scores = dot(q_ref[head], keys)
            d_weights = dot(da_ref[head], v_ref[place, group, pl.ds(start, KEYS)])
            square, inverse = square_of(scores)
            d_scores = jnp.where(same, d_weights * slope_of(scores, square, inverse), 0.0).astype(BF16)
            out.append(sums[head] + dot(d_scores, keys, 1, 1))
        return tuple(out)

    zero = tuple(jnp.zeros((rows, size), F32) for _ in range(heads))
    sums = lax.fori_loop(low // KEYS, (high + KEYS - 1) // KEYS, step, zero)
    dq_ref[...] = jnp.concatenate(
        [unit_back(sums[head], q_raw_ref[head]) for head in range(heads)], axis=1
    ).astype(BF16)


def unit_back(grad, raw):
    scale = lax.rsqrt(jnp.sum(raw * raw, axis=-1, keepdims=True) + NORM_EPS)
    unit = raw * scale
    return scale * (grad - unit * jnp.sum(unit * grad, axis=-1, keepdims=True))


def key_back_kernel(
    lengths_ref, place_ref, index_ref, mine_ref, items_ref, k_ref, v_ref, k_raw_ref, dv_conv_ref, q_ref, da_ref,
    dk_ref, dv_ref,
):
    heads, rows, size = k_ref.shape
    blocks, _, width = q_ref.shape
    first = index_ref[0] * width + pl.program_id(0) * rows
    low, high = item_range(lengths_ref, first, first + rows - 1)
    per = width // KEYS
    mine = mine_ref[...]

    def step(at, sums):
        place = place_ref[at // per]
        start = pl.multiple_of((at % per) * KEYS, KEYS)
        same = mine == items_ref[at // per, :, pl.ds(start, KEYS)]
        out = []
        for head in range(heads):
            group = slice(head * size, (head + 1) * size)
            queries = q_ref[at // per, group, pl.ds(start, KEYS)]
            d_attn = da_ref[place, group, pl.ds(start, KEYS)]
            scores = dot(k_ref[head], queries)
            d_weights = dot(v_ref[head], d_attn)
            square, inverse = square_of(scores)
            fourth = square * square
            weights = jnp.where(same, fourth * fourth, 0.0).astype(BF16)
            d_scores = jnp.where(same, d_weights * slope_of(scores, square, inverse), 0.0).astype(BF16)
            d_keys, d_values = sums[head]
            out.append((d_keys + dot(d_scores, queries, 1, 1), d_values + dot(weights, d_attn, 1, 1)))
        return tuple(out)

    zero = tuple((jnp.zeros((rows, size), F32), jnp.zeros((rows, size), F32)) for _ in range(heads))
    sums = lax.fori_loop(low // KEYS, (high + KEYS - 1) // KEYS, step, zero)
    dk_ref[...] = jnp.concatenate(
        [unit_back(sums[head][0], k_raw_ref[head]) for head in range(heads)], axis=1
    ).astype(BF16)
    dv_ref[...] = jnp.concatenate(
        [sums[head][1] + dv_conv_ref[head] for head in range(heads)], axis=1
    ).astype(BF16)


def attention_back_kernel(d_first_ref, w_out_ref, raw_ref, d_context_ref, turned_ref, da_ref, da_turned_ref):
    heads, rows, size = raw_ref.shape
    d_context = dot(d_first_ref[...], w_out_ref[...], 1, 1).astype(BF16).astype(F32)
    turned_ref[...] = d_context.T.astype(BF16)
    grads = []
    for head in range(heads):
        grad = d_context[:, head * size : (head + 1) * size]
        d_context_ref[head] = grad.astype(BF16)
        grad = unit_back(grad, raw_ref[head])
        da_ref[head] = grad.astype(BF16)
        grads.append(grad)
    da_turned_ref[...] = jnp.concatenate(grads, axis=1).T.astype(BF16)


def conv_back_kernel(
    place_ref, index_ref, mine_ref, edge_ref, taps_ref, mirrored_ref, v_ref, d_context_ref, turned_ref,
    dv_ref, d_taps_ref,
):
    heads, rows, size = d_context_ref.shape
    blocks, _, width = v_ref.shape
    here = pl.program_id(0)
    tile = index_ref[0] * (width // ROWS) + here
    around = mine_ref[...] == edge_ref[pl.ds(here, 1), :]
    start = pl.multiple_of(here * ROWS, ROWS)

    @pl.when(here == 0)
    def _():
        d_taps_ref[...] = jnp.zeros_like(d_taps_ref)

    for head in range(heads):
        group = slice(head * size, (head + 1) * size)
        band = jnp.where(around, band_of(mirrored_ref[head : head + 1, :], False), 0.0)
        band_high, band_low = split_low(band)
        grads = turned_ref[group, pl.ds(start, BAND)]
        dv_ref[head] = dot(band_high, grads, 1, 1) + dot(band_low, grads, 1, 1)
        values = near(v_ref, group, place_ref, tile, width, blocks * (width // ROWS))
        pairs = jnp.where(around, dot(d_context_ref[head], values), 0.0)
        lined = pairs[:8, :]
        for row in range(8, rows, 8):
            lined = lined + pltpu.roll(pairs[row : row + 8, :], BAND - row, 1)
        total = lined[0:1, :]
        for row in range(1, 8):
            total = total + pltpu.roll(lined[row : row + 1, :], BAND - row, 1)
        d_taps_ref[head : head + 1, :] += total


def per_device(
    tokens, item_lengths, w_qkv, b_qv, taps, w_out, b_out, ln1_gain, ln1_bias, w_up, b_up, w_down, b_down,
    ln2_gain, ln2_bias, d_out,
):
    rows, features = tokens.shape
    heads, kernel = taps.shape
    radius = (kernel - 1) // 2
    columns = w_qkv.shape[2]
    size = columns // heads
    blocks = lax.axis_size("seq")
    total = blocks * rows
    index = lax.axis_index("seq").astype(jnp.int32)
    first_row = index * rows

    count = item_lengths.shape[0]
    upto = jnp.arange(count)[None, :] <= jnp.arange(count)[:, None]
    ends = jnp.sum(jnp.where(upto, item_lengths[None, :], 0), axis=1)
    items = item_index(jnp.arange(total, dtype=jnp.int32), ends).reshape(blocks, 1, rows)
    tiles = rows // ROWS
    edge_at = (
        first_row - ROWS + ROWS * jnp.arange(tiles, dtype=jnp.int32)[:, None]
        + jnp.arange(BAND, dtype=jnp.int32)[None, :]
    )
    edge = item_index(edge_at.reshape(-1), ends).reshape(tiles, BAND)
    mine = item_index(first_row + jnp.arange(rows, dtype=jnp.int32), ends)[:, None]
    place = block_places("seq")
    scalars = (item_lengths, place, index[None])
    reach = ROWS - radius
    banded = jnp.pad(taps, ((0, 0), (reach, BAND - reach - kernel)))
    mirrored = jnp.pad(taps[:, ::-1], ((0, 0), (reach, BAND - reach - kernel)))
    mine_spec = pl.BlockSpec((ROWS, 1), lambda i, *_: (i, 0))
    head_spec = pl.BlockSpec((heads, ROWS, size), lambda i, *_: (0, i, 0))
    row_spec = pl.BlockSpec((ROWS, columns), lambda i, *_: (i, 0))

    w_turned = jnp.swapaxes(w_qkv, 1, 2)
    zeros = jnp.zeros((columns,), F32)
    k_raw, k_own, k_turned = project(tokens, w_turned[1], zeros, heads, True)
    keys = gathered(k_turned, "seq")
    k_turned, w_out_late, w_up_late, w_down_late, b_up_late = lax.optimization_barrier(
        (k_turned, w_out, w_up, w_down, b_up)
    )
    v_own, v_turned = project(tokens, w_turned[2], b_qv[1], heads, False)
    values = gathered(v_turned, "seq")
    q_raw, q_own, q_turned = project(tokens, w_turned[0], b_qv[0], heads, True)
    q_turned, values = lax.optimization_barrier((q_turned, values))
    queries = lax.all_gather(q_turned, "seq")
    out_all = gathered(w_out_late, "mp")
    up_all = gathered(w_up_late, "mp")
    b_up_all = gathered(b_up_late, "mp")
    down_all = gathered(w_down_late, "mp")
    parts = up_all.shape[0]

    shape = jax.ShapeDtypeStruct
    pair_flops = 4 * 2 * rows * (total // 2) * columns
    context, attended = call(
        forward_kernel,
        [shape((rows, columns), BF16), shape((heads, rows, size), F32)],
        *scalars, mine, items, edge, banded, q_own, keys, values,
        grid=(tiles,),
        scalars=3,
        in_specs=[mine_spec, None, None, None, head_spec, None, None],
        out_specs=[row_spec, head_spec],
        flops=pair_flops,
    )
    contexts = gathered(context, "mp")
    branch = jnp.einsum("ptc,pcd->td", contexts, out_all, preferred_element_type=F32)
    first_sum = tokens.astype(F32) + branch + b_out
    first_out, normed_one, scale_one = layer_norm(first_sum, ln1_gain, ln1_bias)
    first_low = first_out.astype(BF16)
    mixed = jnp.zeros((rows, features), F32)
    inner_all, act_all = [], []
    for part in range(parts):
        inner = jnp.dot(first_low, up_all[part], preferred_element_type=F32) + b_up_all[part]
        act = jax.nn.gelu(inner, approximate=False).astype(BF16)
        mixed = mixed + jnp.dot(act, down_all[part], preferred_element_type=F32)
        inner_all.append(inner)
        act_all.append(act)
    second_sum = first_out + mixed + b_down
    result, normed_two, scale_two = layer_norm(second_sum, ln2_gain, ln2_bias)
    layer_output = result.astype(BF16)
    d_second, d_ln2_gain, d_ln2_bias = layer_norm_back(d_out.astype(F32), normed_two, scale_two, ln2_gain)
    d_second_low = d_second.astype(BF16)
    d_b_down = jnp.sum(d_second, axis=0)
    d_w_down = jnp.einsum("tf,td->fd", act_all[0], d_second_low, preferred_element_type=F32)
    d_first_out = d_second
    d_inner_all = []
    for part in range(parts):
        inner = inner_all[part]
        d_act = jnp.einsum("td,fd->tf", d_second_low, down_all[part], preferred_element_type=F32)
        normal_cdf = 0.5 * (1.0 + lax.erf(inner / math.sqrt(2.0)))
        normal_pdf = jnp.exp(-0.5 * inner * inner) / math.sqrt(2.0 * math.pi)
        d_inner = (d_act * (normal_cdf + inner * normal_pdf)).astype(BF16)
        d_first_out = d_first_out + jnp.einsum("tf,df->td", d_inner, up_all[part], preferred_element_type=F32)
        d_inner_all.append(d_inner)
    d_b_up = jnp.sum(d_inner_all[0].astype(F32), axis=0)
    d_w_up = jnp.einsum("td,tf->df", first_low, d_inner_all[0], preferred_element_type=F32)
    d_first, d_ln1_gain, d_ln1_bias = layer_norm_back(d_first_out, normed_one, scale_one, ln1_gain)
    d_first_low = d_first.astype(BF16)
    d_b_out = jnp.sum(d_first, axis=0)
    d_w_out = jnp.einsum("tc,td->cd", context, d_first_low, preferred_element_type=F32)

    early = lax.psum(
        tuple(
            grad.astype(BF16)
            for grad in (
                d_w_out, d_b_out, d_ln1_gain, d_ln1_bias, d_w_up, d_b_up, d_w_down, d_b_down, d_ln2_gain, d_ln2_bias,
            )
        ),
        "seq",
    )

    d_context, d_context_turned, da_own, da_turned = call(
        attention_back_kernel,
        [
            shape((heads, rows, size), BF16), shape((columns, rows), BF16),
            shape((heads, rows, size), BF16), shape((columns, rows), BF16),
        ],
        d_first_low, w_out, attended,
        flops=2 * rows * w_out.size,
    )
    d_attended = gathered(da_turned, "seq")
    ahead = [(i, i + 1) for i in range(blocks - 1)]
    behind = [(i + 1, i) for i in range(blocks - 1)]
    context_rim = jnp.concatenate(
        [
            lax.ppermute(d_context_turned[:, rows - ROWS :], "seq", ahead),
            d_context_turned,
            lax.ppermute(d_context_turned[:, :ROWS], "seq", behind),
        ],
        axis=1,
    )
    dv_conv, d_taps_wide = call(
        conv_back_kernel,
        [shape((heads, rows, size), F32), shape((heads, BAND), F32)],
        place, index[None], mine, edge, banded, mirrored, values, d_context, context_rim,
        grid=(tiles,),
        scalars=2,
        in_specs=[mine_spec, None, None, None, None, head_spec, None],
        out_specs=[head_spec, None],
        flops=2 * rows * BAND * columns,
    )
    d_taps = d_taps_wide[:, reach : reach + kernel]
    [dq] = call(
        query_back_kernel,
        [shape((rows, columns), BF16)],
        *scalars, mine, items, q_own, da_own, q_raw, keys, values,
        grid=(tiles,),
        scalars=3,
        in_specs=[mine_spec, None, head_spec, head_spec, head_spec, None, None],
        out_specs=[row_spec],
        flops=2 * pair_flops,
    )
    dk, dv = call(
        key_back_kernel,
        [shape((rows, columns), BF16), shape((rows, columns), BF16)],
        *scalars, mine, items, k_own, v_own, k_raw, dv_conv, queries, d_attended,
        grid=(tiles,),
        scalars=3,
        in_specs=[mine_spec, None, head_spec, head_spec, head_spec, head_spec, None, None],
        out_specs=[row_spec, row_spec],
        flops=3 * pair_flops,
    )
    d_bias = [jnp.sum(part.astype(F32), axis=0) for part in (dq, dv)]
    small = jnp.concatenate([d_bias[0], d_bias[1], d_taps.reshape(-1)]).astype(BF16)
    spare = 64 * features - small.shape[0]
    d_w_turned = [jnp.einsum("te,td->ed", part, tokens, preferred_element_type=F32).astype(BF16) for part in (dq, dk, dv)]
    late = jnp.concatenate(d_w_turned + [jnp.pad(small, (0, spare)).reshape(64, features)], axis=0)
    late = all_sum(late, "seq")
    d_tokens_part = sum(
        jnp.dot(part, w_turned[i], preferred_element_type=F32) for i, part in enumerate((dq, dk, dv))
    )
    d_tokens = (d_first + all_sum(d_tokens_part.astype(BF16), "mp").astype(F32)).astype(BF16)
    d_w_qkv = jnp.swapaxes(late[: 3 * columns].reshape(3, columns, features), 1, 2).astype(F32)
    small = late[3 * columns :].reshape(-1).astype(F32)
    d_b_qv = small[: 2 * columns].reshape(2, columns)
    d_taps = small[2 * columns : 2 * columns + heads * kernel].reshape(heads, kernel)
    d_w_out, d_b_out, d_ln1_gain, d_ln1_bias, d_w_up, d_b_up, d_w_down, d_b_down, d_ln2_gain, d_ln2_bias = [
        grad.astype(F32) for grad in early
    ]
    return (
        layer_output, d_tokens, d_w_qkv, d_b_qv, d_taps, d_w_out, d_b_out, d_ln1_gain, d_ln1_bias, d_w_up, d_b_up,
        d_w_down, d_b_down, d_ln2_gain, d_ln2_bias,
    )


def solution(mesh):
    placed = (
        P("seq", None), P(), P(None, None, "mp"), P(None, "mp"), P("mp", None), P("mp", None), P(), P(), P(),
        P(None, "mp"), P("mp"), P("mp", None), P(), P(), P(), P("seq", None),
    )
    given = (
        P("seq", None), P("seq", None), P(None, None, "mp"), P(None, "mp"), P("mp", None), P("mp", None), P(),
        P(), P(), P(None, "mp"), P("mp"), P("mp", None), P(), P(), P(),
    )
    return jax.shard_map(per_device, mesh=mesh, in_specs=placed, out_specs=given, check_vma=False)
```

```python
import functools
import math

import jax
import jax.numpy as jnp
from jax import lax
from jax.experimental import pallas as pl
from jax.experimental.pallas import tpu as pltpu
from jax.sharding import PartitionSpec as P

SHRINK = 0.95
NORM_EPS = 1e-06
LAYER_EPS = 1e-05
F32 = jnp.float32
BF16 = jnp.bfloat16
KEYS = 256
CHUNK = 256
EDGE = 128
BAND = 3 * EDGE
MIDDLE = 256
WINDOW = 9216
VMEM_BYTES = 56 * 1024 * 1024
SQUARE_OF_V = (
    0.9999936361319989,
    -1.2731008162270503,
    0.4040306859655804,
    -0.20598641392473288,
    0.11615118744625774,
    -0.05772567810293111,
    0.02001158958170149,
    -0.00337422878652264,
)
SQUARE = tuple(factor * (0.5 * SHRINK) ** (0.5 * power) for power, factor in enumerate(SQUARE_OF_V))
SLOPE = 8.0 / math.pi
TAIL_AT = 0.2316419
TAIL = (0.319381530, -0.356563782, 1.781477937, -1.821255978, 1.330274429)


def dot(left, right, left_dim=1, right_dim=0):
    return lax.dot_general(
        left, right, (((left_dim,), (right_dim,)), ((), ())), preferred_element_type=F32
    )


def flipped(cells, axis, mask):
    return lax.ppermute(cells, axis, [(i, i ^ mask) for i in range(lax.axis_size(axis))])


def masks_of(axis):
    return [1 << bit for bit in range(lax.axis_size(axis).bit_length() - 2, -1, -1)]


def block_places(axis, masks):
    apart = jnp.arange(lax.axis_size(axis), dtype=jnp.int32) ^ lax.axis_index(axis).astype(jnp.int32)
    place = jnp.zeros_like(apart)
    for bit, mask in enumerate(masks):
        place = place | (jnp.where((apart & mask) != 0, 1, 0) << bit)
    return place


def all_sum(cells, axis, holds=()):
    index = lax.axis_index(axis)
    masks = masks_of(axis)[::-1]
    waits, stages = iter(holds), []

    def exchanged(array, mask):
        got = flipped(array, axis, mask)
        held = next(waits, ())
        stages.append(after(got, *held) if held else got)
        return stages[-1]

    for mask in masks[:-1]:
        half = cells.shape[0] // 2
        upper = (index & mask) != 0
        sent = lax.dynamic_slice_in_dim(cells, jnp.where(upper, 0, half), half)
        kept = lax.dynamic_slice_in_dim(cells, jnp.where(upper, half, 0), half)
        cells = (kept.astype(F32) + exchanged(sent, mask).astype(F32)).astype(BF16)
    cells = (cells.astype(F32) + exchanged(cells, masks[-1]).astype(F32)).astype(BF16)
    for mask in masks[-2::-1]:
        upper = (index & mask) != 0
        got = exchanged(cells, mask)
        cells = jnp.concatenate([jnp.where(upper, got, cells), jnp.where(upper, cells, got)], axis=0)
    return cells, stages


def after(array, *earlier):
    return lax.optimization_barrier((array, *earlier))[0]


def joined(*arrays):
    return lax.optimization_barrier(arrays)


def stacked(*cells):
    return jnp.concatenate([part if part.ndim == 3 else part[None] for part in cells], axis=0)


def item_index(positions, ends):
    inside = (positions >= 0) & (positions < ends[-1])
    counted = jnp.sum((positions[:, None] >= ends[None, :]).astype(jnp.int32), axis=1)
    return jnp.where(inside, counted, -1)


def call(kernel, out_shape, *args, grid=(), in_specs=None, out_specs=None, scalars=0, flops=0, scratch=()):
    whole = lambda a: pl.BlockSpec(a.shape, lambda *_, n=len(a.shape): (0,) * n)
    ins = [whole(a) if s is None else s for a, s in zip(args[scalars:], in_specs or [None] * 99)]
    outs = [whole(a) if s is None else s for a, s in zip(out_shape, out_specs or [None] * 99)]
    moved = sum(a.size * a.dtype.itemsize for a in (*args, *out_shape))
    return pl.pallas_call(
        kernel,
        out_shape=out_shape,
        grid_spec=pltpu.PrefetchScalarGridSpec(
            num_scalar_prefetch=scalars,
            grid=grid,
            in_specs=ins,
            out_specs=outs,
            scratch_shapes=list(scratch),
        ),
        compiler_params=pltpu.CompilerParams(vmem_limit_bytes=VMEM_BYTES),
        cost_estimate=pl.CostEstimate(flops=1, bytes_accessed=1, transcendentals=0),
    )(*args)


def project_kernel(unit, raw, own, turned, tokens_ref, w_ref, bias_ref, *out_refs):
    out_refs = list(out_refs)
    raw_ref = out_refs.pop(0) if raw else None
    own_ref = out_refs.pop(0) if own else None
    turned_ref = out_refs.pop(0) if turned else None
    product = dot(w_ref[0], tokens_ref[...], 1, 1) + bias_ref[...]
    size = HEAD
    for head in range(product.shape[0] // size):
        part = product[head * size : (head + 1) * size, :]
        if raw:
            raw_ref[head] = part.T
        if unit:
            part = part * lax.rsqrt(jnp.sum(part * part, axis=0, keepdims=True) + NORM_EPS)
        if turned:
            turned_ref[head * size : (head + 1) * size, :] = part.astype(BF16)
        if own:
            own_ref[head] = part.T.astype(BF16)


def square_of(half):
    root = half * lax.rsqrt(half)
    square = jnp.full_like(root, SQUARE[-1])
    for factor in SQUARE[-2::-1]:
        square = square * root + factor
    return square


def tile_of(span_ref):
    return span_ref[0] + jnp.minimum(pl.program_id(0), span_ref[1] - 1)


def held_at(far, near_ref, far_ref, group):
    return jnp.where(far, far_ref[0, group, :], near_ref[0, group, :])


def is_far(span_ref, place_ref, rows):
    return place_ref[tile_of(span_ref) // (rows // KEYS)] >= (place_ref.shape[0] - 1) // 2


def by_chunks(span_ref, rows, work):
    tile = span_ref[0] + pl.program_id(0)
    here = pl.program_id(0) < span_ref[1]
    meets = [
        (tile >= span_ref[2 + 2 * chunk]) & (tile < span_ref[3 + 2 * chunk]) for chunk in range(rows // CHUNK)
    ]
    every = functools.reduce(lambda x, y: x & y, meets)

    @pl.when(here & every)
    def _():
        work(slice(0, rows))

    for chunk, meet in enumerate(meets):

        @pl.when(here & meet & jnp.logical_not(every))
        def _(chunk=chunk):
            work(slice(chunk * CHUNK, (chunk + 1) * CHUNK))


def weights_kernel(
    span_ref, place_ref, v_place_ref, mine_ref, items_ref, own_ref, near_ref, far_ref, weight_ref, slope_ref
):
    heads, rows, size = own_ref.shape
    far = is_far(span_ref, place_ref, rows)

    def work(part):
        same = mine_ref[part, :] == items_ref[0]
        for head in range(heads):
            scores = dot(own_ref[head, part, :], held_at(far, near_ref, far_ref, slice(head * size, (head + 1) * size)))
            half = 1.0 / SHRINK - scores
            square = square_of(half)
            fourth = square * square
            weight = jnp.where(same, fourth * fourth, 0.0)
            weight_ref[0, head, part, :] = weight.astype(BF16)
            slope = weight * lax.rsqrt(square * (half * (1.0 / SHRINK + scores)))
            slope_ref[0, head, part, :] = slope.astype(BF16)

    by_chunks(span_ref, rows, work)


def unit_back(grad, raw):
    scale = lax.rsqrt(jnp.sum(raw * raw, axis=-1, keepdims=True) + NORM_EPS)
    unit = raw * scale
    return scale * (grad - unit * jnp.sum(unit * grad, axis=-1, keepdims=True))


def split_low(wide):
    high = wide.astype(BF16)
    return high, (wide - high.astype(F32)).astype(BF16)


def band_of(taps_row):
    return pltpu.roll(jnp.broadcast_to(taps_row, (EDGE, BAND)), 0, 1, stride=1, stride_axis=0)


def around_of(mine_ref, rim_ref, start):
    return mine_ref[start : start + EDGE, :] == rim_ref[:, start : start + BAND]


def band_sums(taps_ref, head, mine_ref, rim_ref, values):
    band = band_of(taps_ref[head : head + 1, :])
    out = []
    for start in range(0, mine_ref.shape[0], EDGE):
        high, low = split_low(jnp.where(around_of(mine_ref, rim_ref, start), band, 0.0))
        near = values[:, start : start + BAND]
        out.append(dot(high, near, 1, 1) + dot(low, near, 1, 1))
    return jnp.concatenate(out, axis=0)


def rim_values(v_place_ref, sides, own_ref, group):
    index, blocks, rows = v_place_ref[v_place_ref.shape[0] - 1], v_place_ref.shape[0] - 1, own_ref.shape[1]
    ends = []
    for (near_ref, far_ref), beside, part in zip(sides, (-1, 1), (slice(rows - EDGE, rows), slice(0, EDGE))):
        far = v_place_ref[jnp.clip(index + beside, 0, blocks - 1)] >= blocks // 2
        ends.append(jnp.where(far, far_ref[0, group, part], near_ref[0, group, part]))
    return jnp.concatenate([ends[0], own_ref[group, :], ends[1]], axis=1)


def attend_kernel(
    span_ref, place_ref, v_place_ref, weight_ref, v_near_ref, v_far_ref, mine_ref, rim_ref, taps_ref, own_ref,
    before_near_ref, before_far_ref, after_near_ref, after_far_ref, context_ref, raw_ref, v_rim_ref, sum_ref, conv_ref,
):
    heads, rows, size = raw_ref.shape
    far = is_far(span_ref, v_place_ref, rows)

    @pl.when(pl.program_id(0) == 0)
    def _():
        sides = ((before_near_ref, before_far_ref), (after_near_ref, after_far_ref))
        for head in range(heads):
            group = slice(head * size, (head + 1) * size)
            values = rim_values(v_place_ref, sides, own_ref, group)
            v_rim_ref[group, :] = values
            conv_ref[head] = band_sums(taps_ref, head, mine_ref, rim_ref, values)
        sum_ref[...] = jnp.zeros_like(sum_ref)

    def work(part):
        for head in range(heads):
            values = held_at(far, v_near_ref, v_far_ref, slice(head * size, (head + 1) * size))
            sum_ref[head, part, :] += dot(weight_ref[0, head, part, :], values, 1, 1)

    by_chunks(span_ref, rows, work)

    @pl.when(pl.program_id(0) == pl.num_programs(0) - 1)
    def _():
        context = []
        for head in range(heads):
            raw = sum_ref[head]
            raw_ref[head] = raw
            unit = raw * lax.rsqrt(jnp.sum(raw * raw, axis=-1, keepdims=True) + NORM_EPS)
            context.append(unit + conv_ref[head])
        context_ref[...] = jnp.concatenate(context, axis=1).astype(BF16)


def finished(grad, tokens_ref, low_ref, weight_ref, start):
    turned = grad.T.astype(BF16)
    low_ref[...] = grad.astype(BF16)
    weight_ref[start : start + turned.shape[0], :] = dot(turned, tokens_ref[...]).astype(BF16)
    return row_sum(grad.astype(BF16).astype(F32))


def query_back_kernel(
    span_ref, place_ref, v_place_ref, slope_ref, k_near_ref, k_far_ref, v_near_ref, v_far_ref, da_ref, raw_ref,
    tokens_ref, dq_ref, d_w_ref, d_b_ref, sum_ref,
):
    heads, rows, size = raw_ref.shape
    far = is_far(span_ref, place_ref, rows)
    v_far = is_far(span_ref, v_place_ref, rows)

    @pl.when(pl.program_id(0) == 0)
    def _():
        sum_ref[...] = jnp.zeros_like(sum_ref)

    def work(part):
        for head in range(heads):
            group = slice(head * size, (head + 1) * size)
            slope = slope_ref[0, head, part, :].astype(F32)
            d_weights = dot(da_ref[head, part, :], held_at(v_far, v_near_ref, v_far_ref, group))
            d_scores = (d_weights * slope).astype(BF16)
            sum_ref[head, part, :] += dot(d_scores, held_at(far, k_near_ref, k_far_ref, group), 1, 1)

    by_chunks(span_ref, rows, work)

    @pl.when(pl.program_id(0) == pl.num_programs(0) - 1)
    def _():
        grads = [unit_back(sum_ref[head] * SLOPE, raw_ref[head]) for head in range(heads)]
        bias = finished(jnp.concatenate(grads, axis=1), tokens_ref, dq_ref, d_w_ref, 0)
        d_b_ref[...] = jnp.zeros_like(d_b_ref)
        d_b_ref[0:1, : bias.shape[1]] = bias


def key_back_kernel(
    span_ref, place_ref, v_place_ref, weight_ref, slope_ref, q_near_ref, q_far_ref, da_near_ref, da_far_ref, v_ref,
    raw_ref, dv_conv_ref, d_taps_ref, d_b_q_ref, d_w_q_ref, tokens_ref, dk_ref, dv_ref, late_ref, sum_ref, value_ref,
):
    heads, rows, size = raw_ref.shape
    columns = heads * size
    far = is_far(span_ref, place_ref, rows)

    @pl.when(pl.program_id(0) == 0)
    def _():
        sum_ref[...] = jnp.zeros_like(sum_ref)
        value_ref[...] = dv_conv_ref[...]

    def work(part):
        for head in range(heads):
            group = slice(head * size, (head + 1) * size)
            d_attn = held_at(far, da_near_ref, da_far_ref, group)
            slope = slope_ref[0, head, part, :].astype(F32)
            d_scores = (dot(v_ref[head, part, :], d_attn) * slope).astype(BF16)
            sum_ref[head, part, :] += dot(d_scores, held_at(far, q_near_ref, q_far_ref, group), 1, 1)
            value_ref[head, part, :] += dot(weight_ref[0, head, part, :], d_attn, 1, 1)

    by_chunks(span_ref, rows, work)

    @pl.when(pl.program_id(0) == pl.num_programs(0) - 1)
    def _():
        more = 3 * columns
        late_ref[more:, :] = jnp.zeros((late_ref.shape[0] - more, late_ref.shape[1]), BF16)
        late_ref[:columns, :] = d_w_q_ref[...]
        grads = [unit_back(sum_ref[head] * SLOPE, raw_ref[head]) for head in range(heads)]
        finished(jnp.concatenate(grads, axis=1), tokens_ref, dk_ref, late_ref, columns)
        grads = jnp.concatenate([value_ref[head] for head in range(heads)], axis=1)
        bias = finished(grads, tokens_ref, dv_ref, late_ref, 2 * columns)
        late_ref[more : more + 2, :columns] = jnp.concatenate(
            [d_b_q_ref[0:1, :columns], bias], axis=0
        ).astype(BF16)
        late_ref[more + 16 : more + 16 + heads, : d_taps_ref.shape[1]] = d_taps_ref[...].astype(BF16)


def conv_back_kernel(mine_ref, rim_ref, taps_ref, values_ref, d_context_ref, turned_ref, dv_ref, d_taps_ref):
    heads, rows, size = d_context_ref.shape
    for head in range(heads):
        group = slice(head * size, (head + 1) * size)
        dv_ref[head] = band_sums(taps_ref, head, mine_ref, rim_ref, turned_ref[group, :])
        values = values_ref[group, :]
        lined = jnp.zeros((8, BAND), F32)
        for start in range(0, rows, EDGE):
            pairs = dot(d_context_ref[head, start : start + EDGE, :], values[:, start : start + BAND])
            pairs = jnp.where(around_of(mine_ref, rim_ref, start), pairs, 0.0)
            for row in range(0, EDGE, 8):
                part = pairs[row : row + 8, :]
                lined = lined + (pltpu.roll(part, BAND - row, 1) if row else part)
        total = lined[0:1, :]
        for row in range(1, 8):
            total = total + pltpu.roll(lined[row : row + 1, :], BAND - row, 1)
        d_taps_ref[head : head + 1, :] = total


def normal_of(u):
    density = jnp.exp(u * u * -0.5) * (1.0 / math.sqrt(2.0 * math.pi))
    ratio = 1.0 / (1.0 + TAIL_AT * jnp.abs(u))
    tail = jnp.full_like(ratio, TAIL[-1])
    for factor in TAIL[-2::-1]:
        tail = tail * ratio + factor
    tail = tail * (ratio * density)
    return jnp.where(u >= 0.0, 1.0 - tail, tail), density


def normed_of(hidden):
    center = hidden - jnp.mean(hidden, axis=-1, keepdims=True)
    scale = lax.rsqrt(jnp.mean(center * center, axis=-1, keepdims=True) + LAYER_EPS)
    return center * scale, scale


def normed_back(grad, normed, scale, gain):
    d_normed = grad * gain
    centered = d_normed - jnp.mean(d_normed, axis=-1, keepdims=True)
    return scale * (centered - normed * jnp.mean(d_normed * normed, axis=-1, keepdims=True))


def row_sum(array):
    return jnp.sum(array, axis=0, keepdims=True)


def middle_kernel(parts, *refs):
    tokens_ref, near_ref, far_ref, vectors_ref, d_out_ref, raw_ref = refs[:6]
    contexts = [half.at[i] for half in (near_ref, far_ref) for i in range(parts // 2)]
    (
        result_ref, y_low_ref, act_ref, d_second_low_ref, d_inner_ref, d_first_ref, d_first_low_ref, sums_ref,
        d_context_ref, turned_ref, da_ref, da_turned_ref,
        normed_ref, scale_ref, mixed_ref, factor_ref, out_ref, up_ref, down_ref, sem_ref,
    ) = refs[6 + 5 * parts :]
    heads, rows, size = raw_ref.shape
    columns = heads * size
    b_out, gain_one, bias_one, b_down, gain_two, bias_two = [vectors_ref[i : i + 1, :] for i in range(6)]
    chunks = [slice(start, start + MIDDLE) for start in range(0, rows, MIDDLE)]
    targets = [(out_ref, 0, out_ref.shape[1])]
    for to in (up_ref, down_ref):
        targets += [(to, start, to.shape[1] // 2) for start in (0, to.shape[1] // 2)]
    copies = [
        [
            pltpu.make_async_copy(
                refs[6 + piece * parts + part], to.at[part, start : start + count, :], sem_ref.at[piece, part]
            )
            for part in range(parts)
        ]
        for piece, (to, start, count) in enumerate(targets)
    ]
    for of in copies:
        for part in range(parts):
            of[part].start()

    for part in range(parts):
        copies[0][part].wait()
    for chunk in chunks:
        hidden = tokens_ref[chunk, :].astype(F32) + b_out
        for part in range(parts):
            hidden = hidden + dot(contexts[part][chunk, :], out_ref[part, :columns, :])
        normed, scale = normed_of(hidden)
        normed_ref[chunk, :] = normed
        scale_ref[chunk, :] = scale
        first = normed * gain_one + bias_one
        y_low_ref[chunk, :] = first.astype(BF16)
        mixed_ref[chunk, :] = first + b_down

    for part in range(parts):
        for of in copies[1:]:
            of[part].wait()
        b_up = row_sum(out_ref[part, columns : columns + 16, :].astype(F32))
        for chunk in chunks:
            inner = dot(y_low_ref[chunk, :], up_ref[part]) + b_up
            share, density = normal_of(inner)
            act = (inner * share).astype(BF16)
            factor_ref[part, chunk, :] = share + inner * density
            if part == 0:
                act_ref[chunk, :] = act
            mixed_ref[chunk, :] += dot(act, down_ref[part])

    sums = [0.0] * 7
    for chunk in chunks:
        normed, scale = normed_of(mixed_ref[chunk, :])
        result_ref[chunk, :] = (normed * gain_two + bias_two).astype(BF16)
        grad = d_out_ref[chunk, :].astype(F32)
        d_second = normed_back(grad, normed, scale, gain_two)
        d_second_low_ref[chunk, :] = d_second.astype(BF16)
        mixed_ref[chunk, :] = d_second
        for i, array in enumerate((grad * normed, grad, d_second)):
            sums[i] = sums[i] + row_sum(array)

    for part in range(parts):
        for chunk in chunks:
            d_act = dot(d_second_low_ref[chunk, :], down_ref[part], 1, 1)
            d_inner = (d_act * factor_ref[part, chunk, :]).astype(BF16)
            if part == 0:
                d_inner_ref[chunk, :] = d_inner
                sums[6] = sums[6] + row_sum(d_inner.astype(F32))
            mixed_ref[chunk, :] += dot(d_inner, up_ref[part], 1, 1)

    for chunk in chunks:
        grad = mixed_ref[chunk, :]
        normed = normed_ref[chunk, :]
        d_first = normed_back(grad, normed, scale_ref[chunk, :], gain_one)
        d_first_ref[chunk, :] = d_first
        d_first_low = d_first.astype(BF16)
        d_first_low_ref[chunk, :] = d_first_low
        for i, array in enumerate((grad * normed, grad, d_first)):
            sums[3 + i] = sums[3 + i] + row_sum(array)
        d_context = dot(d_first_low, out_ref[0, :columns, :], 1, 1).astype(BF16).astype(F32)
        turned_ref[:, chunk] = d_context.T.astype(BF16)
        grads = []
        for head in range(heads):
            grad = d_context[:, head * size : (head + 1) * size]
            d_context_ref[head, chunk, :] = grad.astype(BF16)
            grad = unit_back(grad, raw_ref[head, chunk, :])
            da_ref[head, chunk, :] = grad.astype(BF16)
            grads.append(grad)
        da_turned_ref[:, chunk] = jnp.concatenate(grads, axis=1).T.astype(BF16)
    sums_ref[...] = jnp.zeros_like(sums_ref)
    for i in range(7):
        sums_ref[i : i + 1, :] = sums[i]


def results_kernel(
    out_ref, up_ref, down_ref, late_ref, vectors_ref, d_out_ref, d_up_ref, d_down_ref, d_qkv_ref, more_ref
):
    columns = d_out_ref.shape[0]
    d_out_ref[...] = out_ref[:columns, :].astype(F32)
    vectors_ref[...] = out_ref[columns:, :].astype(F32)
    d_up_ref[...] = up_ref[...].astype(F32)
    d_down_ref[...] = down_ref[...].astype(F32)
    for i in range(3):
        d_qkv_ref[i] = late_ref[i * columns : (i + 1) * columns, :].astype(F32)
    more_ref[...] = late_ref[3 * columns :, :].astype(F32)


HEAD = 64


def per_device(
    tokens, item_lengths, w_qkv, b_qv, taps, w_out, b_out, ln1_gain, ln1_bias, w_up, b_up, w_down, b_down,
    ln2_gain, ln2_bias, d_out,
):
    rows, features = tokens.shape
    heads, kernel = taps.shape
    radius = (kernel - 1) // 2
    columns = w_qkv.shape[2]
    size = columns // heads
    hidden = w_up.shape[1]
    blocks = lax.axis_size("seq")
    total = blocks * rows
    index = lax.axis_index("seq").astype(jnp.int32)
    first_row = index * rows
    shape = jax.ShapeDtypeStruct
    heads_wide, heads_low = shape((heads, rows, size), F32), shape((heads, rows, size), BF16)
    turned_shape, row_shape = shape((columns, rows), BF16), shape((rows, columns), BF16)
    wide_shape, low_shape = shape((rows, features), F32), shape((rows, features), BF16)

    w_turned = jnp.swapaxes(w_qkv, 1, 2)
    biases = jnp.stack([b_qv[0], jnp.zeros_like(b_qv[0]), b_qv[1]])[:, :, None]

    def project(x, which, unit, outs, *flags):
        return call(
            functools.partial(project_kernel, unit, *flags), outs, x, w_turned, biases[which],
            grid=(1,),
            in_specs=[None, pl.BlockSpec((1, columns, features), lambda *_: (which, 0, 0)), None],
            flops=2 * rows * columns * features,
        )

    masks = masks_of("seq")
    v_masks = masks[-1:] + masks[:-1]
    ahead = [(i, i + 1) for i in range(blocks - 1)]
    behind = [(i + 1, i) for i in range(blocks - 1)]

    def rimmed(turned):
        return jnp.concatenate(
            [
                lax.ppermute(turned[:, rows - EDGE :], "seq", ahead), turned,
                lax.ppermute(turned[:, :EDGE], "seq", behind),
            ],
            axis=1,
        )

    reach = EDGE - radius
    banded = jnp.pad(taps, ((0, 0), (reach, BAND - reach - kernel)))
    mirrored = jnp.pad(taps[:, ::-1], ((0, 0), (reach, BAND - reach - kernel)))
    vectors = jnp.stack([b_out, ln1_gain, ln1_bias, b_down, ln2_gain, ln2_bias, b_out, b_out])

    steps = min(total, WINDOW) // KEYS
    per = rows // KEYS
    at_of = lambda i, span_ref: span_ref[0] + jnp.minimum(i, span_ref[1] - 1)
    tile_spec = pl.BlockSpec(
        (1, heads, rows, KEYS), lambda i, span_ref, *_: (jnp.minimum(i, span_ref[1] - 1), 0, 0, 0)
    )
    items_spec = pl.BlockSpec((1, 1, KEYS), lambda i, span_ref, *_: (at_of(i, span_ref), 0, 0))
    half = blocks // 2

    def halves_of(which):
        def spec(index_of):
            return pl.BlockSpec(
                (1, columns, KEYS),
                lambda i, *refs: (index_of(refs[which][at_of(i, refs[0]) // per]), 0, at_of(i, refs[0]) % per),
            )

        return [spec(lambda place: jnp.minimum(place, half - 1)), spec(lambda place: jnp.maximum(place - half, 0))]

    def side_of(beside):
        def spec(index_of):
            return pl.BlockSpec(
                (1, columns, rows),
                lambda i, *refs: (index_of(refs[2][jnp.clip(refs[2][blocks] + beside, 0, blocks - 1)]), 0, 0),
            )

        return [spec(lambda place: jnp.minimum(place, half - 1)), spec(lambda place: jnp.maximum(place - half, 0))]

    placed, v_placed = halves_of(1), halves_of(2)
    ordered = pl.BlockSpec((1, columns, KEYS), lambda i, *refs: (at_of(i, refs[0]) // per, 0, at_of(i, refs[0]) % per))
    tiles = shape((steps, heads, rows, KEYS), BF16)
    sums = pltpu.VMEM((heads, rows, size), F32)
    pair_flops = 2 * rows * (total // 2) * columns

    def tables(item_lengths):
        count = item_lengths.shape[0]
        upto = jnp.arange(count)[None, :] <= jnp.arange(count)[:, None]
        ends = jnp.sum(jnp.where(upto, item_lengths[None, :], 0), axis=1)
        starts = first_row + CHUNK * jnp.arange(rows // CHUNK, dtype=jnp.int32)[:, None]
        lows = jnp.max(jnp.where(ends[None, :] <= starts, ends[None, :], 0), axis=1)
        highs = jnp.min(jnp.where(ends[None, :] >= starts + CHUNK, ends[None, :], total), axis=1)
        bounds = jnp.stack([lows // KEYS, (highs + KEYS - 1) // KEYS], axis=1)
        span = jnp.concatenate(
            [jnp.stack([bounds[0, 0], bounds[-1, 1] - bounds[0, 0]]), bounds.reshape(-1)]
        ).astype(jnp.int32)
        items = item_index(jnp.arange(total, dtype=jnp.int32), ends).reshape(total // KEYS, 1, KEYS)
        rim = item_index(first_row - EDGE + jnp.arange(rows + 2 * EDGE, dtype=jnp.int32), ends)[None, :]
        mine = item_index(first_row + jnp.arange(rows, dtype=jnp.int32), ends)[:, None]
        place, v_place = [jnp.concatenate([block_places("seq", order), index[None]]) for order in (masks, v_masks)]
        return (span, place, v_place), items, rim, mine, banded, mirrored, vectors

    [k_turned] = project(tokens, 1, True, [turned_shape], False, False, True)
    k_got = flipped(k_turned, "seq", masks[0])
    v_own, v_turned = project(after(tokens, k_turned), 2, False, [heads_low, turned_shape], False, True, True)
    v_got = flipped(v_turned, "seq", v_masks[0])
    far, close = masks_of("mp")
    b_high = lax.reduce_precision(b_up, 8, 7)
    b_mid = lax.reduce_precision(b_up - b_high, 8, 7)
    b_split = jnp.stack([b_high, b_mid, b_up - b_high - b_mid]).astype(BF16)
    w_out_more = jnp.concatenate([w_out, b_split, jnp.zeros((13, features), BF16)])
    up_half, down_half = w_up.shape[0] // 2, w_down.shape[0] // 2
    own = [w_out_more, w_up[:up_half], w_up[up_half:], w_down[:down_half], w_down[down_half:]]
    far_got, close_got, last_got = [], [], []
    k_got, v_got, late_tokens, own[0], own[1] = joined(k_got, v_got, tokens, own[0], own[1])
    far_got.append(flipped(own[0], "mp", far))
    k_cells = stacked(k_turned, k_got)
    v_cells = stacked(v_turned, v_got)
    for mask in masks[1:-1]:
        k_got = flipped(k_cells, "seq", mask)
        q_raw, q_own, q_turned = project(late_tokens, 0, True, [heads_wide, heads_low, turned_shape], True, True, True)
        k_raw, k_own = project(late_tokens, 1, True, [heads_wide, heads_low], True, True, False)
        if mask == masks[1]:
            far_got.append(flipped(own[1], "mp", far))
        k_got, q_own, k_own, v_cells, late_lengths, far_got[0], far_got[1], own[2] = joined(
            k_got, q_own, k_own, v_cells, item_lengths, far_got[0], far_got[1], own[2]
        )
        k_cells = stacked(k_cells, k_got)
    k_got = flipped(k_cells, "seq", masks[-1])
    for mask in v_masks[1:-1]:
        v_got = flipped(v_cells, "seq", mask)
        v_got, v_before = joined(v_got, v_cells)
        v_cells = stacked(v_before, v_got)
    scalars, items, rim, mine, banded, mirrored, vectors = tables(late_lengths)
    far_got.append(flipped(own[2], "mp", far))
    last_got += [flipped(far_got[0], "mp", close), flipped(far_got[1], "mp", close)]
    close_got = [flipped(after(array, q_own), "mp", close) for array in own]
    k_got, v_cells, mine, items, rim, vectors, close_got, far_got[2], last_got, own[3] = joined(
        k_got, v_cells, mine, items, rim, vectors, close_got, far_got[2], last_got, own[3]
    )
    v_got = flipped(v_cells, "seq", v_masks[-1])
    keys = (k_cells, k_got)
    weights, slopes = call(
        weights_kernel, [tiles, tiles], *scalars, mine, items, q_own, *keys,
        grid=(steps,), scalars=3,
        in_specs=[None, items_spec, None, *placed],
        out_specs=[tile_spec, tile_spec],
        flops=8 * pair_flops,
    )
    far_got.append(flipped(own[3], "mp", far))
    last_got.append(flipped(far_got[2], "mp", close))
    v_got, weights, q_turned, far_got[3], last_got[2], own[4] = joined(
        v_got, weights, q_turned, far_got[3], last_got[2], own[4]
    )
    values = (v_cells, v_got)
    far_got.append(flipped(own[4], "mp", far))
    last_got.append(flipped(far_got[3], "mp", close))
    q_got = flipped(q_turned, "seq", masks[0])
    context, attended, v_rim = call(
        attend_kernel, [row_shape, heads_wide, shape((columns, rows + 2 * EDGE), BF16)],
        *scalars, weights, *values, mine, rim, banded, v_turned, *values, *values,
        grid=(steps,), scalars=3,
        in_specs=[tile_spec, *v_placed, None, None, None, None, *side_of(-1), *side_of(1)],
        flops=pair_flops, scratch=[sums, sums],
    )
    q_got, context, far_got[4], last_got[3] = joined(q_got, context, far_got[4], last_got[3])
    q_cells = stacked(q_turned, q_got)
    for mask in masks[1:-1]:
        q_got = flipped(q_cells, "seq", mask)
        q_cells, q_got = joined(q_cells, q_got)
        q_cells = stacked(q_cells, q_got)
    context_got = flipped(context, "mp", far)
    last_got.append(flipped(far_got[4], "mp", close))
    parts = 4
    held = [kind[piece] for piece in range(len(own)) for kind in (own, far_got, close_got, last_got)]
    context_got, q_cells, held = joined(context_got, q_cells, held)
    context_cells = stacked(context, context_got)
    contexts = (context_cells, flipped(context_cells, "mp", close))
    q_got = flipped(q_cells, "seq", masks[-1])

    vmem = lambda a, *lead: pltpu.VMEM((*lead, *a.shape), a.dtype)
    anywhere = pl.BlockSpec(memory_space=pl.ANY)
    hidden_shape = shape((rows, hidden), BF16)
    (
        layer_output, first_low, act_own, d_second_low, d_inner_own, d_first, d_first_low, vector_sums,
        d_context, d_context_turned, da_own, da_turned,
    ) = call(
        functools.partial(middle_kernel, parts),
        [
            low_shape, low_shape, hidden_shape, low_shape, hidden_shape, wide_shape, low_shape,
            shape((16, features), F32), heads_low, turned_shape, heads_low, turned_shape,
        ],
        tokens, *contexts, vectors, d_out, attended, *held,
        grid=(1,),
        in_specs=[None] * 6 + [anywhere] * len(held),
        flops=8 * rows * parts * w_up.size,
        scratch=[
            pltpu.VMEM((rows, features), F32), pltpu.VMEM((rows, 1), F32), pltpu.VMEM((rows, features), F32),
            pltpu.VMEM((parts, rows, hidden), F32), pltpu.VMEM((parts, columns + 16, features), BF16), vmem(w_up, parts), vmem(w_down, parts),
            pltpu.SemaphoreType.DMA((len(own), parts)),
        ],
    )
    d_w_down = jnp.einsum("tf,td->fd", act_own, d_second_low, preferred_element_type=F32).astype(BF16)
    d_w_up = jnp.einsum("td,tf->df", first_low, d_inner_own, preferred_element_type=F32).astype(BF16)
    d_w_out = jnp.einsum("tc,td->cd", context, d_first_low, preferred_element_type=F32).astype(BF16)

    early = lax.psum((jnp.concatenate([d_w_out, vector_sums.astype(BF16)]), d_w_up, d_w_down), "seq")
    da_got = flipped(da_turned, "seq", masks[0])
    da_got, d_w_up, d_w_down, d_w_out, q_got, da_own, d_context_turned = joined(
        da_got, d_w_up, d_w_down, d_w_out, q_got, da_own, d_context_turned
    )
    context_rim = rimmed(d_context_turned)
    queries = (q_cells, q_got)
    da_cells = stacked(da_turned, da_got)
    [dq, d_w_q, d_b_q] = call(
        query_back_kernel, [row_shape, shape((columns, features), BF16), shape((16, features), F32)],
        *scalars, slopes, *keys, *values, da_own, q_raw, tokens,
        grid=(steps,), scalars=3,
        in_specs=[tile_spec, *placed, *v_placed, None, None, None],
        flops=3 * pair_flops, scratch=[sums],
    )
    for mask in masks[1:-1]:
        da_got = flipped(da_cells, "seq", mask)
        da_got, dq, context_rim, k_own = joined(da_got, dq, context_rim, k_own)
        da_cells = stacked(da_cells, da_got)
    da_got = flipped(da_cells, "seq", masks[-1])
    weights_back, slopes_back = call(
        weights_kernel, [tiles, tiles], *scalars, mine, items, k_own, *queries,
        grid=(steps,), scalars=3,
        in_specs=[None, items_spec, None, *placed],
        out_specs=[tile_spec, tile_spec],
        flops=8 * pair_flops,
    )
    dv_conv, d_taps_wide = call(
        conv_back_kernel, [heads_wide, shape((heads, BAND), F32)],
        mine, rim, mirrored, v_rim, d_context, context_rim,
        grid=(1,),
        flops=2 * rows * BAND * columns,
    )
    d_attended = (da_cells, da_got)
    dk, dv, late = call(
        key_back_kernel, [row_shape, row_shape, shape((3 * columns + 64, features), BF16)],
        *scalars, weights_back, slopes_back, *queries, *d_attended, v_own, k_raw, dv_conv, d_taps_wide, d_b_q, d_w_q, tokens,
        grid=(steps,), scalars=3,
        in_specs=[tile_spec, tile_spec, *placed, *placed] + [None] * 7,
        flops=4 * pair_flops, scratch=[sums, sums],
    )
    late_sum, late_stages = all_sum(late, "seq")
    d_tokens_part = sum(
        jnp.dot(part, w_turned[i], preferred_element_type=F32) for i, part in enumerate((dq, dk, dv))
    )
    d_tokens = (d_first + all_sum(d_tokens_part.astype(BF16), "mp")[0].astype(F32)).astype(BF16)
    out_and_vectors, d_w_up, d_w_down = lax.optimization_barrier((late_stages[-1], *early))[1:]
    vectors, d_w_out, d_w_up, d_w_down, d_w_qkv, more = call(
        results_kernel,
        [
            shape((16, features), F32), shape(w_out.shape, F32), shape(w_up.shape, F32), shape(w_down.shape, F32),
            shape((3, columns, features), F32), shape((64, features), F32),
        ],
        out_and_vectors, d_w_up, d_w_down, late_sum,
        grid=(1,),
    )
    d_ln2_gain, d_ln2_bias, d_b_down, d_ln1_gain, d_ln1_bias, d_b_out, d_b_up = [vectors[i] for i in range(7)]
    d_b_qv, d_taps = more[:2, :columns], more[16 : 16 + heads, reach : reach + kernel]
    return (
        layer_output, d_tokens, jnp.swapaxes(d_w_qkv, 1, 2), d_b_qv, d_taps, d_w_out, d_b_out, d_ln1_gain,
        d_ln1_bias, d_w_up, d_b_up, d_w_down, d_b_down, d_ln2_gain, d_ln2_bias,
    )


def solution(mesh):
    placed = (
        P("seq", None), P(), P(None, None, "mp"), P(None, "mp"), P("mp", None), P("mp", None), P(), P(), P(),
        P(None, "mp"), P("mp"), P("mp", None), P(), P(), P(), P("seq", None),
    )
    given = (
        P("seq", None), P("seq", None), P(None, None, "mp"), P(None, "mp"), P("mp", None), P("mp", None), P(),
        P(), P(), P(None, "mp"), P("mp"), P("mp", None), P(), P(), P(),
    )
    return jax.shard_map(per_device, mesh=mesh, in_specs=placed, out_specs=given, check_vma=False)
```

```python
import functools
import math

import jax
import jax.numpy as jnp
from jax import lax
from jax.experimental import pallas as pl
from jax.experimental.pallas import tpu as pltpu
from jax.sharding import PartitionSpec as P

SHRINK = 0.95
NORM_EPS = 1e-06
LAYER_EPS = 1e-05
F32 = jnp.float32
BF16 = jnp.bfloat16
KEYS = 256
CHUNK = 256
EDGE = 128
BAND = 3 * EDGE
MIDDLE = 256
WINDOW = 9216
VMEM_BYTES = 56 * 1024 * 1024
SQUARE_OF_V = (
    0.9999936361319989,
    -1.2731008162270503,
    0.4040306859655804,
    -0.20598641392473288,
    0.11615118744625774,
    -0.05772567810293111,
    0.02001158958170149,
    -0.00337422878652264,
)
SQUARE = tuple(factor * (0.5 * SHRINK) ** (0.5 * power) for power, factor in enumerate(SQUARE_OF_V))
SLOPE = 8.0 / math.pi
TAIL_AT = 0.2316419
TAIL = (0.319381530, -0.356563782, 1.781477937, -1.821255978, 1.330274429)


def dot(left, right, left_dim=1, right_dim=0):
    return lax.dot_general(
        left, right, (((left_dim,), (right_dim,)), ((), ())), preferred_element_type=F32
    )


def flipped(cells, axis, mask):
    return lax.ppermute(cells, axis, [(i, i ^ mask) for i in range(lax.axis_size(axis))])


def masks_of(axis):
    return [1 << bit for bit in range(lax.axis_size(axis).bit_length() - 2, -1, -1)]


def block_places(axis, masks):
    apart = jnp.arange(lax.axis_size(axis), dtype=jnp.int32) ^ lax.axis_index(axis).astype(jnp.int32)
    place = jnp.zeros_like(apart)
    for bit, mask in enumerate(masks):
        place = place | (jnp.where((apart & mask) != 0, 1, 0) << bit)
    return place


def halves_sent(cells, axis, mask):
    half = cells.shape[0] // 2
    upper = (lax.axis_index(axis) & mask) != 0
    sent = lax.dynamic_slice_in_dim(cells, jnp.where(upper, 0, half), half)
    kept = lax.dynamic_slice_in_dim(cells, jnp.where(upper, half, 0), half)
    return kept, flipped(sent, axis, mask)


def added(kept, got):
    return (kept.astype(F32) + got.astype(F32)).astype(BF16)


def united(cells, got, axis, mask):
    upper = (lax.axis_index(axis) & mask) != 0
    return jnp.concatenate([jnp.where(upper, got, cells), jnp.where(upper, cells, got)], axis=0)


class Chain:
    def __init__(self, cells, axis):
        masks = masks_of(axis)[::-1]
        self.cells, self.axis = cells, axis
        self.steps = [("halve", m) for m in masks[:-1]] + [("whole", masks[-1])]
        self.steps += [("gather", m) for m in masks[-2::-1]]
        self.at, self.got = 0, None

    def start(self):
        kind, mask = self.steps[self.at]
        if kind == "halve":
            self.cells, self.got = halves_sent(self.cells, self.axis, mask)
        else:
            self.got = flipped(self.cells, self.axis, mask)

    def finish(self):
        kind, mask = self.steps[self.at]
        self.at += 1
        if kind == "gather":
            self.cells = united(self.cells, self.got, self.axis, mask)
        else:
            self.cells = added(self.cells, self.got)

    @property
    def left(self):
        return len(self.steps) - self.at


def round_end(chains, *arrays):
    gots = [chain.got for chain in chains]
    *arrays, gots, cells = joined(*arrays, gots, [chain.cells for chain in chains])
    for chain, got, kept in zip(chains, gots, cells):
        chain.got, chain.cells = got, kept
        chain.finish()
    return arrays


def after(arrays, *earlier):
    return lax.optimization_barrier((arrays, *earlier))[0]


def joined(*arrays):
    return lax.optimization_barrier(arrays)


def stacked(*cells):
    return jnp.concatenate([part if part.ndim == 3 else part[None] for part in cells], axis=0)


def item_index(positions, ends):
    inside = (positions >= 0) & (positions < ends[-1])
    counted = jnp.sum((positions[:, None] >= ends[None, :]).astype(jnp.int32), axis=1)
    return jnp.where(inside, counted, -1)


def call(kernel, out_shape, *args, grid=(), in_specs=None, out_specs=None, scalars=0, flops=0, scratch=()):
    whole = lambda a: pl.BlockSpec(a.shape, lambda *_, n=len(a.shape): (0,) * n)
    ins = [whole(a) if s is None else s for a, s in zip(args[scalars:], in_specs or [None] * 99)]
    outs = [whole(a) if s is None else s for a, s in zip(out_shape, out_specs or [None] * 99)]
    moved = sum(a.size * a.dtype.itemsize for a in (*args, *out_shape))
    return pl.pallas_call(
        kernel,
        out_shape=out_shape,
        grid_spec=pltpu.PrefetchScalarGridSpec(
            num_scalar_prefetch=scalars,
            grid=grid,
            in_specs=ins,
            out_specs=outs,
            scratch_shapes=list(scratch),
        ),
        compiler_params=pltpu.CompilerParams(vmem_limit_bytes=VMEM_BYTES),
        cost_estimate=pl.CostEstimate(flops=1, bytes_accessed=1, transcendentals=0),
    )(*args)


def project_kernel(unit, raw, own, turned, tokens_ref, w_ref, bias_ref, *out_refs):
    out_refs = list(out_refs)
    raw_ref = out_refs.pop(0) if raw else None
    own_ref = out_refs.pop(0) if own else None
    turned_ref = out_refs.pop(0) if turned else None
    product = dot(w_ref[0], tokens_ref[...], 1, 1) + bias_ref[...]
    size = HEAD
    for head in range(product.shape[0] // size):
        part = product[head * size : (head + 1) * size, :]
        if raw:
            raw_ref[head] = part.T
        if unit:
            part = part * lax.rsqrt(jnp.sum(part * part, axis=0, keepdims=True) + NORM_EPS)
        if turned:
            turned_ref[head * size : (head + 1) * size, :] = part.astype(BF16)
        if own:
            own_ref[head] = part.T.astype(BF16)


def square_of(half):
    root = half * lax.rsqrt(half)
    square = jnp.full_like(root, SQUARE[-1])
    for factor in SQUARE[-2::-1]:
        square = square * root + factor
    return square


def item_of(positions, ends_ref):
    count = jnp.zeros_like(positions)
    for item in range(ends_ref.shape[0]):
        count = count + (positions >= ends_ref[item]).astype(jnp.int32)
    return jnp.where(positions < 0, -1, count)


def own_items(place_ref, ends_ref, rows):
    first = place_ref[place_ref.shape[0] - 1] * rows
    return item_of(first + lax.broadcasted_iota(jnp.int32, (rows, 1), 0), ends_ref)


def rim_items(place_ref, ends_ref, rows):
    first = place_ref[place_ref.shape[0] - 1] * rows - EDGE
    return item_of(first + lax.broadcasted_iota(jnp.int32, (1, rows + 2 * EDGE), 1), ends_ref)


def tile_of(span_ref):
    return span_ref[0] + jnp.minimum(pl.program_id(0), span_ref[1] - 1)


def held_at(far, near_ref, far_ref, group):
    return jnp.where(far, far_ref[0, group, :], near_ref[0, group, :])


def is_far(span_ref, place_ref, rows):
    return place_ref[tile_of(span_ref) // (rows // KEYS)] >= (place_ref.shape[0] - 1) // 2


def by_chunks(span_ref, rows, work):
    tile = span_ref[0] + pl.program_id(0)
    here = pl.program_id(0) < span_ref[1]
    meets = [
        (tile >= span_ref[2 + 2 * chunk]) & (tile < span_ref[3 + 2 * chunk]) for chunk in range(rows // CHUNK)
    ]
    every = functools.reduce(lambda x, y: x & y, meets)

    @pl.when(here & every)
    def _():
        work(slice(0, rows))

    for chunk, meet in enumerate(meets):

        @pl.when(here & meet & jnp.logical_not(every))
        def _(chunk=chunk):
            work(slice(chunk * CHUNK, (chunk + 1) * CHUNK))


def weights_kernel(
    span_ref, place_ref, v_place_ref, ends_ref, own_ref, near_ref, far_ref, weight_ref, slope_ref, mine_ref
):
    heads, rows, size = own_ref.shape
    far = is_far(span_ref, place_ref, rows)

    @pl.when(pl.program_id(0) == 0)
    def _():
        mine_ref[...] = own_items(place_ref, ends_ref, rows)

    def work(part):
        positions = tile_of(span_ref) * KEYS + lax.broadcasted_iota(jnp.int32, (1, KEYS), 1)
        same = mine_ref[part, :] == item_of(positions, ends_ref)
        for head in range(heads):
            scores = dot(own_ref[head, part, :], held_at(far, near_ref, far_ref, slice(head * size, (head + 1) * size)))
            half = 1.0 / SHRINK - scores
            square = square_of(half)
            fourth = square * square
            weight = jnp.where(same, fourth * fourth, 0.0)
            weight_ref[0, head, part, :] = weight.astype(BF16)
            slope = weight * lax.rsqrt(square * (half * (1.0 / SHRINK + scores)))
            slope_ref[0, head, part, :] = slope.astype(BF16)

    by_chunks(span_ref, rows, work)


def unit_back(grad, raw):
    scale = lax.rsqrt(jnp.sum(raw * raw, axis=-1, keepdims=True) + NORM_EPS)
    unit = raw * scale
    return scale * (grad - unit * jnp.sum(unit * grad, axis=-1, keepdims=True))


def split_low(wide):
    high = wide.astype(BF16)
    return high, (wide - high.astype(F32)).astype(BF16)


def band_of(taps_row):
    return pltpu.roll(jnp.broadcast_to(taps_row, (EDGE, BAND)), 0, 1, stride=1, stride_axis=0)


def around_of(mine, rim, start):
    return mine[start : start + EDGE, :] == rim[:, start : start + BAND]


def band_sums(taps_ref, head, mine, rim, values):
    band = band_of(taps_ref[head : head + 1, :])
    out = []
    for start in range(0, mine.shape[0], EDGE):
        high, low = split_low(jnp.where(around_of(mine, rim, start), band, 0.0))
        near = values[:, start : start + BAND]
        out.append(dot(high, near, 1, 1) + dot(low, near, 1, 1))
    return jnp.concatenate(out, axis=0)


def rim_values(v_place_ref, sides, own_ref, group):
    index, blocks, rows = v_place_ref[v_place_ref.shape[0] - 1], v_place_ref.shape[0] - 1, own_ref.shape[1]
    ends = []
    for (near_ref, far_ref), beside, part in zip(sides, (-1, 1), (slice(rows - EDGE, rows), slice(0, EDGE))):
        far = v_place_ref[jnp.clip(index + beside, 0, blocks - 1)] >= blocks // 2
        ends.append(jnp.where(far, far_ref[0, group, part], near_ref[0, group, part]))
    return jnp.concatenate([ends[0], own_ref[group, :], ends[1]], axis=1)


def attend_kernel(
    span_ref, place_ref, v_place_ref, ends_ref, weight_ref, v_near_ref, v_far_ref, taps_ref, own_ref,
    before_near_ref, before_far_ref, after_near_ref, after_far_ref, context_ref, raw_ref, v_rim_ref, sum_ref, conv_ref,
):
    heads, rows, size = raw_ref.shape
    far = is_far(span_ref, v_place_ref, rows)

    @pl.when(pl.program_id(0) == 0)
    def _():
        sides = ((before_near_ref, before_far_ref), (after_near_ref, after_far_ref))
        mine, rim = own_items(place_ref, ends_ref, rows), rim_items(place_ref, ends_ref, rows)
        for head in range(heads):
            group = slice(head * size, (head + 1) * size)
            values = rim_values(v_place_ref, sides, own_ref, group)
            v_rim_ref[group, :] = values
            conv_ref[head] = band_sums(taps_ref, head, mine, rim, values)
        sum_ref[...] = jnp.zeros_like(sum_ref)

    def work(part):
        for head in range(heads):
            values = held_at(far, v_near_ref, v_far_ref, slice(head * size, (head + 1) * size))
            sum_ref[head, part, :] += dot(weight_ref[0, head, part, :], values, 1, 1)

    by_chunks(span_ref, rows, work)

    @pl.when(pl.program_id(0) == pl.num_programs(0) - 1)
    def _():
        context = []
        for head in range(heads):
            raw = sum_ref[head]
            raw_ref[head] = raw
            unit = raw * lax.rsqrt(jnp.sum(raw * raw, axis=-1, keepdims=True) + NORM_EPS)
            context.append(unit + conv_ref[head])
        context_ref[...] = jnp.concatenate(context, axis=1).astype(BF16)


def finished(grad, tokens_ref, low_ref, weight_ref, start):
    turned = grad.T.astype(BF16)
    low_ref[...] = grad.astype(BF16)
    weight_ref[start : start + turned.shape[0], :] = dot(turned, tokens_ref[...]).astype(BF16)
    return row_sum(grad.astype(BF16).astype(F32))


def query_back_kernel(
    span_ref, place_ref, v_place_ref, ends_ref, slope_ref, k_near_ref, k_far_ref, v_near_ref, v_far_ref, da_ref, raw_ref,
    tokens_ref, dq_ref, d_w_ref, d_b_ref, sum_ref,
):
    heads, rows, size = raw_ref.shape
    far = is_far(span_ref, place_ref, rows)
    v_far = is_far(span_ref, v_place_ref, rows)

    @pl.when(pl.program_id(0) == 0)
    def _():
        sum_ref[...] = jnp.zeros_like(sum_ref)

    def work(part):
        for head in range(heads):
            group = slice(head * size, (head + 1) * size)
            slope = slope_ref[0, head, part, :].astype(F32)
            d_weights = dot(da_ref[head, part, :], held_at(v_far, v_near_ref, v_far_ref, group))
            d_scores = (d_weights * slope).astype(BF16)
            sum_ref[head, part, :] += dot(d_scores, held_at(far, k_near_ref, k_far_ref, group), 1, 1)

    by_chunks(span_ref, rows, work)

    @pl.when(pl.program_id(0) == pl.num_programs(0) - 1)
    def _():
        grads = [unit_back(sum_ref[head] * SLOPE, raw_ref[head]) for head in range(heads)]
        bias = finished(jnp.concatenate(grads, axis=1), tokens_ref, dq_ref, d_w_ref, 0)
        d_b_ref[...] = jnp.zeros_like(d_b_ref)
        d_b_ref[0:1, : bias.shape[1]] = bias


def key_back_kernel(
    span_ref, place_ref, v_place_ref, ends_ref, weight_ref, slope_ref, q_near_ref, q_far_ref, da_near_ref, da_far_ref, v_ref,
    raw_ref, dv_conv_ref, d_taps_ref, d_b_q_ref, d_w_q_ref, tokens_ref, dk_ref, dv_ref, late_ref, sum_ref, value_ref,
):
    heads, rows, size = raw_ref.shape
    columns = heads * size
    far = is_far(span_ref, place_ref, rows)

    @pl.when(pl.program_id(0) == 0)
    def _():
        sum_ref[...] = jnp.zeros_like(sum_ref)
        value_ref[...] = dv_conv_ref[...]

    def work(part):
        for head in range(heads):
            group = slice(head * size, (head + 1) * size)
            d_attn = held_at(far, da_near_ref, da_far_ref, group)
            slope = slope_ref[0, head, part, :].astype(F32)
            d_scores = (dot(v_ref[head, part, :], d_attn) * slope).astype(BF16)
            sum_ref[head, part, :] += dot(d_scores, held_at(far, q_near_ref, q_far_ref, group), 1, 1)
            value_ref[head, part, :] += dot(weight_ref[0, head, part, :], d_attn, 1, 1)

    by_chunks(span_ref, rows, work)

    @pl.when(pl.program_id(0) == pl.num_programs(0) - 1)
    def _():
        more = 3 * columns
        late_ref[more:, :] = jnp.zeros((late_ref.shape[0] - more, late_ref.shape[1]), BF16)
        late_ref[:columns, :] = d_w_q_ref[...]
        grads = [unit_back(sum_ref[head] * SLOPE, raw_ref[head]) for head in range(heads)]
        finished(jnp.concatenate(grads, axis=1), tokens_ref, dk_ref, late_ref, columns)
        grads = jnp.concatenate([value_ref[head] for head in range(heads)], axis=1)
        bias = finished(grads, tokens_ref, dv_ref, late_ref, 2 * columns)
        late_ref[more : more + 2, :columns] = jnp.concatenate(
            [d_b_q_ref[0:1, :columns], bias], axis=0
        ).astype(BF16)
        late_ref[more + 16 : more + 16 + heads, : d_taps_ref.shape[1]] = d_taps_ref[...].astype(BF16)


def conv_back_kernel(place_ref, ends_ref, taps_ref, values_ref, d_context_ref, turned_ref, dv_ref, d_taps_ref):
    heads, rows, size = d_context_ref.shape
    mine, rim = own_items(place_ref, ends_ref, rows), rim_items(place_ref, ends_ref, rows)
    for head in range(heads):
        group = slice(head * size, (head + 1) * size)
        dv_ref[head] = band_sums(taps_ref, head, mine, rim, turned_ref[group, :])
        values = values_ref[group, :]
        lined = jnp.zeros((8, BAND), F32)
        for start in range(0, rows, EDGE):
            pairs = dot(d_context_ref[head, start : start + EDGE, :], values[:, start : start + BAND])
            pairs = jnp.where(around_of(mine, rim, start), pairs, 0.0)
            for row in range(0, EDGE, 8):
                part = pairs[row : row + 8, :]
                lined = lined + (pltpu.roll(part, BAND - row, 1) if row else part)
        total = lined[0:1, :]
        for row in range(1, 8):
            total = total + pltpu.roll(lined[row : row + 1, :], BAND - row, 1)
        d_taps_ref[head : head + 1, :] = total


def normal_of(u):
    density = jnp.exp(u * u * -0.5) * (1.0 / math.sqrt(2.0 * math.pi))
    ratio = 1.0 / (1.0 + TAIL_AT * jnp.abs(u))
    tail = jnp.full_like(ratio, TAIL[-1])
    for factor in TAIL[-2::-1]:
        tail = tail * ratio + factor
    tail = tail * (ratio * density)
    return jnp.where(u >= 0.0, 1.0 - tail, tail), density


def normed_of(hidden):
    center = hidden - jnp.mean(hidden, axis=-1, keepdims=True)
    scale = lax.rsqrt(jnp.mean(center * center, axis=-1, keepdims=True) + LAYER_EPS)
    return center * scale, scale


def normed_back(grad, normed, scale, gain):
    d_normed = grad * gain
    centered = d_normed - jnp.mean(d_normed, axis=-1, keepdims=True)
    return scale * (centered - normed * jnp.mean(d_normed * normed, axis=-1, keepdims=True))


def row_sum(array):
    return jnp.sum(array, axis=0, keepdims=True)


def middle_kernel(parts, *refs):
    tokens_ref, near_ref, far_ref, vectors_ref, d_out_ref, raw_ref = refs[:6]
    contexts = [half.at[i] for half in (near_ref, far_ref) for i in range(parts // 2)]
    (
        result_ref, d_first_ref, d_rest_ref, d_w_down_ref,
        d_context_ref, turned_ref, da_ref, da_turned_ref,
        y_low_ref, act_ref, d_second_low_ref, d_inner_ref, d_first_low_ref,
        normed_ref, scale_ref, mixed_ref, factor_ref, out_ref, up_ref, down_ref, sem_ref,
    ) = refs[6 + 5 * parts :]
    heads, rows, size = raw_ref.shape
    columns = heads * size
    b_out, gain_one, bias_one, b_down, gain_two, bias_two = [vectors_ref[i : i + 1, :] for i in range(6)]
    chunks = [slice(start, start + MIDDLE) for start in range(0, rows, MIDDLE)]
    up_cut, down_cut = up_ref.shape[1] // 3, 2 * down_ref.shape[1] // 3
    targets = [
        (0, 0, up_ref, 0, up_cut),
        (1, 0, up_ref, up_cut, up_ref.shape[1] - up_cut),
        (2, 0, down_ref, 0, down_cut),
        (3, 0, down_ref, down_cut, down_ref.shape[1] - down_cut),
        (4, 0, out_ref, 0, out_ref.shape[1]),
    ]
    copies = [
        [
            pltpu.make_async_copy(
                refs[6 + piece * parts + part].at[first : first + count, :],
                to.at[part, start : start + count, :],
                sem_ref.at[i, part],
            )
            for part in range(parts)
        ]
        for i, (piece, first, to, start, count) in enumerate(targets)
    ]
    copies = copies[-1:] + copies[:-1]
    for of in copies:
        for part in range(parts):
            of[part].start()

    for part in range(parts):
        copies[0][part].wait()
    for chunk in chunks:
        hidden = tokens_ref[chunk, :].astype(F32) + b_out
        for part in range(parts):
            hidden = hidden + dot(contexts[part][chunk, :], out_ref[part, :columns, :])
        normed, scale = normed_of(hidden)
        normed_ref[chunk, :] = normed
        scale_ref[chunk, :] = scale
        first = normed * gain_one + bias_one
        y_low_ref[chunk, :] = first.astype(BF16)
        mixed_ref[chunk, :] = first + b_down

    for part in range(parts):
        for of in copies[1:]:
            of[part].wait()
        b_up = row_sum(out_ref[part, columns : columns + 16, :].astype(F32))
        for chunk in chunks:
            inner = dot(y_low_ref[chunk, :], up_ref[part]) + b_up
            share, density = normal_of(inner)
            act = (inner * share).astype(BF16)
            factor_ref[part, chunk, :] = share + inner * density
            if part == 0:
                act_ref[chunk, :] = act
            mixed_ref[chunk, :] += dot(act, down_ref[part])

    sums = [0.0] * 7
    for chunk in chunks:
        normed, scale = normed_of(mixed_ref[chunk, :])
        result_ref[chunk, :] = (normed * gain_two + bias_two).astype(BF16)
        grad = d_out_ref[chunk, :].astype(F32)
        d_second = normed_back(grad, normed, scale, gain_two)
        d_second_low_ref[chunk, :] = d_second.astype(BF16)
        mixed_ref[chunk, :] = d_second
        for i, array in enumerate((grad * normed, grad, d_second)):
            sums[i] = sums[i] + row_sum(array)

    d_w_down_ref[...] = dot(act_ref[...], d_second_low_ref[...], 0, 0).astype(BF16)
    for part in range(parts):
        for chunk in chunks:
            d_act = dot(d_second_low_ref[chunk, :], down_ref[part], 1, 1)
            d_inner = (d_act * factor_ref[part, chunk, :]).astype(BF16)
            if part == 0:
                d_inner_ref[chunk, :] = d_inner
                sums[6] = sums[6] + row_sum(d_inner.astype(F32))
            mixed_ref[chunk, :] += dot(d_inner, up_ref[part], 1, 1)
        if part == 0:
            d_rest_ref[: y_low_ref.shape[1], :] = dot(y_low_ref[...], d_inner_ref[...], 0, 0).astype(BF16)

    for chunk in chunks:
        grad = mixed_ref[chunk, :]
        normed = normed_ref[chunk, :]
        d_first = normed_back(grad, normed, scale_ref[chunk, :], gain_one)
        d_first_ref[chunk, :] = d_first
        d_first_low = d_first.astype(BF16)
        d_first_low_ref[chunk, :] = d_first_low
        for i, array in enumerate((grad * normed, grad, d_first)):
            sums[3 + i] = sums[3 + i] + row_sum(array)
        d_context = dot(d_first_low, out_ref[0, :columns, :], 1, 1).astype(BF16).astype(F32)
        turned_ref[:, chunk] = d_context.T.astype(BF16)
        grads = []
        for head in range(heads):
            grad = d_context[:, head * size : (head + 1) * size]
            d_context_ref[head, chunk, :] = grad.astype(BF16)
            grad = unit_back(grad, raw_ref[head, chunk, :])
            da_ref[head, chunk, :] = grad.astype(BF16)
            grads.append(grad)
        da_turned_ref[:, chunk] = jnp.concatenate(grads, axis=1).T.astype(BF16)
    at_out = y_low_ref.shape[1]
    d_rest_ref[at_out : at_out + columns, :] = dot(contexts[0][...], d_first_low_ref[...], 0, 0).astype(BF16)
    sums.append(jnp.zeros((9, sums[0].shape[1]), F32))
    d_rest_ref[at_out + columns :, :] = jnp.concatenate(sums, axis=0).astype(BF16)


def whole_of(upper_ref, own_ref, got_ref):
    own, got, upper = own_ref[...], got_ref[...], upper_ref[0] != 0
    return jnp.concatenate([jnp.where(upper, got, own), jnp.where(upper, own, got)], axis=0).astype(F32)


def late_results_kernel(upper_ref, late_ref, got_ref, d_w_ref, d_b_ref, d_taps_ref):
    late = whole_of(upper_ref, late_ref, got_ref)
    columns = d_w_ref.shape[1]
    for i in range(3):
        d_w_ref[i] = late[i * columns : (i + 1) * columns, :]
    more = 3 * columns
    d_b_ref[...] = late[more : more + 2, :columns]
    heads, kernel = d_taps_ref.shape
    start = EDGE - (kernel - 1) // 2
    d_taps_ref[...] = late[more + 16 : more + 16 + heads, start : start + kernel]


def results_kernel(
    upper_ref, down_ref, rest_ref, down_got_ref, rest_got_ref, d_out_ref, vectors_ref, d_up_ref, d_down_ref
):
    columns = d_out_ref.shape[0]
    d_down_ref[...] = whole_of(upper_ref, down_ref, down_got_ref)
    rest = whole_of(upper_ref, rest_ref, rest_got_ref)
    at_out = d_up_ref.shape[0]
    d_up_ref[...] = rest[:at_out, :]
    d_out_ref[...] = rest[at_out : at_out + columns, :]
    vectors_ref[...] = rest[at_out + columns :, :]


HEAD = 64


def per_device(
    tokens, item_lengths, w_qkv, b_qv, taps, w_out, b_out, ln1_gain, ln1_bias, w_up, b_up, w_down, b_down,
    ln2_gain, ln2_bias, d_out,
):
    rows, features = tokens.shape
    heads, kernel = taps.shape
    radius = (kernel - 1) // 2
    columns = w_qkv.shape[2]
    size = columns // heads
    hidden = w_up.shape[1]
    blocks = lax.axis_size("seq")
    total = blocks * rows
    index = lax.axis_index("seq").astype(jnp.int32)
    first_row = index * rows
    shape = jax.ShapeDtypeStruct
    heads_wide, heads_low = shape((heads, rows, size), F32), shape((heads, rows, size), BF16)
    turned_shape, row_shape = shape((columns, rows), BF16), shape((rows, columns), BF16)
    wide_shape, low_shape = shape((rows, features), F32), shape((rows, features), BF16)

    w_turned = jnp.swapaxes(w_qkv, 1, 2)
    biases = jnp.stack([b_qv[0], jnp.zeros_like(b_qv[0]), b_qv[1]])[:, :, None]

    def project(x, which, unit, outs, *flags):
        return call(
            functools.partial(project_kernel, unit, *flags), outs, x, w_turned, biases[which],
            grid=(1,),
            in_specs=[None, pl.BlockSpec((1, columns, features), lambda *_: (which, 0, 0)), None],
            flops=2 * rows * columns * features,
        )

    masks = masks_of("seq")
    v_masks = masks[-1:] + masks[:-1]
    ahead = [(i, i + 1) for i in range(blocks - 1)]
    behind = [(i + 1, i) for i in range(blocks - 1)]

    reach = EDGE - radius

    def rims_of(turned):
        ends = turned[:, rows - EDGE :], turned[:, :EDGE]
        return [lax.ppermute(end, "seq", pairs) for end, pairs in zip(ends, (ahead, behind))]

    reach = EDGE - radius

    steps = min(total, WINDOW) // KEYS
    per = rows // KEYS
    at_of = lambda i, span_ref: span_ref[0] + jnp.minimum(i, span_ref[1] - 1)
    tile_spec = pl.BlockSpec(
        (1, heads, rows, KEYS), lambda i, span_ref, *_: (jnp.minimum(i, span_ref[1] - 1), 0, 0, 0)
    )
    half = blocks // 2

    def halves_of(which):
        def spec(index_of):
            return pl.BlockSpec(
                (1, columns, KEYS),
                lambda i, *refs: (index_of(refs[which][at_of(i, refs[0]) // per]), 0, at_of(i, refs[0]) % per),
            )

        return [spec(lambda place: jnp.minimum(place, half - 1)), spec(lambda place: jnp.maximum(place - half, 0))]

    def side_of(beside):
        def spec(index_of):
            return pl.BlockSpec(
                (1, columns, rows),
                lambda i, *refs: (index_of(refs[2][jnp.clip(refs[2][blocks] + beside, 0, blocks - 1)]), 0, 0),
            )

        return [spec(lambda place: jnp.minimum(place, half - 1)), spec(lambda place: jnp.maximum(place - half, 0))]

    placed, v_placed = halves_of(1), halves_of(2)
    ordered = pl.BlockSpec((1, columns, KEYS), lambda i, *refs: (at_of(i, refs[0]) // per, 0, at_of(i, refs[0]) % per))
    tiles = shape((steps, heads, rows, KEYS), BF16)
    sums = pltpu.VMEM((heads, rows, size), F32)
    pair_flops = 2 * rows * (total // 2) * columns

    def tables(item_lengths):
        count = item_lengths.shape[0]
        upto = jnp.arange(count)[None, :] <= jnp.arange(count)[:, None]
        ends = jnp.sum(jnp.where(upto, item_lengths[None, :], 0), axis=1)
        starts = first_row + CHUNK * jnp.arange(rows // CHUNK, dtype=jnp.int32)[:, None]
        lows = jnp.max(jnp.where(ends[None, :] <= starts, ends[None, :], 0), axis=1)
        highs = jnp.min(jnp.where(ends[None, :] >= starts + CHUNK, ends[None, :], total), axis=1)
        bounds = jnp.stack([lows // KEYS, (highs + KEYS - 1) // KEYS], axis=1)
        span = jnp.concatenate(
            [jnp.stack([bounds[0, 0], bounds[-1, 1] - bounds[0, 0]]), bounds.reshape(-1)]
        ).astype(jnp.int32)
        place, v_place = [jnp.concatenate([block_places("seq", order), index[None]]) for order in (masks, v_masks)]
        return span, place, v_place, ends

    small = taps, [b_out, ln1_gain, ln1_bias, b_down, ln2_gain, ln2_bias]
    [k_turned] = project(tokens, 1, True, [turned_shape], False, False, True)
    k_got = flipped(k_turned, "seq", masks[0])
    v_own, v_turned = project(after(tokens, k_turned), 2, False, [heads_low, turned_shape], False, True, True)
    v_got = flipped(v_turned, "seq", v_masks[0])
    far, close = masks_of("mp")
    b_high = lax.reduce_precision(b_up, 8, 7)
    b_mid = lax.reduce_precision(b_up - b_high, 8, 7)
    b_split = jnp.stack([b_high, b_mid, b_up - b_high - b_mid]).astype(BF16)
    w_out_more = jnp.concatenate([w_out, b_split, jnp.zeros((13, features), BF16)])
    up_cut, down_cut = w_up.shape[0] // 3, 2 * w_down.shape[0] // 3
    own = [w_up[:up_cut], w_up[up_cut:], w_down[:down_cut], w_down[down_cut:], w_out_more]
    far_got, last_got = [None] * 5, [None] * 5
    close_got = [flipped(after(array, v_turned), "mp", close) for array in own[:2]]
    k_got, v_got, late_tokens, late_lengths, own, close_got = joined(
        k_got, v_got, tokens, item_lengths, own, close_got
    )
    k_cells = stacked(k_turned, k_got)
    v_cells = stacked(v_turned, v_got)
    k_got = flipped(k_cells, "seq", masks[1])
    late_tokens, late_lengths, own = after((late_tokens, late_lengths, own), k_cells)
    far_got[0] = flipped(own[0], "mp", far)
    q_raw, q_own, q_turned = project(late_tokens, 0, True, [heads_wide, heads_low, turned_shape], True, True, True)
    scalars = tables(late_lengths)
    close_got += [flipped(array, "mp", close) for array in own[2:]]
    k_got, v_cells, q_own, scalars, far_got[0], own, late_tokens, small, close_got = joined(
        k_got, v_cells, q_own, scalars, far_got[0], own, late_tokens, small, close_got
    )
    k_cells = stacked(k_cells, k_got)
    for mask in masks[2:-1]:
        k_got, k_cells = joined(flipped(k_cells, "seq", mask), k_cells)
        k_cells = stacked(k_cells, k_got)
    for mask in v_masks[1:-2]:
        v_got, v_cells = joined(flipped(v_cells, "seq", mask), v_cells)
        v_cells = stacked(v_cells, v_got)
    k_got = flipped(k_cells, "seq", masks[-1])
    v_got = flipped(v_cells, "seq", v_masks[-2])
    own, far_got[0], late_tokens, small = after((own, far_got[0], late_tokens, small), k_cells)
    k_raw, k_own = project(late_tokens, 1, True, [heads_wide, heads_low], True, True, False)
    taps, vectors = small
    vectors = jnp.stack([*vectors, vectors[0], vectors[0]])
    banded = jnp.pad(taps, ((0, 0), (reach, BAND - reach - kernel)))
    mirrored = jnp.pad(taps[:, ::-1], ((0, 0), (reach, BAND - reach - kernel)))
    far_got[1] = flipped(own[1], "mp", far)
    last_got[0] = flipped(far_got[0], "mp", close)
    k_got, v_got, v_cells, far_got[1], last_got[0], own[2], q_own, k_own, k_raw, banded = joined(
        k_got, v_got, v_cells, far_got[1], last_got[0], own[2], q_own, k_own, k_raw, banded
    )
    v_cells = stacked(v_cells, v_got)
    v_got = flipped(v_cells, "seq", v_masks[-1])
    keys = (k_cells, k_got)
    weights, slopes = call(
        weights_kernel, [tiles, tiles], *scalars, q_own, *keys,
        grid=(steps,), scalars=4,
        in_specs=[None, *placed],
        out_specs=[tile_spec, tile_spec],
        flops=8 * pair_flops, scratch=[pltpu.VMEM((rows, 1), jnp.int32)],
    )
    far_got[2], last_got[1] = flipped(own[2], "mp", far), flipped(far_got[1], "mp", close)
    v_got, weights, q_turned, far_got[2], last_got[1], own[3] = joined(
        v_got, weights, q_turned, far_got[2], last_got[1], own[3]
    )
    values = (v_cells, v_got)
    far_got[3], far_got[4] = [flipped(own[piece], "mp", far) for piece in (3, 4)]
    last_got[2] = flipped(far_got[2], "mp", close)
    q_got = flipped(q_turned, "seq", masks[0])
    context, attended, v_rim = call(
        attend_kernel, [row_shape, heads_wide, shape((columns, rows + 2 * EDGE), BF16)],
        *scalars, weights, *values, banded, v_turned, *values, *values,
        grid=(steps,), scalars=4,
        in_specs=[tile_spec, *v_placed, None, None, *side_of(-1), *side_of(1)],
        flops=pair_flops, scratch=[sums, sums],
    )
    q_got, context, far_got[3], far_got[4], last_got[2] = joined(
        q_got, context, far_got[3], far_got[4], last_got[2]
    )
    q_cells = stacked(q_turned, q_got)
    q_got = flipped(q_cells, "seq", masks[1])
    context_got = flipped(context, "mp", far)
    last_got[3], last_got[4] = [flipped(far_got[piece], "mp", close) for piece in (3, 4)]
    parts = 4
    held = [kind[piece] for piece in range(len(own)) for kind in (own, far_got, close_got, last_got)]
    context_got, q_got, q_cells, held = joined(context_got, q_got, q_cells, held)
    q_cells = stacked(q_cells, q_got)
    for mask in masks[2:-1]:
        q_got, q_cells = joined(flipped(q_cells, "seq", mask), q_cells)
        q_cells = stacked(q_cells, q_got)
    q_got = flipped(q_cells, "seq", masks[-1])
    context_cells = stacked(context, context_got)
    contexts = (context_cells, flipped(context_cells, "mp", close))

    vmem = lambda a, *lead: pltpu.VMEM((*lead, *a.shape), a.dtype)
    anywhere = pl.BlockSpec(memory_space=pl.ANY)
    hidden_shape = shape((rows, hidden), BF16)
    (
        layer_output, d_first, d_rest, d_w_down, d_context, d_context_turned, da_own, da_turned,
    ) = call(
        functools.partial(middle_kernel, parts),
        [
            low_shape, wide_shape, shape((features + columns + 16, features), BF16), shape(w_down.shape, BF16),
            heads_low, turned_shape, heads_low, turned_shape,
        ],
        tokens, *contexts, vectors, d_out, attended, *held,
        grid=(1,),
        in_specs=[None] * 6 + [anywhere] * len(held),
        flops=8 * rows * parts * w_up.size,
        scratch=[
            vmem(low_shape), vmem(hidden_shape), vmem(low_shape), vmem(hidden_shape), vmem(low_shape),
            pltpu.VMEM((rows, features), F32), pltpu.VMEM((rows, 1), F32), pltpu.VMEM((rows, features), F32),
            pltpu.VMEM((parts, rows, hidden), F32), pltpu.VMEM((parts, columns + 16, features), BF16), vmem(w_up, parts), vmem(w_down, parts),
            pltpu.SemaphoreType.DMA((5, parts)),
        ],
    )
    q_got, da_turned, d_w_down = joined(q_got, da_turned, d_w_down)
    da_got = flipped(da_turned, "seq", masks[0])
    down_kept, down_got = halves_sent(d_w_down, "seq", masks[-1])
    context_rims = rims_of(d_context_turned)
    da_got, da_own, d_rest, down_got, context_rims = joined(da_got, da_own, d_rest, down_got, context_rims)
    rest_kept, rest_got = halves_sent(d_rest, "seq", masks[-1])
    da_cells = stacked(da_turned, da_got)
    [dq, d_w_q, d_b_q] = call(
        query_back_kernel, [row_shape, shape((columns, features), BF16), shape((16, features), F32)],
        *scalars, slopes, *keys, *values, da_own, q_raw, tokens,
        grid=(steps,), scalars=4,
        in_specs=[tile_spec, *placed, *v_placed, None, None, None],
        flops=3 * pair_flops, scratch=[sums],
    )
    for mask in masks[1:-1]:
        da_got = flipped(da_cells, "seq", mask)
        da_got, dq, k_own, da_cells, rest_got = joined(da_got, dq, k_own, da_cells, rest_got)
        da_cells = stacked(da_cells, da_got)
    da_got = flipped(da_cells, "seq", masks[-1])
    alike = [[i for i in range(blocks) if i & masks[-1] == bit] for bit in (0, masks[-1])]
    down_half, rest_half = added(down_kept, down_got), added(rest_kept, rest_got)
    early = lax.psum((down_half, rest_half), "seq", axis_index_groups=alike)
    k_own = after(k_own, da_cells, down_half, rest_half)
    queries = (q_cells, q_got)
    weights_back, slopes_back = call(
        weights_kernel, [tiles, tiles], *scalars, k_own, *queries,
        grid=(steps,), scalars=4,
        in_specs=[None, *placed],
        out_specs=[tile_spec, tile_spec],
        flops=8 * pair_flops, scratch=[pltpu.VMEM((rows, 1), jnp.int32)],
    )
    context_rims = after(context_rims, weights_back)
    context_rim = jnp.concatenate([context_rims[0], d_context_turned, context_rims[1]], axis=1)
    dv_conv, d_taps_wide = call(
        conv_back_kernel, [heads_wide, shape((heads, BAND), F32)],
        scalars[1], scalars[3], mirrored, v_rim, d_context, context_rim,
        grid=(1,), scalars=2,
        flops=2 * rows * BAND * columns,
    )
    d_attended = (da_cells, da_got)
    dk, dv, late = call(
        key_back_kernel, [row_shape, row_shape, shape((3 * columns + 64, features), BF16)],
        *scalars, weights_back, slopes_back, *queries, *d_attended, v_own, k_raw, dv_conv, d_taps_wide, d_b_q, d_w_q, tokens,
        grid=(steps,), scalars=4,
        in_specs=[tile_spec, tile_spec, *placed, *placed] + [None] * 7,
        flops=4 * pair_flops, scratch=[sums, sums],
    )
    late = Chain(late, "seq")
    d_tokens_part = sum(
        jnp.dot(part, w_turned[i], preferred_element_type=F32) for i, part in enumerate((dq, dk, dv))
    )
    token = Chain(d_tokens_part.astype(BF16), "mp")
    while late.left > 3:
        chains = [chain for chain in (late, token) if chain.left]
        for chain in chains:
            chain.start()
        if late.left == 4:
            [early] = round_end(chains, early)
        else:
            round_end(chains)
    early_got = [flipped(array, "seq", masks[-1]) for array in early]
    while late.left:
        chains = [chain for chain in (late, token) if chain.left]
        for chain in chains:
            chain.start()
        if late.left == 2:
            early_got, early = round_end(chains, early_got, early)
        elif late.left == 1:
            break
        else:
            round_end(chains)
    d_tokens = (d_first + token.cells.astype(F32)).astype(BF16)
    upper = ((index & masks[-1]) != 0).astype(jnp.int32)[None]
    d_w_out, vectors, d_w_up, d_w_down = call(
        results_kernel,
        [shape(w_out.shape, F32), shape((16, features), F32), shape(w_up.shape, F32), shape(w_down.shape, F32)],
        upper, *early, *early_got,
        grid=(1,), scalars=1,
    )
    d_w_qkv, d_b_qv, d_taps = call(
        late_results_kernel,
        [shape((3, columns, features), F32), shape((2, columns), F32), shape((heads, kernel), F32)],
        upper, late.cells, late.got,
        grid=(1,), scalars=1,
    )
    d_ln2_gain, d_ln2_bias, d_b_down, d_ln1_gain, d_ln1_bias, d_b_out, d_b_up = [vectors[i] for i in range(7)]
    return (
        layer_output, d_tokens, jnp.swapaxes(d_w_qkv, 1, 2), d_b_qv, d_taps, d_w_out, d_b_out, d_ln1_gain,
        d_ln1_bias, d_w_up, d_b_up, d_w_down, d_b_down, d_ln2_gain, d_ln2_bias,
    )


def solution(mesh):
    placed = (
        P("seq", None), P(), P(None, None, "mp"), P(None, "mp"), P("mp", None), P("mp", None), P(), P(), P(),
        P(None, "mp"), P("mp"), P("mp", None), P(), P(), P(), P("seq", None),
    )
    given = (
        P("seq", None), P("seq", None), P(None, None, "mp"), P(None, "mp"), P("mp", None), P("mp", None), P(),
        P(), P(), P(None, "mp"), P("mp"), P("mp", None), P(), P(), P(),
    )
    return jax.shard_map(per_device, mesh=mesh, in_specs=placed, out_specs=given, check_vma=False)
```

```python
import functools
import math

import jax
import jax.numpy as jnp
from jax import lax
from jax.experimental import pallas as pl
from jax.experimental.pallas import tpu as pltpu
from jax.sharding import PartitionSpec as P

SHRINK = 0.95
NORM_EPS = 1e-06
LAYER_EPS = 1e-05
F32 = jnp.float32
BF16 = jnp.bfloat16
KEYS = 256
CHUNK = 256
EDGE = 128
BAND = 3 * EDGE
MIDDLE = 256
WINDOW = 9216
VMEM_BYTES = 56 * 1024 * 1024
SQUARE_OF_V = (
    0.9999936361319989,
    -1.2731008162270503,
    0.4040306859655804,
    -0.20598641392473288,
    0.11615118744625774,
    -0.05772567810293111,
    0.02001158958170149,
    -0.00337422878652264,
)
SQUARE = tuple(factor * (0.5 * SHRINK) ** (0.5 * power) for power, factor in enumerate(SQUARE_OF_V))
SLOPE = 8.0 / math.pi
TAIL_AT = 0.2316419
TAIL = (0.319381530, -0.356563782, 1.781477937, -1.821255978, 1.330274429)


def dot(left, right, left_dim=1, right_dim=0):
    return lax.dot_general(
        left, right, (((left_dim,), (right_dim,)), ((), ())), preferred_element_type=F32
    )


def flipped(cells, axis, mask):
    return lax.ppermute(cells, axis, [(i, i ^ mask) for i in range(lax.axis_size(axis))])


def masks_of(axis):
    return [1 << bit for bit in range(lax.axis_size(axis).bit_length() - 2, -1, -1)]


def block_places(axis, masks):
    apart = jnp.arange(lax.axis_size(axis), dtype=jnp.int32) ^ lax.axis_index(axis).astype(jnp.int32)
    place = jnp.zeros_like(apart)
    for bit, mask in enumerate(masks):
        place = place | (jnp.where((apart & mask) != 0, 1, 0) << bit)
    return place


def halves_sent(cells, axis, mask):
    half = cells.shape[0] // 2
    upper = (lax.axis_index(axis) & mask) != 0
    sent = lax.dynamic_slice_in_dim(cells, jnp.where(upper, 0, half), half)
    kept = lax.dynamic_slice_in_dim(cells, jnp.where(upper, half, 0), half)
    return kept, flipped(sent, axis, mask)


def added(kept, got):
    return (kept.astype(F32) + got.astype(F32)).astype(BF16)


def united(cells, got, axis, mask):
    upper = (lax.axis_index(axis) & mask) != 0
    return jnp.concatenate([jnp.where(upper, got, cells), jnp.where(upper, cells, got)], axis=0)


class Chain:
    def __init__(self, cells, axis, masks=None):
        masks = masks or masks_of(axis)[::-1]
        self.cells, self.axis = cells, axis
        self.steps = [("halve", m) for m in masks[:-1]] + [("whole", masks[-1])]
        self.steps += [("gather", m) for m in masks[-2::-1]]
        self.at, self.got = 0, None

    def start(self):
        kind, mask = self.steps[self.at]
        if kind == "halve":
            self.cells, self.got = halves_sent(self.cells, self.axis, mask)
        else:
            self.got = flipped(self.cells, self.axis, mask)

    def finish(self):
        kind, mask = self.steps[self.at]
        self.at += 1
        if kind == "gather":
            self.cells = united(self.cells, self.got, self.axis, mask)
        else:
            self.cells = added(self.cells, self.got)

    @property
    def left(self):
        return len(self.steps) - self.at


def round_end(chains, *arrays):
    gots = [chain.got for chain in chains]
    *arrays, gots, cells = joined(*arrays, gots, [chain.cells for chain in chains])
    for chain, got, kept in zip(chains, gots, cells):
        chain.got, chain.cells = got, kept
        chain.finish()
    return arrays


def after(arrays, *earlier):
    return lax.optimization_barrier((arrays, *earlier))[0]


def joined(*arrays):
    return lax.optimization_barrier(arrays)


def stacked(*cells):
    return jnp.concatenate([part if part.ndim == 3 else part[None] for part in cells], axis=0)


def item_index(positions, ends):
    inside = (positions >= 0) & (positions < ends[-1])
    counted = jnp.sum((positions[:, None] >= ends[None, :]).astype(jnp.int32), axis=1)
    return jnp.where(inside, counted, -1)


def call(kernel, out_shape, *args, grid=(), in_specs=None, out_specs=None, scalars=0, flops=0, scratch=()):
    whole = lambda a: pl.BlockSpec(a.shape, lambda *_, n=len(a.shape): (0,) * n)
    ins = [whole(a) if s is None else s for a, s in zip(args[scalars:], in_specs or [None] * 99)]
    outs = [whole(a) if s is None else s for a, s in zip(out_shape, out_specs or [None] * 99)]
    moved = sum(a.size * a.dtype.itemsize for a in (*args, *out_shape))
    return pl.pallas_call(
        kernel,
        out_shape=out_shape,
        grid_spec=pltpu.PrefetchScalarGridSpec(
            num_scalar_prefetch=scalars,
            grid=grid,
            in_specs=ins,
            out_specs=outs,
            scratch_shapes=list(scratch),
        ),
        compiler_params=pltpu.CompilerParams(vmem_limit_bytes=VMEM_BYTES),
        cost_estimate=pl.CostEstimate(flops=1, bytes_accessed=1, transcendentals=0),
    )(*args)


def project_kernel(unit, raw, own, turned, tokens_ref, w_ref, bias_ref, *out_refs):
    out_refs = list(out_refs)
    raw_ref = out_refs.pop(0) if raw else None
    own_ref = out_refs.pop(0) if own else None
    turned_ref = out_refs.pop(0) if turned else None
    product = dot(w_ref[0], tokens_ref[...], 1, 1) + bias_ref[...]
    size = HEAD
    for head in range(product.shape[0] // size):
        part = product[head * size : (head + 1) * size, :]
        if raw:
            raw_ref[head] = part.T
        if unit:
            part = part * lax.rsqrt(jnp.sum(part * part, axis=0, keepdims=True) + NORM_EPS)
        if turned:
            turned_ref[head * size : (head + 1) * size, :] = part.astype(BF16)
        if own:
            own_ref[head] = part.T.astype(BF16)


def square_of(half):
    root = half * lax.rsqrt(half)
    square = jnp.full_like(root, SQUARE[-1])
    for factor in SQUARE[-2::-1]:
        square = square * root + factor
    return square


def item_of(positions, ends_ref):
    count = jnp.zeros_like(positions)
    for item in range(ends_ref.shape[0]):
        count = count + (positions >= ends_ref[item]).astype(jnp.int32)
    return jnp.where(positions < 0, -1, count)


def own_items(place_ref, ends_ref, rows):
    first = place_ref[place_ref.shape[0] - 1] * rows
    return item_of(first + lax.broadcasted_iota(jnp.int32, (rows, 1), 0), ends_ref)


def rim_items(place_ref, ends_ref, rows):
    first = place_ref[place_ref.shape[0] - 1] * rows - EDGE
    return item_of(first + lax.broadcasted_iota(jnp.int32, (1, rows + 2 * EDGE), 1), ends_ref)


def tile_of(span_ref):
    return span_ref[0] + jnp.minimum(pl.program_id(0), span_ref[1] - 1)


def held_at(far, near_ref, far_ref, group):
    return jnp.where(far, far_ref[0, group, :], near_ref[0, group, :])


def is_far(span_ref, place_ref, rows):
    return place_ref[tile_of(span_ref) // (rows // KEYS)] >= (place_ref.shape[0] - 1) // 2


def by_chunks(span_ref, rows, work):
    tile = span_ref[0] + pl.program_id(0)
    here = pl.program_id(0) < span_ref[1]
    meets = [
        (tile >= span_ref[2 + 2 * chunk]) & (tile < span_ref[3 + 2 * chunk]) for chunk in range(rows // CHUNK)
    ]
    every = functools.reduce(lambda x, y: x & y, meets)

    @pl.when(here & every)
    def _():
        work(slice(0, rows))

    for chunk, meet in enumerate(meets):

        @pl.when(here & meet & jnp.logical_not(every))
        def _(chunk=chunk):
            work(slice(chunk * CHUNK, (chunk + 1) * CHUNK))


def weights_kernel(
    span_ref, place_ref, v_place_ref, ends_ref, own_ref, near_ref, far_ref, weight_ref, slope_ref, mine_ref
):
    heads, rows, size = own_ref.shape
    far = is_far(span_ref, place_ref, rows)

    @pl.when(pl.program_id(0) == 0)
    def _():
        mine_ref[...] = own_items(place_ref, ends_ref, rows)

    def work(part):
        positions = tile_of(span_ref) * KEYS + lax.broadcasted_iota(jnp.int32, (1, KEYS), 1)
        same = mine_ref[part, :] == item_of(positions, ends_ref)
        for head in range(heads):
            scores = dot(own_ref[head, part, :], held_at(far, near_ref, far_ref, slice(head * size, (head + 1) * size)))
            half = 1.0 / SHRINK - scores
            square = square_of(half)
            fourth = square * square
            weight = jnp.where(same, fourth * fourth, 0.0)
            weight_ref[0, head, part, :] = weight.astype(BF16)
            slope = weight * lax.rsqrt(square * (half * (1.0 / SHRINK + scores)))
            slope_ref[0, head, part, :] = slope.astype(BF16)

    by_chunks(span_ref, rows, work)


def unit_back(grad, raw):
    scale = lax.rsqrt(jnp.sum(raw * raw, axis=-1, keepdims=True) + NORM_EPS)
    unit = raw * scale
    return scale * (grad - unit * jnp.sum(unit * grad, axis=-1, keepdims=True))


def split_low(wide):
    high = wide.astype(BF16)
    return high, (wide - high.astype(F32)).astype(BF16)


def band_of(taps_row):
    return pltpu.roll(jnp.broadcast_to(taps_row, (EDGE, BAND)), 0, 1, stride=1, stride_axis=0)


def around_of(mine, rim, start):
    return mine[start : start + EDGE, :] == rim[:, start : start + BAND]


def band_sums(taps_ref, head, mine, rim, values):
    band = band_of(taps_ref[head : head + 1, :])
    out = []
    for start in range(0, mine.shape[0], EDGE):
        high, low = split_low(jnp.where(around_of(mine, rim, start), band, 0.0))
        near = values[:, start : start + BAND]
        out.append(dot(high, near, 1, 1) + dot(low, near, 1, 1))
    return jnp.concatenate(out, axis=0)


def rim_values(v_place_ref, sides, own_ref, group):
    index, blocks, rows = v_place_ref[v_place_ref.shape[0] - 1], v_place_ref.shape[0] - 1, own_ref.shape[1]
    ends = []
    for (near_ref, far_ref), beside, part in zip(sides, (-1, 1), (slice(rows - EDGE, rows), slice(0, EDGE))):
        far = v_place_ref[jnp.clip(index + beside, 0, blocks - 1)] >= blocks // 2
        ends.append(jnp.where(far, far_ref[0, group, part], near_ref[0, group, part]))
    return jnp.concatenate([ends[0], own_ref[group, :], ends[1]], axis=1)


def attend_kernel(
    span_ref, place_ref, v_place_ref, ends_ref, weight_ref, v_near_ref, v_far_ref, taps_ref, own_ref,
    before_near_ref, before_far_ref, after_near_ref, after_far_ref, context_ref, raw_ref, v_rim_ref, sum_ref, conv_ref,
):
    heads, rows, size = raw_ref.shape
    far = is_far(span_ref, v_place_ref, rows)

    @pl.when(pl.program_id(0) == 0)
    def _():
        sides = ((before_near_ref, before_far_ref), (after_near_ref, after_far_ref))
        mine, rim = own_items(place_ref, ends_ref, rows), rim_items(place_ref, ends_ref, rows)
        for head in range(heads):
            group = slice(head * size, (head + 1) * size)
            values = rim_values(v_place_ref, sides, own_ref, group)
            v_rim_ref[group, :] = values
            conv_ref[head] = band_sums(taps_ref, head, mine, rim, values)
        sum_ref[...] = jnp.zeros_like(sum_ref)

    def work(part):
        for head in range(heads):
            values = held_at(far, v_near_ref, v_far_ref, slice(head * size, (head + 1) * size))
            sum_ref[head, part, :] += dot(weight_ref[0, head, part, :], values, 1, 1)

    by_chunks(span_ref, rows, work)

    @pl.when(pl.program_id(0) == pl.num_programs(0) - 1)
    def _():
        context = []
        for head in range(heads):
            raw = sum_ref[head]
            raw_ref[head] = raw
            unit = raw * lax.rsqrt(jnp.sum(raw * raw, axis=-1, keepdims=True) + NORM_EPS)
            context.append(unit + conv_ref[head])
        context_ref[...] = jnp.concatenate(context, axis=1).astype(BF16)


def finished(grad, tokens_ref, low_ref, weight_ref, start):
    turned = grad.T.astype(BF16)
    low_ref[...] = grad.astype(BF16)
    weight_ref[start : start + turned.shape[0], :] = dot(turned, tokens_ref[...]).astype(BF16)
    return row_sum(grad.astype(BF16).astype(F32))


def query_back_kernel(
    span_ref, place_ref, v_place_ref, ends_ref, slope_ref, k_near_ref, k_far_ref, v_near_ref, v_far_ref, da_ref, raw_ref,
    tokens_ref, dq_ref, d_w_ref, d_b_ref, sum_ref,
):
    heads, rows, size = raw_ref.shape
    far = is_far(span_ref, place_ref, rows)
    v_far = is_far(span_ref, v_place_ref, rows)

    @pl.when(pl.program_id(0) == 0)
    def _():
        sum_ref[...] = jnp.zeros_like(sum_ref)

    def work(part):
        for head in range(heads):
            group = slice(head * size, (head + 1) * size)
            slope = slope_ref[0, head, part, :].astype(F32)
            d_weights = dot(da_ref[head, part, :], held_at(v_far, v_near_ref, v_far_ref, group))
            d_scores = (d_weights * slope).astype(BF16)
            sum_ref[head, part, :] += dot(d_scores, held_at(far, k_near_ref, k_far_ref, group), 1, 1)

    by_chunks(span_ref, rows, work)

    @pl.when(pl.program_id(0) == pl.num_programs(0) - 1)
    def _():
        grads = [unit_back(sum_ref[head] * SLOPE, raw_ref[head]) for head in range(heads)]
        bias = finished(jnp.concatenate(grads, axis=1), tokens_ref, dq_ref, d_w_ref, 0)
        d_b_ref[...] = jnp.zeros_like(d_b_ref)
        d_b_ref[0:1, : bias.shape[1]] = bias


def key_back_kernel(
    span_ref, place_ref, v_place_ref, ends_ref, weight_ref, slope_ref, q_near_ref, q_far_ref, da_near_ref, da_far_ref, v_ref,
    raw_ref, dv_conv_ref, d_taps_ref, d_b_q_ref, d_w_q_ref, tokens_ref, dk_ref, dv_ref, late_ref, sum_ref, value_ref,
):
    heads, rows, size = raw_ref.shape
    columns = heads * size
    far = is_far(span_ref, place_ref, rows)

    @pl.when(pl.program_id(0) == 0)
    def _():
        sum_ref[...] = jnp.zeros_like(sum_ref)
        value_ref[...] = dv_conv_ref[...]

    def work(part):
        for head in range(heads):
            group = slice(head * size, (head + 1) * size)
            d_attn = held_at(far, da_near_ref, da_far_ref, group)
            slope = slope_ref[0, head, part, :].astype(F32)
            d_scores = (dot(v_ref[head, part, :], d_attn) * slope).astype(BF16)
            sum_ref[head, part, :] += dot(d_scores, held_at(far, q_near_ref, q_far_ref, group), 1, 1)
            value_ref[head, part, :] += dot(weight_ref[0, head, part, :], d_attn, 1, 1)

    by_chunks(span_ref, rows, work)

    @pl.when(pl.program_id(0) == pl.num_programs(0) - 1)
    def _():
        more = 3 * columns
        late_ref[more:, :] = jnp.zeros((late_ref.shape[0] - more, late_ref.shape[1]), BF16)
        late_ref[:columns, :] = d_w_q_ref[...]
        grads = [unit_back(sum_ref[head] * SLOPE, raw_ref[head]) for head in range(heads)]
        finished(jnp.concatenate(grads, axis=1), tokens_ref, dk_ref, late_ref, columns)
        grads = jnp.concatenate([value_ref[head] for head in range(heads)], axis=1)
        bias = finished(grads, tokens_ref, dv_ref, late_ref, 2 * columns)
        late_ref[more : more + 2, :columns] = jnp.concatenate(
            [d_b_q_ref[0:1, :columns], bias], axis=0
        ).astype(BF16)
        late_ref[more + 16 : more + 16 + heads, : d_taps_ref.shape[1]] = d_taps_ref[...].astype(BF16)


def conv_back_kernel(place_ref, ends_ref, taps_ref, values_ref, d_context_ref, turned_ref, dv_ref, d_taps_ref):
    heads, rows, size = d_context_ref.shape
    mine, rim = own_items(place_ref, ends_ref, rows), rim_items(place_ref, ends_ref, rows)
    for head in range(heads):
        group = slice(head * size, (head + 1) * size)
        dv_ref[head] = band_sums(taps_ref, head, mine, rim, turned_ref[group, :])
        values = values_ref[group, :]
        lined = jnp.zeros((8, BAND), F32)
        for start in range(0, rows, EDGE):
            pairs = dot(d_context_ref[head, start : start + EDGE, :], values[:, start : start + BAND])
            pairs = jnp.where(around_of(mine, rim, start), pairs, 0.0)
            for row in range(0, EDGE, 8):
                part = pairs[row : row + 8, :]
                lined = lined + (pltpu.roll(part, BAND - row, 1) if row else part)
        total = lined[0:1, :]
        for row in range(1, 8):
            total = total + pltpu.roll(lined[row : row + 1, :], BAND - row, 1)
        d_taps_ref[head : head + 1, :] = total


def normal_of(u):
    density = jnp.exp(u * u * -0.5) * (1.0 / math.sqrt(2.0 * math.pi))
    ratio = 1.0 / (1.0 + TAIL_AT * jnp.abs(u))
    tail = jnp.full_like(ratio, TAIL[-1])
    for factor in TAIL[-2::-1]:
        tail = tail * ratio + factor
    tail = tail * (ratio * density)
    return jnp.where(u >= 0.0, 1.0 - tail, tail), density


def normed_of(hidden):
    center = hidden - jnp.mean(hidden, axis=-1, keepdims=True)
    scale = lax.rsqrt(jnp.mean(center * center, axis=-1, keepdims=True) + LAYER_EPS)
    return center * scale, scale


def normed_back(grad, normed, scale, gain):
    d_normed = grad * gain
    centered = d_normed - jnp.mean(d_normed, axis=-1, keepdims=True)
    return scale * (centered - normed * jnp.mean(d_normed * normed, axis=-1, keepdims=True))


def row_sum(array):
    return jnp.sum(array, axis=0, keepdims=True)


def middle_kernel(parts, *refs):
    tokens_ref, near_ref, far_ref, vectors_ref, d_out_ref, raw_ref = refs[:6]
    contexts = [half.at[i] for half in (near_ref, far_ref) for i in range(parts // 2)]
    (
        result_ref, d_first_ref, d_rest_ref, d_w_down_ref,
        d_context_ref, turned_ref, da_ref, da_turned_ref,
        y_low_ref, act_ref, d_second_low_ref, d_inner_ref, d_first_low_ref,
        normed_ref, scale_ref, mixed_ref, factor_ref, out_ref, up_ref, down_ref, sem_ref,
    ) = refs[6 + 5 * parts :]
    heads, rows, size = raw_ref.shape
    columns = heads * size
    b_out, gain_one, bias_one, b_down, gain_two, bias_two = [vectors_ref[i : i + 1, :] for i in range(6)]
    chunks = [slice(start, start + MIDDLE) for start in range(0, rows, MIDDLE)]
    up_cut, down_cut = up_ref.shape[1] // 3, 2 * down_ref.shape[1] // 3
    targets = [
        (0, 0, up_ref, 0, up_cut),
        (1, 0, up_ref, up_cut, up_ref.shape[1] - up_cut),
        (2, 0, down_ref, 0, down_cut),
        (3, 0, down_ref, down_cut, down_ref.shape[1] - down_cut),
        (4, 0, out_ref, 0, out_ref.shape[1]),
    ]
    copies = [
        [
            pltpu.make_async_copy(
                refs[6 + piece * parts + part].at[first : first + count, :],
                to.at[part, start : start + count, :],
                sem_ref.at[i, part],
            )
            for part in range(parts)
        ]
        for i, (piece, first, to, start, count) in enumerate(targets)
    ]
    copies = copies[-1:] + copies[:-1]
    for of in copies:
        for part in range(parts):
            of[part].start()

    for part in range(parts):
        copies[0][part].wait()
    for chunk in chunks:
        hidden = tokens_ref[chunk, :].astype(F32) + b_out
        for part in range(parts):
            hidden = hidden + dot(contexts[part][chunk, :], out_ref[part, :columns, :])
        normed, scale = normed_of(hidden)
        normed_ref[chunk, :] = normed
        scale_ref[chunk, :] = scale
        first = normed * gain_one + bias_one
        y_low_ref[chunk, :] = first.astype(BF16)
        mixed_ref[chunk, :] = first + b_down

    for part in range(parts):
        for of in copies[1:]:
            of[part].wait()
        b_up = row_sum(out_ref[part, columns : columns + 16, :].astype(F32))
        for chunk in chunks:
            inner = dot(y_low_ref[chunk, :], up_ref[part]) + b_up
            share, density = normal_of(inner)
            act = (inner * share).astype(BF16)
            factor_ref[part, chunk, :] = share + inner * density
            if part == 0:
                act_ref[chunk, :] = act
            mixed_ref[chunk, :] += dot(act, down_ref[part])

    sums = [0.0] * 7
    for chunk in chunks:
        normed, scale = normed_of(mixed_ref[chunk, :])
        result_ref[chunk, :] = (normed * gain_two + bias_two).astype(BF16)
        grad = d_out_ref[chunk, :].astype(F32)
        d_second = normed_back(grad, normed, scale, gain_two)
        d_second_low_ref[chunk, :] = d_second.astype(BF16)
        mixed_ref[chunk, :] = d_second
        for i, array in enumerate((grad * normed, grad, d_second)):
            sums[i] = sums[i] + row_sum(array)

    d_w_down_ref[...] = dot(act_ref[...], d_second_low_ref[...], 0, 0).astype(BF16)
    for part in range(parts):
        for chunk in chunks:
            d_act = dot(d_second_low_ref[chunk, :], down_ref[part], 1, 1)
            d_inner = (d_act * factor_ref[part, chunk, :]).astype(BF16)
            if part == 0:
                d_inner_ref[chunk, :] = d_inner
                sums[6] = sums[6] + row_sum(d_inner.astype(F32))
            mixed_ref[chunk, :] += dot(d_inner, up_ref[part], 1, 1)
        if part == 0:
            d_rest_ref[: y_low_ref.shape[1], :] = dot(y_low_ref[...], d_inner_ref[...], 0, 0).astype(BF16)

    for chunk in chunks:
        grad = mixed_ref[chunk, :]
        normed = normed_ref[chunk, :]
        d_first = normed_back(grad, normed, scale_ref[chunk, :], gain_one)
        d_first_ref[chunk, :] = d_first
        d_first_low = d_first.astype(BF16)
        d_first_low_ref[chunk, :] = d_first_low
        for i, array in enumerate((grad * normed, grad, d_first)):
            sums[3 + i] = sums[3 + i] + row_sum(array)
        d_context = dot(d_first_low, out_ref[0, :columns, :], 1, 1).astype(BF16).astype(F32)
        turned_ref[:, chunk] = d_context.T.astype(BF16)
        grads = []
        for head in range(heads):
            grad = d_context[:, head * size : (head + 1) * size]
            d_context_ref[head, chunk, :] = grad.astype(BF16)
            grad = unit_back(grad, raw_ref[head, chunk, :])
            da_ref[head, chunk, :] = grad.astype(BF16)
            grads.append(grad)
        da_turned_ref[:, chunk] = jnp.concatenate(grads, axis=1).T.astype(BF16)
    at_out = y_low_ref.shape[1]
    d_rest_ref[at_out : at_out + columns, :] = dot(contexts[0][...], d_first_low_ref[...], 0, 0).astype(BF16)
    sums.append(jnp.zeros((57, sums[0].shape[1]), F32))
    d_rest_ref[at_out + columns :, :] = jnp.concatenate(sums, axis=0).astype(BF16)


def whole_of(upper_ref, own, got):
    upper = upper_ref[0] != 0
    return jnp.concatenate([jnp.where(upper, got, own), jnp.where(upper, own, got)], axis=0).astype(F32)


def late_results_kernel(upper_ref, late_ref, got_ref, d_w_ref, d_b_ref, d_taps_ref):
    late = whole_of(upper_ref, late_ref[...], got_ref[...])
    columns = d_w_ref.shape[1]
    for i in range(3):
        d_w_ref[i] = late[i * columns : (i + 1) * columns, :]
    more = 3 * columns
    d_b_ref[...] = late[more : more + 2, :columns]
    heads, kernel = d_taps_ref.shape
    start = EDGE - (kernel - 1) // 2
    d_taps_ref[...] = late[more + 16 : more + 16 + heads, start : start + kernel]


def results_kernel(
    upper_ref, early_ref, got_ref, d_out_ref, vectors_ref, d_up_ref, d_down_ref
):
    columns = d_out_ref.shape[0]
    cut = d_down_ref.shape[0] // 2
    d_down_ref[...] = whole_of(upper_ref, early_ref[:cut, :], got_ref[:cut, :])
    rest = whole_of(upper_ref, early_ref[cut:, :], got_ref[cut:, :])
    at_out = d_up_ref.shape[0]
    d_up_ref[...] = rest[:at_out, :]
    d_out_ref[...] = rest[at_out : at_out + columns, :]
    vectors_ref[...] = rest[at_out + columns : at_out + columns + 16, :]


HEAD = 64


def per_device(
    tokens, item_lengths, w_qkv, b_qv, taps, w_out, b_out, ln1_gain, ln1_bias, w_up, b_up, w_down, b_down,
    ln2_gain, ln2_bias, d_out,
):
    rows, features = tokens.shape
    heads, kernel = taps.shape
    radius = (kernel - 1) // 2
    columns = w_qkv.shape[2]
    size = columns // heads
    hidden = w_up.shape[1]
    blocks = lax.axis_size("seq")
    total = blocks * rows
    index = lax.axis_index("seq").astype(jnp.int32)
    first_row = index * rows
    shape = jax.ShapeDtypeStruct
    heads_wide, heads_low = shape((heads, rows, size), F32), shape((heads, rows, size), BF16)
    turned_shape, row_shape = shape((columns, rows), BF16), shape((rows, columns), BF16)
    wide_shape, low_shape = shape((rows, features), F32), shape((rows, features), BF16)

    w_turned = jnp.swapaxes(w_qkv, 1, 2)
    biases = jnp.stack([b_qv[0], jnp.zeros_like(b_qv[0]), b_qv[1]])[:, :, None]

    def project(x, which, unit, outs, *flags):
        return call(
            functools.partial(project_kernel, unit, *flags), outs, x, w_turned, biases[which],
            grid=(1,),
            in_specs=[None, pl.BlockSpec((1, columns, features), lambda *_: (which, 0, 0)), None],
            flops=2 * rows * columns * features,
        )

    masks = masks_of("seq")
    v_masks = masks[-1:] + masks[:-1]
    ahead = [(i, i + 1) for i in range(blocks - 1)]
    behind = [(i + 1, i) for i in range(blocks - 1)]

    reach = EDGE - radius

    def rims_of(turned):
        ends = turned[:, rows - EDGE :], turned[:, :EDGE]
        return [lax.ppermute(end, "seq", pairs) for end, pairs in zip(ends, (ahead, behind))]

    reach = EDGE - radius

    steps = min(total, WINDOW) // KEYS
    per = rows // KEYS
    at_of = lambda i, span_ref: span_ref[0] + jnp.minimum(i, span_ref[1] - 1)
    tile_spec = pl.BlockSpec(
        (1, heads, rows, KEYS), lambda i, span_ref, *_: (jnp.minimum(i, span_ref[1] - 1), 0, 0, 0)
    )
    half = blocks // 2

    def halves_of(which):
        def spec(index_of):
            return pl.BlockSpec(
                (1, columns, KEYS),
                lambda i, *refs: (index_of(refs[which][at_of(i, refs[0]) // per]), 0, at_of(i, refs[0]) % per),
            )

        return [spec(lambda place: jnp.minimum(place, half - 1)), spec(lambda place: jnp.maximum(place - half, 0))]

    def side_of(beside):
        def spec(index_of):
            return pl.BlockSpec(
                (1, columns, rows),
                lambda i, *refs: (index_of(refs[2][jnp.clip(refs[2][blocks] + beside, 0, blocks - 1)]), 0, 0),
            )

        return [spec(lambda place: jnp.minimum(place, half - 1)), spec(lambda place: jnp.maximum(place - half, 0))]

    placed, v_placed = halves_of(1), halves_of(2)
    ordered = pl.BlockSpec((1, columns, KEYS), lambda i, *refs: (at_of(i, refs[0]) // per, 0, at_of(i, refs[0]) % per))
    tiles = shape((steps, heads, rows, KEYS), BF16)
    sums = pltpu.VMEM((heads, rows, size), F32)
    pair_flops = 2 * rows * (total // 2) * columns

    def tables(item_lengths):
        count = item_lengths.shape[0]
        upto = jnp.arange(count)[None, :] <= jnp.arange(count)[:, None]
        ends = jnp.sum(jnp.where(upto, item_lengths[None, :], 0), axis=1)
        starts = first_row + CHUNK * jnp.arange(rows // CHUNK, dtype=jnp.int32)[:, None]
        lows = jnp.max(jnp.where(ends[None, :] <= starts, ends[None, :], 0), axis=1)
        highs = jnp.min(jnp.where(ends[None, :] >= starts + CHUNK, ends[None, :], total), axis=1)
        bounds = jnp.stack([lows // KEYS, (highs + KEYS - 1) // KEYS], axis=1)
        span = jnp.concatenate(
            [jnp.stack([bounds[0, 0], bounds[-1, 1] - bounds[0, 0]]), bounds.reshape(-1)]
        ).astype(jnp.int32)
        place, v_place = [jnp.concatenate([block_places("seq", order), index[None]]) for order in (masks, v_masks)]
        return span, place, v_place, ends

    small = taps, [b_out, ln1_gain, ln1_bias, b_down, ln2_gain, ln2_bias]
    [k_turned] = project(tokens, 1, True, [turned_shape], False, False, True)
    k_got = flipped(k_turned, "seq", masks[0])
    far, close = masks_of("mp")
    b_high = lax.reduce_precision(b_up, 8, 7)
    b_mid = lax.reduce_precision(b_up - b_high, 8, 7)
    b_split = jnp.stack([b_high, b_mid, b_up - b_high - b_mid]).astype(BF16)
    w_out_more = jnp.concatenate([w_out, b_split, jnp.zeros((13, features), BF16)])
    up_cut, down_cut = w_up.shape[0] // 3, 2 * w_down.shape[0] // 3
    own = [w_up[:up_cut], w_up[up_cut:], w_down[:down_cut], w_down[down_cut:], w_out_more]
    far_got, last_got = [None] * 5, [None] * 5
    close_got = [flipped(after(array, k_turned), "mp", close) for array in own[:2]]
    k_got, late_tokens, late_lengths, own, close_got = joined(k_got, tokens, item_lengths, own, close_got)
    k_cells = stacked(k_turned, k_got)
    k_got = flipped(k_cells, "seq", masks[1])
    late_tokens, late_lengths, own = after((late_tokens, late_lengths, own), k_cells)
    v_own, v_turned = project(late_tokens, 2, False, [heads_low, turned_shape], False, True, True)
    v_got = flipped(v_turned, "seq", v_masks[0])
    far_got[0] = flipped(own[0], "mp", far)
    q_raw, q_own, q_turned = project(late_tokens, 0, True, [heads_wide, heads_low, turned_shape], True, True, True)
    scalars = tables(late_lengths)
    close_got += [flipped(array, "mp", close) for array in own[2:]]
    k_got, v_got, q_own, scalars, far_got[0], own, late_tokens, small, close_got = joined(
        k_got, v_got, q_own, scalars, far_got[0], own, late_tokens, small, close_got
    )
    k_cells = stacked(k_cells, k_got)
    v_cells = stacked(v_turned, v_got)
    for mask in masks[2:-1]:
        k_got, k_cells = joined(flipped(k_cells, "seq", mask), k_cells)
        k_cells = stacked(k_cells, k_got)
    for mask in v_masks[1:-2]:
        v_got, v_cells = joined(flipped(v_cells, "seq", mask), v_cells)
        v_cells = stacked(v_cells, v_got)
    k_got = flipped(k_cells, "seq", masks[-1])
    v_got = flipped(v_cells, "seq", v_masks[-2])
    own, far_got[0], late_tokens, small = after((own, far_got[0], late_tokens, small), k_cells)
    k_raw, k_own = project(late_tokens, 1, True, [heads_wide, heads_low], True, True, False)
    taps, vectors = small
    vectors = jnp.stack([*vectors, vectors[0], vectors[0]])
    banded = jnp.pad(taps, ((0, 0), (reach, BAND - reach - kernel)))
    mirrored = jnp.pad(taps[:, ::-1], ((0, 0), (reach, BAND - reach - kernel)))
    far_got[1] = flipped(own[1], "mp", far)
    last_got[0] = flipped(far_got[0], "mp", close)
    k_got, v_got, v_cells, far_got[1], last_got[0], own[2], q_own, k_own, k_raw, banded = joined(
        k_got, v_got, v_cells, far_got[1], last_got[0], own[2], q_own, k_own, k_raw, banded
    )
    v_cells = stacked(v_cells, v_got)
    v_got = flipped(v_cells, "seq", v_masks[-1])
    keys = (k_cells, k_got)
    weights, slopes = call(
        weights_kernel, [tiles, tiles], *scalars, q_own, *keys,
        grid=(steps,), scalars=4,
        in_specs=[None, *placed],
        out_specs=[tile_spec, tile_spec],
        flops=8 * pair_flops, scratch=[pltpu.VMEM((rows, 1), jnp.int32)],
    )
    far_got[2], last_got[1] = flipped(own[2], "mp", far), flipped(far_got[1], "mp", close)
    v_got, weights, q_turned, far_got[2], last_got[1], own[3] = joined(
        v_got, weights, q_turned, far_got[2], last_got[1], own[3]
    )
    values = (v_cells, v_got)
    far_got[3], far_got[4] = [flipped(own[piece], "mp", far) for piece in (3, 4)]
    last_got[2] = flipped(far_got[2], "mp", close)
    q_got = flipped(q_turned, "seq", masks[0])
    context, attended, v_rim = call(
        attend_kernel, [row_shape, heads_wide, shape((columns, rows + 2 * EDGE), BF16)],
        *scalars, weights, *values, banded, v_turned, *values, *values,
        grid=(steps,), scalars=4,
        in_specs=[tile_spec, *v_placed, None, None, *side_of(-1), *side_of(1)],
        flops=pair_flops, scratch=[sums, sums],
    )
    q_got, context, far_got[3], far_got[4], last_got[2] = joined(
        q_got, context, far_got[3], far_got[4], last_got[2]
    )
    q_cells = stacked(q_turned, q_got)
    q_got = flipped(q_cells, "seq", masks[1])
    context_got = flipped(context, "mp", far)
    last_got[3], last_got[4] = [flipped(far_got[piece], "mp", close) for piece in (3, 4)]
    parts = 4
    held = [kind[piece] for piece in range(len(own)) for kind in (own, far_got, close_got, last_got)]
    context_got, q_got, q_cells, held = joined(context_got, q_got, q_cells, held)
    q_cells = stacked(q_cells, q_got)
    for mask in masks[2:-1]:
        q_got, q_cells = joined(flipped(q_cells, "seq", mask), q_cells)
        q_cells = stacked(q_cells, q_got)
    q_got = flipped(q_cells, "seq", masks[-1])
    context_cells = stacked(context, context_got)
    contexts = (context_cells, flipped(context_cells, "mp", close))

    vmem = lambda a, *lead: pltpu.VMEM((*lead, *a.shape), a.dtype)
    anywhere = pl.BlockSpec(memory_space=pl.ANY)
    hidden_shape = shape((rows, hidden), BF16)
    (
        layer_output, d_first, d_rest, d_w_down, d_context, d_context_turned, da_own, da_turned,
    ) = call(
        functools.partial(middle_kernel, parts),
        [
            low_shape, wide_shape, shape((features + columns + 64, features), BF16), shape(w_down.shape, BF16),
            heads_low, turned_shape, heads_low, turned_shape,
        ],
        tokens, *contexts, vectors, d_out, attended, *held,
        grid=(1,),
        in_specs=[None] * 6 + [anywhere] * len(held),
        flops=8 * rows * parts * w_up.size,
        scratch=[
            vmem(low_shape), vmem(hidden_shape), vmem(low_shape), vmem(hidden_shape), vmem(low_shape),
            pltpu.VMEM((rows, features), F32), pltpu.VMEM((rows, 1), F32), pltpu.VMEM((rows, features), F32),
            pltpu.VMEM((parts, rows, hidden), F32), pltpu.VMEM((parts, columns + 16, features), BF16), vmem(w_up, parts), vmem(w_down, parts),
            pltpu.SemaphoreType.DMA((5, parts)),
        ],
    )
    q_got, da_turned, d_w_down = joined(q_got, da_turned, d_w_down)
    da_got = flipped(da_turned, "seq", masks[0])
    down_kept, down_got = halves_sent(d_w_down, "seq", masks[-1])
    context_rims = rims_of(d_context_turned)
    da_got, da_own, d_rest, down_got, context_rims = joined(da_got, da_own, d_rest, down_got, context_rims)
    rest_kept, rest_got = halves_sent(d_rest, "seq", masks[-1])
    da_cells = stacked(da_turned, da_got)
    [dq, d_w_q, d_b_q] = call(
        query_back_kernel, [row_shape, shape((columns, features), BF16), shape((16, features), F32)],
        *scalars, slopes, *keys, *values, da_own, q_raw, tokens,
        grid=(steps,), scalars=4,
        in_specs=[tile_spec, *placed, *v_placed, None, None, None],
        flops=3 * pair_flops, scratch=[sums],
    )
    for mask in masks[1:-1]:
        da_got = flipped(da_cells, "seq", mask)
        da_got, dq, k_own, da_cells, rest_got = joined(da_got, dq, k_own, da_cells, rest_got)
        da_cells = stacked(da_cells, da_got)
    da_got = flipped(da_cells, "seq", masks[-1])
    early = Chain(
        jnp.concatenate([added(down_kept, down_got), added(rest_kept, rest_got)]), "seq", masks_of("seq")[-2::-1]
    )
    early.start()
    k_own = after(k_own, da_cells, early.cells)
    queries = (q_cells, q_got)
    context_rims = after(context_rims, early.cells, da_cells)
    context_rim = jnp.concatenate([context_rims[0], d_context_turned, context_rims[1]], axis=1)
    dv_conv, d_taps_wide = call(
        conv_back_kernel, [heads_wide, shape((heads, BAND), F32)],
        scalars[1], scalars[3], mirrored, v_rim, d_context, context_rim,
        grid=(1,), scalars=2,
        flops=2 * rows * BAND * columns,
    )
    k_own = after(k_own, dv_conv)
    weights_back, slopes_back = call(
        weights_kernel, [tiles, tiles], *scalars, k_own, *queries,
        grid=(steps,), scalars=4,
        in_specs=[None, *placed],
        out_specs=[tile_spec, tile_spec],
        flops=8 * pair_flops, scratch=[pltpu.VMEM((rows, 1), jnp.int32)],
    )
    da_got, weights_back, dv_conv, da_cells = round_end([early], da_got, weights_back, dv_conv, da_cells)
    early.start()
    d_attended = (after(da_cells, early.cells), da_got)
    dk, dv, late = call(
        key_back_kernel, [row_shape, row_shape, shape((3 * columns + 64, features), BF16)],
        *scalars, weights_back, slopes_back, *queries, *d_attended, v_own, k_raw, dv_conv, d_taps_wide, d_b_q, d_w_q, tokens,
        grid=(steps,), scalars=4,
        in_specs=[tile_spec, tile_spec, *placed, *placed] + [None] * 7,
        flops=4 * pair_flops, scratch=[sums, sums],
    )
    late = Chain(late, "seq")
    d_tokens_part = sum(
        jnp.dot(part, w_turned[i], preferred_element_type=F32) for i, part in enumerate((dq, dk, dv))
    )
    token = Chain(d_tokens_part.astype(BF16), "mp")
    late.start()
    token.start()
    round_end([late, token, early])
    while early.left > 1:
        early.start()
        round_end([early])
    early.start()
    [late.cells] = round_end([early], late.cells)
    early_got = flipped(early.cells, "seq", masks[-1])
    late.start()
    token.start()
    while late.left > 1:
        ending = [chain for chain in (late, token) if chain.left]
        if late.left == 2:
            early_got, early.cells = round_end(ending, early_got, early.cells)
        else:
            round_end(ending)
        late.start()
        if token.left:
            token.start()
    d_tokens = (d_first + token.cells.astype(F32)).astype(BF16)
    upper = ((index & masks[-1]) != 0).astype(jnp.int32)[None]
    d_w_out, vectors, d_w_up, d_w_down = call(
        results_kernel,
        [shape(w_out.shape, F32), shape((16, features), F32), shape(w_up.shape, F32), shape(w_down.shape, F32)],
        upper, early.cells, early_got,
        grid=(1,), scalars=1,
    )
    d_w_qkv, d_b_qv, d_taps = call(
        late_results_kernel,
        [shape((3, columns, features), F32), shape((2, columns), F32), shape((heads, kernel), F32)],
        upper, late.cells, after(late.got, d_w_up),
        grid=(1,), scalars=1,
    )
    d_ln2_gain, d_ln2_bias, d_b_down, d_ln1_gain, d_ln1_bias, d_b_out, d_b_up = [vectors[i] for i in range(7)]
    return (
        layer_output, d_tokens, jnp.swapaxes(d_w_qkv, 1, 2), d_b_qv, d_taps, d_w_out, d_b_out, d_ln1_gain,
        d_ln1_bias, d_w_up, d_b_up, d_w_down, d_b_down, d_ln2_gain, d_ln2_bias,
    )


def solution(mesh):
    placed = (
        P("seq", None), P(), P(None, None, "mp"), P(None, "mp"), P("mp", None), P("mp", None), P(), P(), P(),
        P(None, "mp"), P("mp"), P("mp", None), P(), P(), P(), P("seq", None),
    )
    given = (
        P("seq", None), P("seq", None), P(None, None, "mp"), P(None, "mp"), P("mp", None), P("mp", None), P(),
        P(), P(), P(None, "mp"), P("mp"), P("mp", None), P(), P(), P(),
    )
    return jax.shard_map(per_device, mesh=mesh, in_specs=placed, out_specs=given, check_vma=False)
```

```python
import functools
import math

import jax
import jax.numpy as jnp
from jax import lax
from jax.experimental import pallas as pl
from jax.experimental.pallas import tpu as pltpu
from jax.sharding import PartitionSpec as P

SHRINK = 0.95
NORM_EPS = 1e-06
LAYER_EPS = 1e-05
F32 = jnp.float32
BF16 = jnp.bfloat16
KEYS = 256
CHUNK = 256
EDGE = 128
BAND = 3 * EDGE
MIDDLE = 256
WINDOW = 9216
VMEM_BYTES = 56 * 1024 * 1024
SQUARE_OF_V = (
    0.9999749564601563,
    -1.2727596259559684,
    0.4015752180623806,
    -0.19691031557208122,
    0.0973894823303103,
    -0.03584738041945528,
    0.006577941225358227,
)
SQUARE = tuple(factor * (0.5 * SHRINK) ** (0.5 * power) for power, factor in enumerate(SQUARE_OF_V))
SLOPE = 8.0 / math.pi
TAIL_AT = 0.2316419
TAIL = (0.319381530, -0.356563782, 1.781477937, -1.821255978, 1.330274429)


def dot(left, right, left_dim=1, right_dim=0):
    return lax.dot_general(
        left, right, (((left_dim,), (right_dim,)), ((), ())), preferred_element_type=F32
    )


def flipped(cells, axis, mask):
    return lax.ppermute(cells, axis, [(i, i ^ mask) for i in range(lax.axis_size(axis))])


def masks_of(axis):
    return [1 << bit for bit in range(lax.axis_size(axis).bit_length() - 2, -1, -1)]


def block_places(axis, masks):
    apart = jnp.arange(lax.axis_size(axis), dtype=jnp.int32) ^ lax.axis_index(axis).astype(jnp.int32)
    place = jnp.zeros_like(apart)
    for bit, mask in enumerate(masks):
        place = place | (jnp.where((apart & mask) != 0, 1, 0) << bit)
    return place


def halves_sent(cells, axis, mask):
    half = cells.shape[0] // 2
    upper = (lax.axis_index(axis) & mask) != 0
    sent = lax.dynamic_slice_in_dim(cells, jnp.where(upper, 0, half), half)
    kept = lax.dynamic_slice_in_dim(cells, jnp.where(upper, half, 0), half)
    return kept, flipped(sent, axis, mask)


def added(kept, got):
    return (kept.astype(F32) + got.astype(F32)).astype(BF16)


def united(cells, got, axis, mask):
    upper = (lax.axis_index(axis) & mask) != 0
    return jnp.concatenate([jnp.where(upper, got, cells), jnp.where(upper, cells, got)], axis=0)


class Chain:
    def __init__(self, cells, axis, masks=None):
        masks = masks or masks_of(axis)[::-1]
        self.cells, self.axis = cells, axis
        self.steps = [("halve", m) for m in masks[:-1]] + [("whole", masks[-1])]
        self.steps += [("gather", m) for m in masks[-2::-1]]
        self.at, self.got = 0, None

    def start(self):
        kind, mask = self.steps[self.at]
        if kind == "halve":
            self.cells, self.got = halves_sent(self.cells, self.axis, mask)
        else:
            self.got = flipped(self.cells, self.axis, mask)

    def finish(self):
        kind, mask = self.steps[self.at]
        self.at += 1
        if kind == "gather":
            self.cells = united(self.cells, self.got, self.axis, mask)
        else:
            self.cells = added(self.cells, self.got)

    @property
    def left(self):
        return len(self.steps) - self.at


def round_end(chains, *arrays):
    gots = [chain.got for chain in chains]
    *arrays, gots, cells = joined(*arrays, gots, [chain.cells for chain in chains])
    for chain, got, kept in zip(chains, gots, cells):
        chain.got, chain.cells = got, kept
        chain.finish()
    return arrays


def after(arrays, *earlier):
    return lax.optimization_barrier((arrays, *earlier))[0]


def joined(*arrays):
    return lax.optimization_barrier(arrays)


def stacked(*cells):
    return jnp.concatenate([part if part.ndim == 3 else part[None] for part in cells], axis=0)


def item_index(positions, ends):
    inside = (positions >= 0) & (positions < ends[-1])
    counted = jnp.sum((positions[:, None] >= ends[None, :]).astype(jnp.int32), axis=1)
    return jnp.where(inside, counted, -1)


def call(kernel, out_shape, *args, grid=(), in_specs=None, out_specs=None, scalars=0, flops=0, scratch=()):
    whole = lambda a: pl.BlockSpec(a.shape, lambda *_, n=len(a.shape): (0,) * n)
    ins = [whole(a) if s is None else s for a, s in zip(args[scalars:], in_specs or [None] * 99)]
    outs = [whole(a) if s is None else s for a, s in zip(out_shape, out_specs or [None] * 99)]
    moved = sum(a.size * a.dtype.itemsize for a in (*args, *out_shape))
    return pl.pallas_call(
        kernel,
        out_shape=out_shape,
        grid_spec=pltpu.PrefetchScalarGridSpec(
            num_scalar_prefetch=scalars,
            grid=grid,
            in_specs=ins,
            out_specs=outs,
            scratch_shapes=list(scratch),
        ),
        compiler_params=pltpu.CompilerParams(vmem_limit_bytes=VMEM_BYTES),
        cost_estimate=pl.CostEstimate(flops=1, bytes_accessed=1, transcendentals=0),
    )(*args)


def project_kernel(unit, raw, own, turned, tokens_ref, w_ref, bias_ref, *out_refs):
    out_refs = list(out_refs)
    raw_ref = out_refs.pop(0) if raw else None
    own_ref = out_refs.pop(0) if own else None
    turned_ref = out_refs.pop(0) if turned else None
    product = dot(w_ref[0], tokens_ref[...], 1, 1) + bias_ref[...]
    size = HEAD
    for head in range(product.shape[0] // size):
        part = product[head * size : (head + 1) * size, :]
        if raw:
            raw_ref[head] = part.T
        if unit:
            part = part * lax.rsqrt(jnp.sum(part * part, axis=0, keepdims=True) + NORM_EPS)
        if turned:
            turned_ref[head * size : (head + 1) * size, :] = part.astype(BF16)
        if own:
            own_ref[head] = part.T.astype(BF16)


def square_of(half):
    root = half * lax.rsqrt(half)
    square = jnp.full_like(root, SQUARE[-1])
    for factor in SQUARE[-2::-1]:
        square = square * root + factor
    return square


def item_of(positions, ends_ref):
    count = jnp.zeros_like(positions)
    for item in range(ends_ref.shape[0]):
        count = count + (positions >= ends_ref[item]).astype(jnp.int32)
    return jnp.where(positions < 0, -1, count)


def own_items(place_ref, ends_ref, rows):
    first = place_ref[place_ref.shape[0] - 1] * rows
    return item_of(first + lax.broadcasted_iota(jnp.int32, (rows, 1), 0), ends_ref)


def rim_items(place_ref, ends_ref, rows):
    first = place_ref[place_ref.shape[0] - 1] * rows - EDGE
    return item_of(first + lax.broadcasted_iota(jnp.int32, (1, rows + 2 * EDGE), 1), ends_ref)


def tile_of(span_ref):
    return span_ref[0] + jnp.minimum(pl.program_id(0), span_ref[1] - 1)


def held_at(far, near_ref, far_ref, group):
    return jnp.where(far, far_ref[0, group, :], near_ref[0, group, :])


def is_far(span_ref, place_ref, rows):
    return place_ref[tile_of(span_ref) // (rows // KEYS)] >= (place_ref.shape[0] - 1) // 2


def by_chunks(span_ref, rows, work):
    tile = span_ref[0] + pl.program_id(0)
    here = pl.program_id(0) < span_ref[1]
    meets = [
        (tile >= span_ref[2 + 2 * chunk]) & (tile < span_ref[3 + 2 * chunk]) for chunk in range(rows // CHUNK)
    ]
    every = functools.reduce(lambda x, y: x & y, meets)

    @pl.when(here & every)
    def _():
        work(slice(0, rows))

    for chunk, meet in enumerate(meets):

        @pl.when(here & meet & jnp.logical_not(every))
        def _(chunk=chunk):
            work(slice(chunk * CHUNK, (chunk + 1) * CHUNK))


def weights_kernel(
    span_ref, place_ref, v_place_ref, ends_ref, own_ref, near_ref, far_ref, weight_ref, slope_ref, mine_ref
):
    heads, rows, size = own_ref.shape
    far = is_far(span_ref, place_ref, rows)

    @pl.when(pl.program_id(0) == 0)
    def _():
        mine_ref[...] = own_items(place_ref, ends_ref, rows)

    def work(part):
        positions = tile_of(span_ref) * KEYS + lax.broadcasted_iota(jnp.int32, (1, KEYS), 1)
        same = mine_ref[part, :] == item_of(positions, ends_ref)
        for head in range(heads):
            scores = dot(own_ref[head, part, :], held_at(far, near_ref, far_ref, slice(head * size, (head + 1) * size)))
            half = 1.0 / SHRINK - scores
            square = square_of(half)
            fourth = square * square
            weight = jnp.where(same, fourth * fourth, 0.0)
            weight_ref[0, head, part, :] = weight.astype(BF16)
            slope = weight * lax.rsqrt(square * (half * (1.0 / SHRINK + scores)))
            slope_ref[0, head, part, :] = slope.astype(BF16)

    by_chunks(span_ref, rows, work)


def unit_back(grad, raw):
    scale = lax.rsqrt(jnp.sum(raw * raw, axis=-1, keepdims=True) + NORM_EPS)
    unit = raw * scale
    return scale * (grad - unit * jnp.sum(unit * grad, axis=-1, keepdims=True))


def split_low(wide):
    high = wide.astype(BF16)
    return high, (wide - high.astype(F32)).astype(BF16)


def band_of(taps_row):
    return pltpu.roll(jnp.broadcast_to(taps_row, (EDGE, BAND)), 0, 1, stride=1, stride_axis=0)


def around_of(mine, rim, start):
    return mine[start : start + EDGE, :] == rim[:, start : start + BAND]


def band_sums(taps_ref, head, mine, rim, values):
    band = band_of(taps_ref[head : head + 1, :])
    out = []
    for start in range(0, mine.shape[0], EDGE):
        high, low = split_low(jnp.where(around_of(mine, rim, start), band, 0.0))
        near = values[:, start : start + BAND]
        out.append(dot(high, near, 1, 1) + dot(low, near, 1, 1))
    return jnp.concatenate(out, axis=0)


def rim_values(v_place_ref, sides, own_ref, group):
    index, blocks, rows = v_place_ref[v_place_ref.shape[0] - 1], v_place_ref.shape[0] - 1, own_ref.shape[1]
    ends = []
    for (near_ref, far_ref), beside, part in zip(sides, (-1, 1), (slice(rows - EDGE, rows), slice(0, EDGE))):
        far = v_place_ref[jnp.clip(index + beside, 0, blocks - 1)] >= blocks // 2
        ends.append(jnp.where(far, far_ref[0, group, part], near_ref[0, group, part]))
    return jnp.concatenate([ends[0], own_ref[group, :], ends[1]], axis=1)


def attend_kernel(
    span_ref, place_ref, v_place_ref, ends_ref, weight_ref, v_near_ref, v_far_ref, taps_ref, own_ref,
    before_near_ref, before_far_ref, after_near_ref, after_far_ref, context_ref, raw_ref, v_rim_ref, sum_ref, conv_ref,
):
    heads, rows, size = raw_ref.shape
    far = is_far(span_ref, v_place_ref, rows)

    @pl.when(pl.program_id(0) == 0)
    def _():
        sides = ((before_near_ref, before_far_ref), (after_near_ref, after_far_ref))
        mine, rim = own_items(place_ref, ends_ref, rows), rim_items(place_ref, ends_ref, rows)
        for head in range(heads):
            group = slice(head * size, (head + 1) * size)
            values = rim_values(v_place_ref, sides, own_ref, group)
            v_rim_ref[group, :] = values
            conv_ref[head] = band_sums(taps_ref, head, mine, rim, values)
        sum_ref[...] = jnp.zeros_like(sum_ref)

    def work(part):
        for head in range(heads):
            values = held_at(far, v_near_ref, v_far_ref, slice(head * size, (head + 1) * size))
            sum_ref[head, part, :] += dot(weight_ref[0, head, part, :], values, 1, 1)

    by_chunks(span_ref, rows, work)

    @pl.when(pl.program_id(0) == pl.num_programs(0) - 1)
    def _():
        context = []
        for head in range(heads):
            raw = sum_ref[head]
            raw_ref[head] = raw
            unit = raw * lax.rsqrt(jnp.sum(raw * raw, axis=-1, keepdims=True) + NORM_EPS)
            context.append(unit + conv_ref[head])
        context_ref[...] = jnp.concatenate(context, axis=1).astype(BF16)


def finished(grad, tokens_ref, low_ref, weight_ref, start):
    turned = grad.T.astype(BF16)
    low_ref[...] = grad.astype(BF16)
    weight_ref[start : start + turned.shape[0], :] = dot(turned, tokens_ref[...]).astype(BF16)
    return row_sum(grad.astype(BF16).astype(F32))


def query_back_kernel(
    span_ref, place_ref, v_place_ref, ends_ref, slope_ref, k_near_ref, k_far_ref, v_near_ref, v_far_ref, da_ref, raw_ref,
    tokens_ref, dq_ref, d_w_ref, d_b_ref, sum_ref,
):
    heads, rows, size = raw_ref.shape
    far = is_far(span_ref, place_ref, rows)
    v_far = is_far(span_ref, v_place_ref, rows)

    @pl.when(pl.program_id(0) == 0)
    def _():
        sum_ref[...] = jnp.zeros_like(sum_ref)

    def work(part):
        for head in range(heads):
            group = slice(head * size, (head + 1) * size)
            slope = slope_ref[0, head, part, :].astype(F32)
            d_weights = dot(da_ref[head, part, :], held_at(v_far, v_near_ref, v_far_ref, group))
            d_scores = (d_weights * slope).astype(BF16)
            sum_ref[head, part, :] += dot(d_scores, held_at(far, k_near_ref, k_far_ref, group), 1, 1)

    by_chunks(span_ref, rows, work)

    @pl.when(pl.program_id(0) == pl.num_programs(0) - 1)
    def _():
        grads = [unit_back(sum_ref[head] * SLOPE, raw_ref[head]) for head in range(heads)]
        bias = finished(jnp.concatenate(grads, axis=1), tokens_ref, dq_ref, d_w_ref, 0)
        d_b_ref[...] = jnp.zeros_like(d_b_ref)
        d_b_ref[0:1, : bias.shape[1]] = bias


def key_back_kernel(
    span_ref, place_ref, v_place_ref, ends_ref, weight_ref, slope_ref, q_near_ref, q_far_ref, da_near_ref, da_far_ref, v_ref,
    raw_ref, dv_conv_ref, d_taps_ref, d_b_q_ref, d_w_q_ref, tokens_ref, dk_ref, dv_ref, late_ref, sum_ref, value_ref,
):
    heads, rows, size = raw_ref.shape
    columns = heads * size
    far = is_far(span_ref, place_ref, rows)

    @pl.when(pl.program_id(0) == 0)
    def _():
        sum_ref[...] = jnp.zeros_like(sum_ref)
        value_ref[...] = dv_conv_ref[...]

    def work(part):
        for head in range(heads):
            group = slice(head * size, (head + 1) * size)
            d_attn = held_at(far, da_near_ref, da_far_ref, group)
            slope = slope_ref[0, head, part, :].astype(F32)
            d_scores = (dot(v_ref[head, part, :], d_attn) * slope).astype(BF16)
            sum_ref[head, part, :] += dot(d_scores, held_at(far, q_near_ref, q_far_ref, group), 1, 1)
            value_ref[head, part, :] += dot(weight_ref[0, head, part, :], d_attn, 1, 1)

    by_chunks(span_ref, rows, work)

    @pl.when(pl.program_id(0) == pl.num_programs(0) - 1)
    def _():
        more = 3 * columns
        late_ref[more:, :] = jnp.zeros((late_ref.shape[0] - more, late_ref.shape[1]), BF16)
        late_ref[:columns, :] = d_w_q_ref[...]
        grads = [unit_back(sum_ref[head] * SLOPE, raw_ref[head]) for head in range(heads)]
        finished(jnp.concatenate(grads, axis=1), tokens_ref, dk_ref, late_ref, columns)
        grads = jnp.concatenate([value_ref[head] for head in range(heads)], axis=1)
        bias = finished(grads, tokens_ref, dv_ref, late_ref, 2 * columns)
        late_ref[more : more + 2, :columns] = jnp.concatenate(
            [d_b_q_ref[0:1, :columns], bias], axis=0
        ).astype(BF16)
        late_ref[more + 16 : more + 16 + heads, : d_taps_ref.shape[1]] = d_taps_ref[...].astype(BF16)


def conv_back_kernel(place_ref, ends_ref, taps_ref, values_ref, d_context_ref, turned_ref, dv_ref, d_taps_ref):
    heads, rows, size = d_context_ref.shape
    mine, rim = own_items(place_ref, ends_ref, rows), rim_items(place_ref, ends_ref, rows)
    for head in range(heads):
        group = slice(head * size, (head + 1) * size)
        dv_ref[head] = band_sums(taps_ref, head, mine, rim, turned_ref[group, :])
        values = values_ref[group, :]
        lined = jnp.zeros((8, BAND), F32)
        for start in range(0, rows, EDGE):
            pairs = dot(d_context_ref[head, start : start + EDGE, :], values[:, start : start + BAND])
            pairs = jnp.where(around_of(mine, rim, start), pairs, 0.0)
            for row in range(0, EDGE, 8):
                part = pairs[row : row + 8, :]
                lined = lined + (pltpu.roll(part, BAND - row, 1) if row else part)
        total = lined[0:1, :]
        for row in range(1, 8):
            total = total + pltpu.roll(lined[row : row + 1, :], BAND - row, 1)
        d_taps_ref[head : head + 1, :] = total


def normal_of(u):
    density = jnp.exp(u * u * -0.5) * (1.0 / math.sqrt(2.0 * math.pi))
    ratio = 1.0 / (1.0 + TAIL_AT * jnp.abs(u))
    tail = jnp.full_like(ratio, TAIL[-1])
    for factor in TAIL[-2::-1]:
        tail = tail * ratio + factor
    tail = tail * (ratio * density)
    return jnp.where(u >= 0.0, 1.0 - tail, tail), density


def normed_of(hidden):
    center = hidden - jnp.mean(hidden, axis=-1, keepdims=True)
    scale = lax.rsqrt(jnp.mean(center * center, axis=-1, keepdims=True) + LAYER_EPS)
    return center * scale, scale


def normed_back(grad, normed, scale, gain):
    d_normed = grad * gain
    centered = d_normed - jnp.mean(d_normed, axis=-1, keepdims=True)
    return scale * (centered - normed * jnp.mean(d_normed * normed, axis=-1, keepdims=True))


def row_sum(array):
    return jnp.sum(array, axis=0, keepdims=True)


def middle_kernel(parts, *refs):
    tokens_ref, near_ref, far_ref, vectors_ref, d_out_ref, raw_ref = refs[:6]
    contexts = [half.at[i] for half in (near_ref, far_ref) for i in range(parts // 2)]
    (
        result_ref, d_first_ref, d_rest_ref, d_w_down_ref,
        d_context_ref, turned_ref, da_ref, da_turned_ref,
        y_low_ref, act_ref, d_second_low_ref, d_inner_ref, d_first_low_ref,
        normed_ref, scale_ref, mixed_ref, factor_ref, out_ref, up_ref, down_ref, sem_ref,
    ) = refs[6 + 5 * parts :]
    heads, rows, size = raw_ref.shape
    columns = heads * size
    b_out, gain_one, bias_one, b_down, gain_two, bias_two = [vectors_ref[i : i + 1, :] for i in range(6)]
    chunks = [slice(start, start + MIDDLE) for start in range(0, rows, MIDDLE)]
    up_cut, down_cut = up_ref.shape[1] // 3, 3 * down_ref.shape[1] // 4
    targets = [
        (0, 0, up_ref, 0, up_cut),
        (1, 0, up_ref, up_cut, up_ref.shape[1] - up_cut),
        (2, 0, down_ref, 0, down_cut),
        (3, 0, down_ref, down_cut, down_ref.shape[1] - down_cut),
        (4, 0, out_ref, 0, out_ref.shape[1]),
    ]
    copies = [
        [
            pltpu.make_async_copy(
                refs[6 + piece * parts + part].at[first : first + count, :],
                to.at[part, start : start + count, :],
                sem_ref.at[i, part],
            )
            for part in range(parts)
        ]
        for i, (piece, first, to, start, count) in enumerate(targets)
    ]
    copies = copies[-1:] + copies[:-1]
    for of in copies:
        for part in range(parts):
            of[part].start()

    for part in range(parts):
        copies[0][part].wait()
    for chunk in chunks:
        hidden = tokens_ref[chunk, :].astype(F32) + b_out
        for part in range(parts):
            hidden = hidden + dot(contexts[part][chunk, :], out_ref[part, :columns, :])
        normed, scale = normed_of(hidden)
        normed_ref[chunk, :] = normed
        scale_ref[chunk, :] = scale
        first = normed * gain_one + bias_one
        y_low_ref[chunk, :] = first.astype(BF16)
        mixed_ref[chunk, :] = first + b_down

    for part in range(parts):
        for of in copies[1:]:
            of[part].wait()
        b_up = row_sum(out_ref[part, columns : columns + 16, :].astype(F32))
        for chunk in chunks:
            inner = dot(y_low_ref[chunk, :], up_ref[part]) + b_up
            share, density = normal_of(inner)
            act = (inner * share).astype(BF16)
            factor_ref[part, chunk, :] = share + inner * density
            if part == 0:
                act_ref[chunk, :] = act
            mixed_ref[chunk, :] += dot(act, down_ref[part])

    sums = [0.0] * 7
    for chunk in chunks:
        normed, scale = normed_of(mixed_ref[chunk, :])
        result_ref[chunk, :] = (normed * gain_two + bias_two).astype(BF16)
        grad = d_out_ref[chunk, :].astype(F32)
        d_second = normed_back(grad, normed, scale, gain_two)
        d_second_low_ref[chunk, :] = d_second.astype(BF16)
        mixed_ref[chunk, :] = d_second
        for i, array in enumerate((grad * normed, grad, d_second)):
            sums[i] = sums[i] + row_sum(array)

    d_w_down_ref[...] = dot(act_ref[...], d_second_low_ref[...], 0, 0).astype(BF16)
    for part in range(parts):
        for chunk in chunks:
            d_act = dot(d_second_low_ref[chunk, :], down_ref[part], 1, 1)
            d_inner = (d_act * factor_ref[part, chunk, :]).astype(BF16)
            if part == 0:
                d_inner_ref[chunk, :] = d_inner
                sums[6] = sums[6] + row_sum(d_inner.astype(F32))
            mixed_ref[chunk, :] += dot(d_inner, up_ref[part], 1, 1)
        if part == 0:
            d_rest_ref[: y_low_ref.shape[1], :] = dot(y_low_ref[...], d_inner_ref[...], 0, 0).astype(BF16)

    for chunk in chunks:
        grad = mixed_ref[chunk, :]
        normed = normed_ref[chunk, :]
        d_first = normed_back(grad, normed, scale_ref[chunk, :], gain_one)
        d_first_ref[chunk, :] = d_first
        d_first_low = d_first.astype(BF16)
        d_first_low_ref[chunk, :] = d_first_low
        for i, array in enumerate((grad * normed, grad, d_first)):
            sums[3 + i] = sums[3 + i] + row_sum(array)
        d_context = dot(d_first_low, out_ref[0, :columns, :], 1, 1).astype(BF16).astype(F32)
        turned_ref[:, chunk] = d_context.T.astype(BF16)
        grads = []
        for head in range(heads):
            grad = d_context[:, head * size : (head + 1) * size]
            d_context_ref[head, chunk, :] = grad.astype(BF16)
            grad = unit_back(grad, raw_ref[head, chunk, :])
            da_ref[head, chunk, :] = grad.astype(BF16)
            grads.append(grad)
        da_turned_ref[:, chunk] = jnp.concatenate(grads, axis=1).T.astype(BF16)
    at_out = y_low_ref.shape[1]
    d_rest_ref[at_out : at_out + columns, :] = dot(contexts[0][...], d_first_low_ref[...], 0, 0).astype(BF16)
    sums.append(jnp.zeros((57, sums[0].shape[1]), F32))
    d_rest_ref[at_out + columns :, :] = jnp.concatenate(sums, axis=0).astype(BF16)


def whole_of(upper_ref, own, got):
    upper = upper_ref[0] != 0
    return jnp.concatenate([jnp.where(upper, got, own), jnp.where(upper, own, got)], axis=0).astype(F32)


def late_results_kernel(upper_ref, late_ref, got_ref, d_w_ref, d_b_ref, d_taps_ref):
    late = whole_of(upper_ref, late_ref[...], got_ref[...])
    columns = d_w_ref.shape[1]
    for i in range(3):
        d_w_ref[i] = late[i * columns : (i + 1) * columns, :]
    more = 3 * columns
    d_b_ref[...] = late[more : more + 2, :columns]
    heads, kernel = d_taps_ref.shape
    start = EDGE - (kernel - 1) // 2
    d_taps_ref[...] = late[more + 16 : more + 16 + heads, start : start + kernel]


def results_kernel(
    upper_ref, early_ref, got_ref, d_out_ref, vectors_ref, d_up_ref, d_down_ref
):
    columns = d_out_ref.shape[0]
    cut = d_down_ref.shape[0] // 2
    d_down_ref[...] = whole_of(upper_ref, early_ref[:cut, :], got_ref[:cut, :])
    rest = whole_of(upper_ref, early_ref[cut:, :], got_ref[cut:, :])
    at_out = d_up_ref.shape[0]
    d_up_ref[...] = rest[:at_out, :]
    d_out_ref[...] = rest[at_out : at_out + columns, :]
    vectors_ref[...] = rest[at_out + columns : at_out + columns + 16, :]


HEAD = 64


def per_device(
    tokens, item_lengths, w_qkv, b_qv, taps, w_out, b_out, ln1_gain, ln1_bias, w_up, b_up, w_down, b_down,
    ln2_gain, ln2_bias, d_out,
):
    rows, features = tokens.shape
    heads, kernel = taps.shape
    radius = (kernel - 1) // 2
    columns = w_qkv.shape[2]
    size = columns // heads
    hidden = w_up.shape[1]
    blocks = lax.axis_size("seq")
    total = blocks * rows
    index = lax.axis_index("seq").astype(jnp.int32)
    first_row = index * rows
    shape = jax.ShapeDtypeStruct
    heads_wide, heads_low = shape((heads, rows, size), F32), shape((heads, rows, size), BF16)
    turned_shape, row_shape = shape((columns, rows), BF16), shape((rows, columns), BF16)
    wide_shape, low_shape = shape((rows, features), F32), shape((rows, features), BF16)

    w_turned = jnp.swapaxes(w_qkv, 1, 2)
    biases = jnp.stack([b_qv[0], jnp.zeros_like(b_qv[0]), b_qv[1]])[:, :, None]

    def project(x, which, unit, outs, *flags):
        return call(
            functools.partial(project_kernel, unit, *flags), outs, x, w_turned, biases[which],
            grid=(1,),
            in_specs=[None, pl.BlockSpec((1, columns, features), lambda *_: (which, 0, 0)), None],
            flops=2 * rows * columns * features,
        )

    masks = masks_of("seq")
    v_masks = masks[-1:] + masks[:-1]
    ahead = [(i, i + 1) for i in range(blocks - 1)]
    behind = [(i + 1, i) for i in range(blocks - 1)]

    reach = EDGE - radius

    def rims_of(turned):
        ends = turned[:, rows - EDGE :], turned[:, :EDGE]
        return [lax.ppermute(end, "seq", pairs) for end, pairs in zip(ends, (ahead, behind))]

    reach = EDGE - radius

    steps = min(total, WINDOW) // KEYS
    per = rows // KEYS
    at_of = lambda i, span_ref: span_ref[0] + jnp.minimum(i, span_ref[1] - 1)
    tile_spec = pl.BlockSpec(
        (1, heads, rows, KEYS), lambda i, span_ref, *_: (jnp.minimum(i, span_ref[1] - 1), 0, 0, 0)
    )
    half = blocks // 2

    def halves_of(which):
        def spec(index_of):
            return pl.BlockSpec(
                (1, columns, KEYS),
                lambda i, *refs: (index_of(refs[which][at_of(i, refs[0]) // per]), 0, at_of(i, refs[0]) % per),
            )

        return [spec(lambda place: jnp.minimum(place, half - 1)), spec(lambda place: jnp.maximum(place - half, 0))]

    def side_of(beside):
        def spec(index_of):
            return pl.BlockSpec(
                (1, columns, rows),
                lambda i, *refs: (index_of(refs[2][jnp.clip(refs[2][blocks] + beside, 0, blocks - 1)]), 0, 0),
            )

        return [spec(lambda place: jnp.minimum(place, half - 1)), spec(lambda place: jnp.maximum(place - half, 0))]

    placed, v_placed = halves_of(1), halves_of(2)
    ordered = pl.BlockSpec((1, columns, KEYS), lambda i, *refs: (at_of(i, refs[0]) // per, 0, at_of(i, refs[0]) % per))
    tiles = shape((steps, heads, rows, KEYS), BF16)
    sums = pltpu.VMEM((heads, rows, size), F32)
    pair_flops = 2 * rows * (total // 2) * columns

    def tables(item_lengths):
        count = item_lengths.shape[0]
        upto = jnp.arange(count)[None, :] <= jnp.arange(count)[:, None]
        ends = jnp.sum(jnp.where(upto, item_lengths[None, :], 0), axis=1)
        starts = first_row + CHUNK * jnp.arange(rows // CHUNK, dtype=jnp.int32)[:, None]
        lows = jnp.max(jnp.where(ends[None, :] <= starts, ends[None, :], 0), axis=1)
        highs = jnp.min(jnp.where(ends[None, :] >= starts + CHUNK, ends[None, :], total), axis=1)
        bounds = jnp.stack([lows // KEYS, (highs + KEYS - 1) // KEYS], axis=1)
        span = jnp.concatenate(
            [jnp.stack([bounds[0, 0], bounds[-1, 1] - bounds[0, 0]]), bounds.reshape(-1)]
        ).astype(jnp.int32)
        place, v_place = [jnp.concatenate([block_places("seq", order), index[None]]) for order in (masks, v_masks)]
        return span, place, v_place, ends

    small = taps, [b_out, ln1_gain, ln1_bias, b_down, ln2_gain, ln2_bias]
    [k_turned] = project(tokens, 1, True, [turned_shape], False, False, True)
    k_got = flipped(k_turned, "seq", masks[0])
    far, close = masks_of("mp")
    b_high = lax.reduce_precision(b_up, 8, 7)
    b_mid = lax.reduce_precision(b_up - b_high, 8, 7)
    b_split = jnp.stack([b_high, b_mid, b_up - b_high - b_mid]).astype(BF16)
    w_out_more = jnp.concatenate([w_out, b_split, jnp.zeros((13, features), BF16)])
    up_cut, down_cut = w_up.shape[0] // 3, 3 * w_down.shape[0] // 4
    own = [w_up[:up_cut], w_up[up_cut:], w_down[:down_cut], w_down[down_cut:], w_out_more]
    far_got, last_got = [None] * 5, [None] * 5
    close_got = [flipped(after(array, k_turned), "mp", close) for array in own[:2]]
    k_got, late_tokens, late_lengths, own, close_got = joined(k_got, tokens, item_lengths, own, close_got)
    k_cells = stacked(k_turned, k_got)
    k_got = flipped(k_cells, "seq", masks[1])
    late_tokens, late_lengths, own = after((late_tokens, late_lengths, own), k_cells)
    v_own, v_turned = project(late_tokens, 2, False, [heads_low, turned_shape], False, True, True)
    v_got = flipped(v_turned, "seq", v_masks[0])
    far_got[0] = flipped(own[0], "mp", far)
    q_raw, q_own, q_turned = project(late_tokens, 0, True, [heads_wide, heads_low, turned_shape], True, True, True)
    scalars = tables(late_lengths)
    close_got += [flipped(array, "mp", close) for array in own[2:]]
    k_got, v_got, q_own, scalars, far_got[0], own, late_tokens, small, close_got = joined(
        k_got, v_got, q_own, scalars, far_got[0], own, late_tokens, small, close_got
    )
    k_cells = stacked(k_cells, k_got)
    v_cells = stacked(v_turned, v_got)
    for mask in masks[2:-1]:
        k_got, k_cells = joined(flipped(k_cells, "seq", mask), k_cells)
        k_cells = stacked(k_cells, k_got)
    for mask in v_masks[1:-2]:
        v_got, v_cells = joined(flipped(v_cells, "seq", mask), v_cells)
        v_cells = stacked(v_cells, v_got)
    k_got = flipped(k_cells, "seq", masks[-1])
    v_got = flipped(v_cells, "seq", v_masks[-2])
    own, far_got[0], late_tokens, small = after((own, far_got[0], late_tokens, small), k_cells)
    k_raw, k_own = project(late_tokens, 1, True, [heads_wide, heads_low], True, True, False)
    taps, vectors = small
    vectors = jnp.stack([*vectors, vectors[0], vectors[0]])
    banded = jnp.pad(taps, ((0, 0), (reach, BAND - reach - kernel)))
    mirrored = jnp.pad(taps[:, ::-1], ((0, 0), (reach, BAND - reach - kernel)))
    far_got[1] = flipped(own[1], "mp", far)
    last_got[0] = flipped(far_got[0], "mp", close)
    k_got, v_got, v_cells, far_got[1], last_got[0], own[2], q_own, k_own, k_raw, banded = joined(
        k_got, v_got, v_cells, far_got[1], last_got[0], own[2], q_own, k_own, k_raw, banded
    )
    v_cells = stacked(v_cells, v_got)
    v_got = flipped(v_cells, "seq", v_masks[-1])
    keys = (k_cells, k_got)
    weights, slopes = call(
        weights_kernel, [tiles, tiles], *scalars, q_own, *keys,
        grid=(steps,), scalars=4,
        in_specs=[None, *placed],
        out_specs=[tile_spec, tile_spec],
        flops=8 * pair_flops, scratch=[pltpu.VMEM((rows, 1), jnp.int32)],
    )
    far_got[2], last_got[1] = flipped(own[2], "mp", far), flipped(far_got[1], "mp", close)
    v_got, weights, q_turned, far_got[2], last_got[1], own[3] = joined(
        v_got, weights, q_turned, far_got[2], last_got[1], own[3]
    )
    values = (v_cells, v_got)
    far_got[3], far_got[4] = [flipped(own[piece], "mp", far) for piece in (3, 4)]
    last_got[2] = flipped(far_got[2], "mp", close)
    q_got = flipped(q_turned, "seq", masks[0])
    context, attended, v_rim = call(
        attend_kernel, [row_shape, heads_wide, shape((columns, rows + 2 * EDGE), BF16)],
        *scalars, weights, *values, banded, v_turned, *values, *values,
        grid=(steps,), scalars=4,
        in_specs=[tile_spec, *v_placed, None, None, *side_of(-1), *side_of(1)],
        flops=pair_flops, scratch=[sums, sums],
    )
    q_got, context, far_got[3], far_got[4], last_got[2] = joined(
        q_got, context, far_got[3], far_got[4], last_got[2]
    )
    q_cells = stacked(q_turned, q_got)
    q_got = flipped(q_cells, "seq", masks[1])
    context_got = flipped(context, "mp", far)
    last_got[3], last_got[4] = [flipped(far_got[piece], "mp", close) for piece in (3, 4)]
    parts = 4
    held = [kind[piece] for piece in range(len(own)) for kind in (own, far_got, close_got, last_got)]
    context_got, q_got, q_cells, held = joined(context_got, q_got, q_cells, held)
    q_cells = stacked(q_cells, q_got)
    for mask in masks[2:-1]:
        q_got, q_cells = joined(flipped(q_cells, "seq", mask), q_cells)
        q_cells = stacked(q_cells, q_got)
    q_got = flipped(q_cells, "seq", masks[-1])
    context_cells = stacked(context, context_got)
    contexts = (context_cells, flipped(context_cells, "mp", close))

    vmem = lambda a, *lead: pltpu.VMEM((*lead, *a.shape), a.dtype)
    anywhere = pl.BlockSpec(memory_space=pl.ANY)
    hidden_shape = shape((rows, hidden), BF16)
    (
        layer_output, d_first, d_rest, d_w_down, d_context, d_context_turned, da_own, da_turned,
    ) = call(
        functools.partial(middle_kernel, parts),
        [
            low_shape, wide_shape, shape((features + columns + 64, features), BF16), shape(w_down.shape, BF16),
            heads_low, turned_shape, heads_low, turned_shape,
        ],
        tokens, *contexts, vectors, d_out, attended, *held,
        grid=(1,),
        in_specs=[None] * 6 + [anywhere] * len(held),
        flops=8 * rows * parts * w_up.size,
        scratch=[
            vmem(low_shape), vmem(hidden_shape), vmem(low_shape), vmem(hidden_shape), vmem(low_shape),
            pltpu.VMEM((rows, features), F32), pltpu.VMEM((rows, 1), F32), pltpu.VMEM((rows, features), F32),
            pltpu.VMEM((parts, rows, hidden), F32), pltpu.VMEM((parts, columns + 16, features), BF16), vmem(w_up, parts), vmem(w_down, parts),
            pltpu.SemaphoreType.DMA((5, parts)),
        ],
    )
    q_got, da_turned, d_w_down = joined(q_got, da_turned, d_w_down)
    da_got = flipped(da_turned, "seq", masks[0])
    down_kept, down_got = halves_sent(d_w_down, "seq", masks[-1])
    context_rims = rims_of(d_context_turned)
    da_got, da_own, d_rest, down_got, context_rims = joined(da_got, da_own, d_rest, down_got, context_rims)
    rest_kept, rest_got = halves_sent(d_rest, "seq", masks[-1])
    da_cells = stacked(da_turned, da_got)
    [dq, d_w_q, d_b_q] = call(
        query_back_kernel, [row_shape, shape((columns, features), BF16), shape((16, features), F32)],
        *scalars, slopes, *keys, *values, da_own, q_raw, tokens,
        grid=(steps,), scalars=4,
        in_specs=[tile_spec, *placed, *v_placed, None, None, None],
        flops=3 * pair_flops, scratch=[sums],
    )
    for mask in masks[1:-1]:
        da_got = flipped(da_cells, "seq", mask)
        da_got, dq, k_own, da_cells, rest_got = joined(da_got, dq, k_own, da_cells, rest_got)
        da_cells = stacked(da_cells, da_got)
    da_got = flipped(da_cells, "seq", masks[-1])
    early = Chain(
        jnp.concatenate([added(down_kept, down_got), added(rest_kept, rest_got)]), "seq", masks_of("seq")[-2::-1]
    )
    early.start()
    k_own = after(k_own, da_cells, early.cells)
    queries = (q_cells, q_got)
    context_rims = after(context_rims, early.cells, da_cells)
    context_rim = jnp.concatenate([context_rims[0], d_context_turned, context_rims[1]], axis=1)
    dv_conv, d_taps_wide = call(
        conv_back_kernel, [heads_wide, shape((heads, BAND), F32)],
        scalars[1], scalars[3], mirrored, v_rim, d_context, context_rim,
        grid=(1,), scalars=2,
        flops=2 * rows * BAND * columns,
    )
    k_own = after(k_own, dv_conv)
    weights_back, slopes_back = call(
        weights_kernel, [tiles, tiles], *scalars, k_own, *queries,
        grid=(steps,), scalars=4,
        in_specs=[None, *placed],
        out_specs=[tile_spec, tile_spec],
        flops=8 * pair_flops, scratch=[pltpu.VMEM((rows, 1), jnp.int32)],
    )
    da_got, weights_back, dv_conv, da_cells = round_end([early], da_got, weights_back, dv_conv, da_cells)
    early.start()
    d_attended = (after(da_cells, early.cells), da_got)
    dk, dv, late = call(
        key_back_kernel, [row_shape, row_shape, shape((3 * columns + 64, features), BF16)],
        *scalars, weights_back, slopes_back, *queries, *d_attended, v_own, k_raw, dv_conv, d_taps_wide, d_b_q, d_w_q, tokens,
        grid=(steps,), scalars=4,
        in_specs=[tile_spec, tile_spec, *placed, *placed] + [None] * 7,
        flops=4 * pair_flops, scratch=[sums, sums],
    )
    late = Chain(late, "seq")
    late.start()
    d_parts = after((dq, dk, dv), late.cells)
    d_tokens_part = sum(
        jnp.dot(part, w_turned[i], preferred_element_type=F32) for i, part in enumerate(d_parts)
    )
    token = Chain(d_tokens_part.astype(BF16), "mp")
    token.start()
    round_end([late, token, early])
    while early.left > 1:
        early.start()
        round_end([early])
    early.start()
    [late.cells] = round_end([early], late.cells)
    early_got = flipped(early.cells, "seq", masks[-1])
    late.start()
    token.start()
    while late.left > 1:
        ending = [chain for chain in (late, token) if chain.left]
        if late.left == 2:
            early_got, early.cells = round_end(ending, early_got, early.cells)
        else:
            round_end(ending)
        late.start()
        if token.left:
            token.start()
    d_tokens = (d_first + token.cells.astype(F32)).astype(BF16)
    upper = ((index & masks[-1]) != 0).astype(jnp.int32)[None]
    d_w_out, vectors, d_w_up, d_w_down = call(
        results_kernel,
        [shape(w_out.shape, F32), shape((16, features), F32), shape(w_up.shape, F32), shape(w_down.shape, F32)],
        upper, early.cells, early_got,
        grid=(1,), scalars=1,
    )
    d_w_qkv, d_b_qv, d_taps = call(
        late_results_kernel,
        [shape((3, columns, features), F32), shape((2, columns), F32), shape((heads, kernel), F32)],
        upper, late.cells, after(late.got, d_w_up),
        grid=(1,), scalars=1,
    )
    d_ln2_gain, d_ln2_bias, d_b_down, d_ln1_gain, d_ln1_bias, d_b_out, d_b_up = [vectors[i] for i in range(7)]
    return (
        layer_output, d_tokens, jnp.swapaxes(d_w_qkv, 1, 2), d_b_qv, d_taps, d_w_out, d_b_out, d_ln1_gain,
        d_ln1_bias, d_w_up, d_b_up, d_w_down, d_b_down, d_ln2_gain, d_ln2_bias,
    )


def solution(mesh):
    placed = (
        P("seq", None), P(), P(None, None, "mp"), P(None, "mp"), P("mp", None), P("mp", None), P(), P(), P(),
        P(None, "mp"), P("mp"), P("mp", None), P(), P(), P(), P("seq", None),
    )
    given = (
        P("seq", None), P("seq", None), P(None, None, "mp"), P(None, "mp"), P("mp", None), P("mp", None), P(),
        P(), P(), P(None, "mp"), P("mp"), P("mp", None), P(), P(), P(),
    )
    return jax.shard_map(per_device, mesh=mesh, in_specs=placed, out_specs=given, check_vma=False)
```

```python
import functools
import math

import jax
import jax.numpy as jnp
from jax import lax
from jax.experimental import pallas as pl
from jax.experimental.pallas import tpu as pltpu
from jax.sharding import PartitionSpec as P

SHRINK = 0.95
NORM_EPS = 1e-06
LAYER_EPS = 1e-05
F32 = jnp.float32
BF16 = jnp.bfloat16
KEYS = 256
CHUNK = 256
EDGE = 128
BAND = 3 * EDGE
MIDDLE = 256
WINDOW = 9216
VMEM_BYTES = 56 * 1024 * 1024
SQUARE_OF_V = (
    0.9999936361319989,
    -1.2731008162270503,
    0.4040306859655804,
    -0.20598641392473288,
    0.11615118744625774,
    -0.05772567810293111,
    0.02001158958170149,
    -0.00337422878652264,
)
SQUARE = tuple(factor * (0.5 * SHRINK) ** (0.5 * power) for power, factor in enumerate(SQUARE_OF_V))
SLOPE = 8.0 / math.pi
TAIL_AT = 0.2316419
TAIL = (0.319381530, -0.356563782, 1.781477937, -1.821255978, 1.330274429)


def dot(left, right, left_dim=1, right_dim=0):
    return lax.dot_general(
        left, right, (((left_dim,), (right_dim,)), ((), ())), preferred_element_type=F32
    )


def flipped(cells, axis, mask):
    return lax.ppermute(cells, axis, [(i, i ^ mask) for i in range(lax.axis_size(axis))])


def masks_of(axis):
    return [1 << bit for bit in range(lax.axis_size(axis).bit_length() - 2, -1, -1)]


def block_places(axis, masks):
    apart = jnp.arange(lax.axis_size(axis), dtype=jnp.int32) ^ lax.axis_index(axis).astype(jnp.int32)
    place = jnp.zeros_like(apart)
    for bit, mask in enumerate(masks):
        place = place | (jnp.where((apart & mask) != 0, 1, 0) << bit)
    return place


def halves_sent(cells, axis, mask):
    half = cells.shape[0] // 2
    upper = (lax.axis_index(axis) & mask) != 0
    sent = lax.dynamic_slice_in_dim(cells, jnp.where(upper, 0, half), half)
    kept = lax.dynamic_slice_in_dim(cells, jnp.where(upper, half, 0), half)
    return kept, flipped(sent, axis, mask)


def added(kept, got):
    return (kept.astype(F32) + got.astype(F32)).astype(BF16)


def united(cells, got, axis, mask):
    upper = (lax.axis_index(axis) & mask) != 0
    return jnp.concatenate([jnp.where(upper, got, cells), jnp.where(upper, cells, got)], axis=0)


class Chain:
    def __init__(self, cells, axis, masks=None):
        masks = masks or masks_of(axis)[::-1]
        self.cells, self.axis = cells, axis
        self.steps = [("halve", m) for m in masks[:-1]] + [("whole", masks[-1])]
        self.steps += [("gather", m) for m in masks[-2::-1]]
        self.at, self.got = 0, None

    def start(self):
        kind, mask = self.steps[self.at]
        if kind == "halve":
            self.cells, self.got = halves_sent(self.cells, self.axis, mask)
        else:
            self.got = flipped(self.cells, self.axis, mask)

    def finish(self):
        kind, mask = self.steps[self.at]
        self.at += 1
        if kind == "gather":
            self.cells = united(self.cells, self.got, self.axis, mask)
        else:
            self.cells = added(self.cells, self.got)

    @property
    def left(self):
        return len(self.steps) - self.at


def round_end(chains, *arrays):
    gots = [chain.got for chain in chains]
    *arrays, gots, cells = joined(*arrays, gots, [chain.cells for chain in chains])
    for chain, got, kept in zip(chains, gots, cells):
        chain.got, chain.cells = got, kept
        chain.finish()
    return arrays


def after(arrays, *earlier):
    return lax.optimization_barrier((arrays, *earlier))[0]


def joined(*arrays):
    return lax.optimization_barrier(arrays)


def stacked(*cells):
    return jnp.concatenate([part if part.ndim == 3 else part[None] for part in cells], axis=0)


def item_index(positions, ends):
    inside = (positions >= 0) & (positions < ends[-1])
    counted = jnp.sum((positions[:, None] >= ends[None, :]).astype(jnp.int32), axis=1)
    return jnp.where(inside, counted, -1)


def call(kernel, out_shape, *args, grid=(), in_specs=None, out_specs=None, scalars=0, flops=0, scratch=()):
    whole = lambda a: pl.BlockSpec(a.shape, lambda *_, n=len(a.shape): (0,) * n)
    ins = [whole(a) if s is None else s for a, s in zip(args[scalars:], in_specs or [None] * 99)]
    outs = [whole(a) if s is None else s for a, s in zip(out_shape, out_specs or [None] * 99)]
    moved = sum(a.size * a.dtype.itemsize for a in (*args, *out_shape))
    return pl.pallas_call(
        kernel,
        out_shape=out_shape,
        grid_spec=pltpu.PrefetchScalarGridSpec(
            num_scalar_prefetch=scalars,
            grid=grid,
            in_specs=ins,
            out_specs=outs,
            scratch_shapes=list(scratch),
        ),
        compiler_params=pltpu.CompilerParams(vmem_limit_bytes=VMEM_BYTES),
        cost_estimate=pl.CostEstimate(flops=1, bytes_accessed=1, transcendentals=0),
    )(*args)


def project_kernel(unit, raw, own, turned, tokens_ref, w_ref, bias_ref, *out_refs):
    out_refs = list(out_refs)
    raw_ref = out_refs.pop(0) if raw else None
    own_ref = out_refs.pop(0) if own else None
    turned_ref = out_refs.pop(0) if turned else None
    product = dot(w_ref[0], tokens_ref[...], 1, 1) + bias_ref[...]
    size = HEAD
    for head in range(product.shape[0] // size):
        part = product[head * size : (head + 1) * size, :]
        if raw:
            raw_ref[head] = part.T
        if unit:
            part = part * lax.rsqrt(jnp.sum(part * part, axis=0, keepdims=True) + NORM_EPS)
        if turned:
            turned_ref[head * size : (head + 1) * size, :] = part.astype(BF16)
        if own:
            own_ref[head] = part.T.astype(BF16)


def square_of(half):
    root = half * lax.rsqrt(half)
    square = jnp.full_like(root, SQUARE[-1])
    for factor in SQUARE[-2::-1]:
        square = square * root + factor
    return square


def item_of(positions, ends_ref):
    count = jnp.zeros_like(positions)
    for item in range(ends_ref.shape[0]):
        count = count + (positions >= ends_ref[item]).astype(jnp.int32)
    return jnp.where(positions < 0, -1, count)


def own_items(place_ref, ends_ref, rows):
    first = place_ref[place_ref.shape[0] - 1] * rows
    return item_of(first + lax.broadcasted_iota(jnp.int32, (rows, 1), 0), ends_ref)


def rim_items(place_ref, ends_ref, rows):
    first = place_ref[place_ref.shape[0] - 1] * rows - EDGE
    return item_of(first + lax.broadcasted_iota(jnp.int32, (1, rows + 2 * EDGE), 1), ends_ref)


def tile_of(span_ref):
    return span_ref[0] + jnp.minimum(pl.program_id(0), span_ref[1] - 1)


def held_at(far, near_ref, far_ref, group):
    return jnp.where(far, far_ref[0, group, :], near_ref[0, group, :])


def is_far(span_ref, place_ref, rows):
    return place_ref[tile_of(span_ref) // (rows // KEYS)] >= (place_ref.shape[0] - 1) // 2


def by_chunks(span_ref, rows, work):
    tile = span_ref[0] + pl.program_id(0)
    here = pl.program_id(0) < span_ref[1]
    meets = [
        (tile >= span_ref[2 + 2 * chunk]) & (tile < span_ref[3 + 2 * chunk]) for chunk in range(rows // CHUNK)
    ]
    every = functools.reduce(lambda x, y: x & y, meets)

    @pl.when(here & every)
    def _():
        work(slice(0, rows))

    for chunk, meet in enumerate(meets):

        @pl.when(here & meet & jnp.logical_not(every))
        def _(chunk=chunk):
            work(slice(chunk * CHUNK, (chunk + 1) * CHUNK))


def weights_kernel(
    span_ref, place_ref, v_place_ref, ends_ref, own_ref, near_ref, far_ref, weight_ref, slope_ref, mine_ref
):
    heads, rows, size = own_ref.shape
    far = is_far(span_ref, place_ref, rows)

    @pl.when(pl.program_id(0) == 0)
    def _():
        mine_ref[...] = own_items(place_ref, ends_ref, rows)

    def work(part):
        positions = tile_of(span_ref) * KEYS + lax.broadcasted_iota(jnp.int32, (1, KEYS), 1)
        same = mine_ref[part, :] == item_of(positions, ends_ref)
        for head in range(heads):
            scores = dot(own_ref[head, part, :], held_at(far, near_ref, far_ref, slice(head * size, (head + 1) * size)))
            half = 1.0 / SHRINK - scores
            square = square_of(half)
            fourth = square * square
            weight = jnp.where(same, fourth * fourth, 0.0)
            weight_ref[0, head, part, :] = weight.astype(BF16)
            slope = weight * lax.rsqrt(square * (half * (1.0 / SHRINK + scores)))
            slope_ref[0, head, part, :] = slope.astype(BF16)

    by_chunks(span_ref, rows, work)


def unit_back(grad, raw):
    scale = lax.rsqrt(jnp.sum(raw * raw, axis=-1, keepdims=True) + NORM_EPS)
    unit = raw * scale
    return scale * (grad - unit * jnp.sum(unit * grad, axis=-1, keepdims=True))


def split_low(wide):
    high = wide.astype(BF16)
    return high, (wide - high.astype(F32)).astype(BF16)


def band_of(taps_row):
    return pltpu.roll(jnp.broadcast_to(taps_row, (EDGE, BAND)), 0, 1, stride=1, stride_axis=0)


def around_of(mine, rim, start):
    return mine[start : start + EDGE, :] == rim[:, start : start + BAND]


def band_sums(taps_ref, head, mine, rim, values):
    band = band_of(taps_ref[head : head + 1, :])
    out = []
    for start in range(0, mine.shape[0], EDGE):
        high, low = split_low(jnp.where(around_of(mine, rim, start), band, 0.0))
        near = values[:, start : start + BAND]
        out.append(dot(high, near, 1, 1) + dot(low, near, 1, 1))
    return jnp.concatenate(out, axis=0)


def rim_values(v_place_ref, sides, own_ref, group):
    index, blocks, rows = v_place_ref[v_place_ref.shape[0] - 1], v_place_ref.shape[0] - 1, own_ref.shape[1]
    ends = []
    for (near_ref, far_ref), beside, part in zip(sides, (-1, 1), (slice(rows - EDGE, rows), slice(0, EDGE))):
        far = v_place_ref[jnp.clip(index + beside, 0, blocks - 1)] >= blocks // 2
        ends.append(jnp.where(far, far_ref[0, group, part], near_ref[0, group, part]))
    return jnp.concatenate([ends[0], own_ref[group, :], ends[1]], axis=1)


def attend_kernel(
    span_ref, place_ref, v_place_ref, ends_ref, weight_ref, v_near_ref, v_far_ref, taps_ref, own_ref,
    before_near_ref, before_far_ref, after_near_ref, after_far_ref, context_ref, raw_ref, v_rim_ref, sum_ref, conv_ref,
):
    heads, rows, size = raw_ref.shape
    far = is_far(span_ref, v_place_ref, rows)

    @pl.when(pl.program_id(0) == 0)
    def _():
        sides = ((before_near_ref, before_far_ref), (after_near_ref, after_far_ref))
        mine, rim = own_items(place_ref, ends_ref, rows), rim_items(place_ref, ends_ref, rows)
        for head in range(heads):
            group = slice(head * size, (head + 1) * size)
            values = rim_values(v_place_ref, sides, own_ref, group)
            v_rim_ref[group, :] = values
            conv_ref[head] = band_sums(taps_ref, head, mine, rim, values)
        sum_ref[...] = jnp.zeros_like(sum_ref)

    def work(part):
        for head in range(heads):
            values = held_at(far, v_near_ref, v_far_ref, slice(head * size, (head + 1) * size))
            sum_ref[head, part, :] += dot(weight_ref[0, head, part, :], values, 1, 1)

    by_chunks(span_ref, rows, work)

    @pl.when(pl.program_id(0) == pl.num_programs(0) - 1)
    def _():
        context = []
        for head in range(heads):
            raw = sum_ref[head]
            raw_ref[head] = raw
            unit = raw * lax.rsqrt(jnp.sum(raw * raw, axis=-1, keepdims=True) + NORM_EPS)
            context.append(unit + conv_ref[head])
        context_ref[...] = jnp.concatenate(context, axis=1).astype(BF16)


def finished(grad, tokens_ref, low_ref, weight_ref, start):
    turned = grad.T.astype(BF16)
    low_ref[...] = grad.astype(BF16)
    weight_ref[start : start + turned.shape[0], :] = dot(turned, tokens_ref[...]).astype(BF16)
    return row_sum(grad.astype(BF16).astype(F32))


def query_back_kernel(
    span_ref, place_ref, v_place_ref, ends_ref, slope_ref, k_near_ref, k_far_ref, v_near_ref, v_far_ref, da_ref, raw_ref,
    tokens_ref, dq_ref, d_w_ref, d_b_ref, sum_ref,
):
    heads, rows, size = raw_ref.shape
    far = is_far(span_ref, place_ref, rows)
    v_far = is_far(span_ref, v_place_ref, rows)

    @pl.when(pl.program_id(0) == 0)
    def _():
        sum_ref[...] = jnp.zeros_like(sum_ref)

    def work(part):
        for head in range(heads):
            group = slice(head * size, (head + 1) * size)
            slope = slope_ref[0, head, part, :].astype(F32)
            d_weights = dot(da_ref[head, part, :], held_at(v_far, v_near_ref, v_far_ref, group))
            d_scores = (d_weights * slope).astype(BF16)
            sum_ref[head, part, :] += dot(d_scores, held_at(far, k_near_ref, k_far_ref, group), 1, 1)

    by_chunks(span_ref, rows, work)

    @pl.when(pl.program_id(0) == pl.num_programs(0) - 1)
    def _():
        grads = [unit_back(sum_ref[head] * SLOPE, raw_ref[head]) for head in range(heads)]
        bias = finished(jnp.concatenate(grads, axis=1), tokens_ref, dq_ref, d_w_ref, 0)
        d_b_ref[...] = jnp.zeros_like(d_b_ref)
        d_b_ref[0:1, : bias.shape[1]] = bias


def key_back_kernel(
    span_ref, place_ref, v_place_ref, ends_ref, weight_ref, slope_ref, q_near_ref, q_far_ref, da_near_ref, da_far_ref, v_ref,
    raw_ref, dv_conv_ref, d_taps_ref, d_b_q_ref, d_w_q_ref, tokens_ref, dk_ref, dv_ref, late_ref, sum_ref, value_ref,
):
    heads, rows, size = raw_ref.shape
    columns = heads * size
    far = is_far(span_ref, place_ref, rows)

    @pl.when(pl.program_id(0) == 0)
    def _():
        sum_ref[...] = jnp.zeros_like(sum_ref)
        value_ref[...] = dv_conv_ref[...]

    def work(part):
        for head in range(heads):
            group = slice(head * size, (head + 1) * size)
            d_attn = held_at(far, da_near_ref, da_far_ref, group)
            slope = slope_ref[0, head, part, :].astype(F32)
            d_scores = (dot(v_ref[head, part, :], d_attn) * slope).astype(BF16)
            sum_ref[head, part, :] += dot(d_scores, held_at(far, q_near_ref, q_far_ref, group), 1, 1)
            value_ref[head, part, :] += dot(weight_ref[0, head, part, :], d_attn, 1, 1)

    by_chunks(span_ref, rows, work)

    @pl.when(pl.program_id(0) == pl.num_programs(0) - 1)
    def _():
        more = 3 * columns
        late_ref[more:, :] = jnp.zeros((late_ref.shape[0] - more, late_ref.shape[1]), BF16)
        late_ref[:columns, :] = d_w_q_ref[...]
        grads = [unit_back(sum_ref[head] * SLOPE, raw_ref[head]) for head in range(heads)]
        finished(jnp.concatenate(grads, axis=1), tokens_ref, dk_ref, late_ref, columns)
        grads = jnp.concatenate([value_ref[head] for head in range(heads)], axis=1)
        bias = finished(grads, tokens_ref, dv_ref, late_ref, 2 * columns)
        late_ref[more : more + 2, :columns] = jnp.concatenate(
            [d_b_q_ref[0:1, :columns], bias], axis=0
        ).astype(BF16)
        late_ref[more + 16 : more + 16 + heads, : d_taps_ref.shape[1]] = d_taps_ref[...].astype(BF16)


def conv_back_kernel(place_ref, ends_ref, taps_ref, values_ref, d_context_ref, turned_ref, dv_ref, d_taps_ref):
    heads, rows, size = d_context_ref.shape
    mine, rim = own_items(place_ref, ends_ref, rows), rim_items(place_ref, ends_ref, rows)
    for head in range(heads):
        group = slice(head * size, (head + 1) * size)
        dv_ref[head] = band_sums(taps_ref, head, mine, rim, turned_ref[group, :])
        values = values_ref[group, :]
        lined = jnp.zeros((8, BAND), F32)
        for start in range(0, rows, EDGE):
            pairs = dot(d_context_ref[head, start : start + EDGE, :], values[:, start : start + BAND])
            pairs = jnp.where(around_of(mine, rim, start), pairs, 0.0)
            for row in range(0, EDGE, 8):
                part = pairs[row : row + 8, :]
                lined = lined + (pltpu.roll(part, BAND - row, 1) if row else part)
        total = lined[0:1, :]
        for row in range(1, 8):
            total = total + pltpu.roll(lined[row : row + 1, :], BAND - row, 1)
        d_taps_ref[head : head + 1, :] = total


def normal_of(u):
    density = jnp.exp(u * u * -0.5) * (1.0 / math.sqrt(2.0 * math.pi))
    ratio = 1.0 / (1.0 + TAIL_AT * jnp.abs(u))
    tail = jnp.full_like(ratio, TAIL[-1])
    for factor in TAIL[-2::-1]:
        tail = tail * ratio + factor
    tail = tail * (ratio * density)
    return jnp.where(u >= 0.0, 1.0 - tail, tail), density


def normed_of(hidden):
    center = hidden - jnp.mean(hidden, axis=-1, keepdims=True)
    scale = lax.rsqrt(jnp.mean(center * center, axis=-1, keepdims=True) + LAYER_EPS)
    return center * scale, scale


def normed_back(grad, normed, scale, gain):
    d_normed = grad * gain
    centered = d_normed - jnp.mean(d_normed, axis=-1, keepdims=True)
    return scale * (centered - normed * jnp.mean(d_normed * normed, axis=-1, keepdims=True))


def row_sum(array):
    return jnp.sum(array, axis=0, keepdims=True)


def middle_kernel(parts, *refs):
    tokens_ref, near_ref, far_ref, vectors_ref, d_out_ref, raw_ref = refs[:6]
    contexts = [half.at[i] for half in (near_ref, far_ref) for i in range(parts // 2)]
    (
        result_ref, d_first_ref, d_early_ref,
        d_context_ref, turned_ref, da_ref, da_turned_ref,
        y_low_ref, act_ref, d_second_low_ref, d_inner_ref, d_first_low_ref,
        normed_ref, scale_ref, mixed_ref, factor_ref, out_ref, up_ref, down_ref, sem_ref,
    ) = refs[6 + 5 * parts :]
    heads, rows, size = raw_ref.shape
    columns = heads * size
    b_out, gain_one, bias_one, b_down, gain_two, bias_two = [vectors_ref[i : i + 1, :] for i in range(6)]
    chunks = [slice(start, start + MIDDLE) for start in range(0, rows, MIDDLE)]
    up_cut, down_cut = up_ref.shape[1] // 3, 2 * down_ref.shape[1] // 3
    targets = [
        (0, 0, up_ref, 0, up_cut),
        (1, 0, up_ref, up_cut, up_ref.shape[1] - up_cut),
        (2, 0, down_ref, 0, down_cut),
        (3, 0, down_ref, down_cut, down_ref.shape[1] - down_cut),
        (4, 0, out_ref, 0, out_ref.shape[1]),
    ]
    copies = [
        [
            pltpu.make_async_copy(
                refs[6 + piece * parts + part].at[first : first + count, :],
                to.at[part, start : start + count, :],
                sem_ref.at[i, part],
            )
            for part in range(parts)
        ]
        for i, (piece, first, to, start, count) in enumerate(targets)
    ]
    copies = copies[-1:] + copies[:-1]
    for of in copies:
        for part in range(parts):
            of[part].start()

    for part in range(parts):
        copies[0][part].wait()
    for chunk in chunks:
        hidden = tokens_ref[chunk, :].astype(F32) + b_out
        for part in range(parts):
            hidden = hidden + dot(contexts[part][chunk, :], out_ref[part, :columns, :])
        normed, scale = normed_of(hidden)
        normed_ref[chunk, :] = normed
        scale_ref[chunk, :] = scale
        first = normed * gain_one + bias_one
        y_low_ref[chunk, :] = first.astype(BF16)
        mixed_ref[chunk, :] = first + b_down

    for part in range(parts):
        for of in copies[1:]:
            of[part].wait()
        b_up = row_sum(out_ref[part, columns : columns + 16, :].astype(F32))
        for chunk in chunks:
            inner = dot(y_low_ref[chunk, :], up_ref[part]) + b_up
            share, density = normal_of(inner)
            act = (inner * share).astype(BF16)
            factor_ref[part, chunk, :] = share + inner * density
            if part == 0:
                act_ref[chunk, :] = act
            mixed_ref[chunk, :] += dot(act, down_ref[part])

    sums = [0.0] * 7
    for chunk in chunks:
        normed, scale = normed_of(mixed_ref[chunk, :])
        result_ref[chunk, :] = (normed * gain_two + bias_two).astype(BF16)
        grad = d_out_ref[chunk, :].astype(F32)
        d_second = normed_back(grad, normed, scale, gain_two)
        d_second_low_ref[chunk, :] = d_second.astype(BF16)
        mixed_ref[chunk, :] = d_second
        for i, array in enumerate((grad * normed, grad, d_second)):
            sums[i] = sums[i] + row_sum(array)

    at_rest = act_ref.shape[1]
    d_early_ref[:at_rest, :] = dot(act_ref[...], d_second_low_ref[...], 0, 0).astype(BF16)
    for part in range(parts):
        for chunk in chunks:
            d_act = dot(d_second_low_ref[chunk, :], down_ref[part], 1, 1)
            d_inner = (d_act * factor_ref[part, chunk, :]).astype(BF16)
            if part == 0:
                d_inner_ref[chunk, :] = d_inner
                sums[6] = sums[6] + row_sum(d_inner.astype(F32))
            mixed_ref[chunk, :] += dot(d_inner, up_ref[part], 1, 1)
        if part == 0:
            d_early_ref[at_rest : at_rest + y_low_ref.shape[1], :] = dot(y_low_ref[...], d_inner_ref[...], 0, 0).astype(BF16)

    for chunk in chunks:
        grad = mixed_ref[chunk, :]
        normed = normed_ref[chunk, :]
        d_first = normed_back(grad, normed, scale_ref[chunk, :], gain_one)
        d_first_ref[chunk, :] = d_first
        d_first_low = d_first.astype(BF16)
        d_first_low_ref[chunk, :] = d_first_low
        for i, array in enumerate((grad * normed, grad, d_first)):
            sums[3 + i] = sums[3 + i] + row_sum(array)
        d_context = dot(d_first_low, out_ref[0, :columns, :], 1, 1).astype(BF16).astype(F32)
        turned_ref[:, chunk] = d_context.T.astype(BF16)
        grads = []
        for head in range(heads):
            grad = d_context[:, head * size : (head + 1) * size]
            d_context_ref[head, chunk, :] = grad.astype(BF16)
            grad = unit_back(grad, raw_ref[head, chunk, :])
            da_ref[head, chunk, :] = grad.astype(BF16)
            grads.append(grad)
        da_turned_ref[:, chunk] = jnp.concatenate(grads, axis=1).T.astype(BF16)
    at_out = at_rest + y_low_ref.shape[1]
    d_early_ref[at_out : at_out + columns, :] = dot(contexts[0][...], d_first_low_ref[...], 0, 0).astype(BF16)
    sums.append(jnp.zeros((57, sums[0].shape[1]), F32))
    d_early_ref[at_out + columns :, :] = jnp.concatenate(sums, axis=0).astype(BF16)


def whole_of(upper_ref, own, got):
    upper = upper_ref[0] != 0
    return jnp.concatenate([jnp.where(upper, got, own), jnp.where(upper, own, got)], axis=0).astype(F32)


def late_results_kernel(upper_ref, late_ref, got_ref, d_w_ref, d_b_ref, d_taps_ref):
    late = whole_of(upper_ref, late_ref[...], got_ref[...])
    columns = d_w_ref.shape[1]
    for i in range(3):
        d_w_ref[i] = late[i * columns : (i + 1) * columns, :]
    more = 3 * columns
    d_b_ref[...] = late[more : more + 2, :columns]
    heads, kernel = d_taps_ref.shape
    start = EDGE - (kernel - 1) // 2
    d_taps_ref[...] = late[more + 16 : more + 16 + heads, start : start + kernel]


def results_kernel(
    upper_ref, early_ref, got_ref, d_out_ref, vectors_ref, d_up_ref, d_down_ref
):
    columns = d_out_ref.shape[0]
    early = whole_of(upper_ref, early_ref[...], got_ref[...])
    d_down_ref[...] = early[: d_down_ref.shape[0], :]
    rest = early[d_down_ref.shape[0] :, :]
    at_out = d_up_ref.shape[0]
    d_up_ref[...] = rest[:at_out, :]
    d_out_ref[...] = rest[at_out : at_out + columns, :]
    vectors_ref[...] = rest[at_out + columns : at_out + columns + 16, :]


HEAD = 64


def per_device(
    tokens, item_lengths, w_qkv, b_qv, taps, w_out, b_out, ln1_gain, ln1_bias, w_up, b_up, w_down, b_down,
    ln2_gain, ln2_bias, d_out,
):
    rows, features = tokens.shape
    heads, kernel = taps.shape
    radius = (kernel - 1) // 2
    columns = w_qkv.shape[2]
    size = columns // heads
    hidden = w_up.shape[1]
    blocks = lax.axis_size("seq")
    total = blocks * rows
    index = lax.axis_index("seq").astype(jnp.int32)
    first_row = index * rows
    shape = jax.ShapeDtypeStruct
    heads_wide, heads_low = shape((heads, rows, size), F32), shape((heads, rows, size), BF16)
    turned_shape, row_shape = shape((columns, rows), BF16), shape((rows, columns), BF16)
    wide_shape, low_shape = shape((rows, features), F32), shape((rows, features), BF16)

    w_turned = jnp.swapaxes(w_qkv, 1, 2)
    biases = jnp.stack([b_qv[0], jnp.zeros_like(b_qv[0]), b_qv[1]])[:, :, None]

    def project(x, which, unit, outs, *flags):
        return call(
            functools.partial(project_kernel, unit, *flags), outs, x, w_turned, biases[which],
            grid=(1,),
            in_specs=[None, pl.BlockSpec((1, columns, features), lambda *_: (which, 0, 0)), None],
            flops=2 * rows * columns * features,
        )

    masks = masks_of("seq")
    v_masks = masks[-1:] + masks[:-1]
    ahead = [(i, i + 1) for i in range(blocks - 1)]
    behind = [(i + 1, i) for i in range(blocks - 1)]

    reach = EDGE - radius

    def rims_of(turned):
        ends = turned[:, rows - EDGE :], turned[:, :EDGE]
        return [lax.ppermute(end, "seq", pairs) for end, pairs in zip(ends, (ahead, behind))]

    reach = EDGE - radius

    steps = min(total, WINDOW) // KEYS
    per = rows // KEYS
    at_of = lambda i, span_ref: span_ref[0] + jnp.minimum(i, span_ref[1] - 1)
    tile_spec = pl.BlockSpec(
        (1, heads, rows, KEYS), lambda i, span_ref, *_: (jnp.minimum(i, span_ref[1] - 1), 0, 0, 0)
    )
    half = blocks // 2

    def halves_of(which):
        def spec(index_of):
            return pl.BlockSpec(
                (1, columns, KEYS),
                lambda i, *refs: (index_of(refs[which][at_of(i, refs[0]) // per]), 0, at_of(i, refs[0]) % per),
            )

        return [spec(lambda place: jnp.minimum(place, half - 1)), spec(lambda place: jnp.maximum(place - half, 0))]

    def side_of(beside):
        def spec(index_of):
            return pl.BlockSpec(
                (1, columns, rows),
                lambda i, *refs: (index_of(refs[2][jnp.clip(refs[2][blocks] + beside, 0, blocks - 1)]), 0, 0),
            )

        return [spec(lambda place: jnp.minimum(place, half - 1)), spec(lambda place: jnp.maximum(place - half, 0))]

    placed, v_placed = halves_of(1), halves_of(2)
    ordered = pl.BlockSpec((1, columns, KEYS), lambda i, *refs: (at_of(i, refs[0]) // per, 0, at_of(i, refs[0]) % per))
    tiles = shape((steps, heads, rows, KEYS), BF16)
    sums = pltpu.VMEM((heads, rows, size), F32)
    pair_flops = 2 * rows * (total // 2) * columns

    def tables(item_lengths):
        count = item_lengths.shape[0]
        upto = jnp.arange(count)[None, :] <= jnp.arange(count)[:, None]
        ends = jnp.sum(jnp.where(upto, item_lengths[None, :], 0), axis=1)
        starts = first_row + CHUNK * jnp.arange(rows // CHUNK, dtype=jnp.int32)[:, None]
        lows = jnp.max(jnp.where(ends[None, :] <= starts, ends[None, :], 0), axis=1)
        highs = jnp.min(jnp.where(ends[None, :] >= starts + CHUNK, ends[None, :], total), axis=1)
        bounds = jnp.stack([lows // KEYS, (highs + KEYS - 1) // KEYS], axis=1)
        span = jnp.concatenate(
            [jnp.stack([bounds[0, 0], bounds[-1, 1] - bounds[0, 0]]), bounds.reshape(-1)]
        ).astype(jnp.int32)
        place, v_place = [jnp.concatenate([block_places("seq", order), index[None]]) for order in (masks, v_masks)]
        return span, place, v_place, ends

    small = taps, [b_out, ln1_gain, ln1_bias, b_down, ln2_gain, ln2_bias]
    [k_turned] = project(tokens, 1, True, [turned_shape], False, False, True)
    k_got = flipped(k_turned, "seq", masks[0])
    far, close = masks_of("mp")
    b_high = lax.reduce_precision(b_up, 8, 7)
    b_mid = lax.reduce_precision(b_up - b_high, 8, 7)
    b_split = jnp.stack([b_high, b_mid, b_up - b_high - b_mid]).astype(BF16)
    w_out_more = jnp.concatenate([w_out, b_split, jnp.zeros((13, features), BF16)])
    up_cut, down_cut = w_up.shape[0] // 3, 2 * w_down.shape[0] // 3
    own = [w_up[:up_cut], w_up[up_cut:], w_down[:down_cut], w_down[down_cut:], w_out_more]
    far_got, last_got = [None] * 5, [None] * 5
    close_got = [flipped(after(array, k_turned), "mp", close) for array in own[:2]]
    k_got, late_tokens, late_lengths, own, close_got = joined(k_got, tokens, item_lengths, own, close_got)
    k_cells = stacked(k_turned, k_got)
    k_got = flipped(k_cells, "seq", masks[1])
    late_tokens, late_lengths, own = after((late_tokens, late_lengths, own), k_cells)
    v_own, v_turned = project(late_tokens, 2, False, [heads_low, turned_shape], False, True, True)
    v_got = flipped(v_turned, "seq", v_masks[0])
    far_got[0] = flipped(own[0], "mp", far)
    q_raw, q_own, q_turned = project(late_tokens, 0, True, [heads_wide, heads_low, turned_shape], True, True, True)
    scalars = tables(late_lengths)
    close_got += [flipped(array, "mp", close) for array in own[2:]]
    k_got, v_got, q_own, scalars, far_got[0], own, late_tokens, small, close_got = joined(
        k_got, v_got, q_own, scalars, far_got[0], own, late_tokens, small, close_got
    )
    k_cells = stacked(k_cells, k_got)
    v_cells = stacked(v_turned, v_got)
    for mask in masks[2:-1]:
        k_got, k_cells = joined(flipped(k_cells, "seq", mask), k_cells)
        k_cells = stacked(k_cells, k_got)
    for mask in v_masks[1:-2]:
        v_got, v_cells = joined(flipped(v_cells, "seq", mask), v_cells)
        v_cells = stacked(v_cells, v_got)
    k_got = flipped(k_cells, "seq", masks[-1])
    v_got = flipped(v_cells, "seq", v_masks[-2])
    own, far_got[0], late_tokens, small = after((own, far_got[0], late_tokens, small), k_cells)
    k_raw, k_own = project(late_tokens, 1, True, [heads_wide, heads_low], True, True, False)
    taps, vectors = small
    vectors = jnp.stack([*vectors, vectors[0], vectors[0]])
    banded = jnp.pad(taps, ((0, 0), (reach, BAND - reach - kernel)))
    mirrored = jnp.pad(taps[:, ::-1], ((0, 0), (reach, BAND - reach - kernel)))
    far_got[1] = flipped(own[1], "mp", far)
    last_got[0] = flipped(far_got[0], "mp", close)
    k_got, v_got, v_cells, far_got[1], last_got[0], own[2], q_own, k_own, k_raw, banded = joined(
        k_got, v_got, v_cells, far_got[1], last_got[0], own[2], q_own, k_own, k_raw, banded
    )
    v_cells = stacked(v_cells, v_got)
    v_got = flipped(v_cells, "seq", v_masks[-1])
    keys = (k_cells, k_got)
    weights, slopes = call(
        weights_kernel, [tiles, tiles], *scalars, q_own, *keys,
        grid=(steps,), scalars=4,
        in_specs=[None, *placed],
        out_specs=[tile_spec, tile_spec],
        flops=8 * pair_flops, scratch=[pltpu.VMEM((rows, 1), jnp.int32)],
    )
    far_got[2], last_got[1] = flipped(own[2], "mp", far), flipped(far_got[1], "mp", close)
    v_got, weights, q_turned, far_got[2], last_got[1], own[3] = joined(
        v_got, weights, q_turned, far_got[2], last_got[1], own[3]
    )
    values = (v_cells, v_got)
    far_got[3], far_got[4] = [flipped(own[piece], "mp", far) for piece in (3, 4)]
    last_got[2] = flipped(far_got[2], "mp", close)
    q_got = flipped(q_turned, "seq", masks[0])
    context, attended, v_rim = call(
        attend_kernel, [row_shape, heads_wide, shape((columns, rows + 2 * EDGE), BF16)],
        *scalars, weights, *values, banded, v_turned, *values, *values,
        grid=(steps,), scalars=4,
        in_specs=[tile_spec, *v_placed, None, None, *side_of(-1), *side_of(1)],
        flops=pair_flops, scratch=[sums, sums],
    )
    q_got, context, far_got[3], far_got[4], last_got[2] = joined(
        q_got, context, far_got[3], far_got[4], last_got[2]
    )
    q_cells = stacked(q_turned, q_got)
    q_got = flipped(q_cells, "seq", masks[1])
    context_got = flipped(context, "mp", far)
    last_got[3], last_got[4] = [flipped(far_got[piece], "mp", close) for piece in (3, 4)]
    parts = 4
    held = [kind[piece] for piece in range(len(own)) for kind in (own, far_got, close_got, last_got)]
    context_got, q_got, q_cells, held = joined(context_got, q_got, q_cells, held)
    q_cells = stacked(q_cells, q_got)
    for mask in masks[2:-1]:
        q_got, q_cells = joined(flipped(q_cells, "seq", mask), q_cells)
        q_cells = stacked(q_cells, q_got)
    q_got = flipped(q_cells, "seq", masks[-1])
    context_cells = stacked(context, context_got)
    contexts = (context_cells, flipped(context_cells, "mp", close))

    vmem = lambda a, *lead: pltpu.VMEM((*lead, *a.shape), a.dtype)
    anywhere = pl.BlockSpec(memory_space=pl.ANY)
    hidden_shape = shape((rows, hidden), BF16)
    (
        layer_output, d_first, d_early, d_context, d_context_turned, da_own, da_turned,
    ) = call(
        functools.partial(middle_kernel, parts),
        [
            low_shape, wide_shape, shape((hidden + features + columns + 64, features), BF16),
            heads_low, turned_shape, heads_low, turned_shape,
        ],
        tokens, *contexts, vectors, d_out, attended, *held,
        grid=(1,),
        in_specs=[None] * 6 + [anywhere] * len(held),
        flops=8 * rows * parts * w_up.size,
        scratch=[
            vmem(low_shape), vmem(hidden_shape), vmem(low_shape), vmem(hidden_shape), vmem(low_shape),
            pltpu.VMEM((rows, features), F32), pltpu.VMEM((rows, 1), F32), pltpu.VMEM((rows, features), F32),
            pltpu.VMEM((parts, rows, hidden), F32), pltpu.VMEM((parts, columns + 16, features), BF16), vmem(w_up, parts), vmem(w_down, parts),
            pltpu.SemaphoreType.DMA((5, parts)),
        ],
    )
    q_got, da_turned, d_context_turned, d_early = joined(q_got, da_turned, d_context_turned, d_early)
    da_got = flipped(da_turned, "seq", masks[0])
    early_kept, early_got = halves_sent(d_early, "seq", masks[-1])
    da_got, da_own, d_context_turned = joined(da_got, da_own, d_context_turned)
    context_rims = rims_of(d_context_turned)
    da_cells = stacked(da_turned, da_got)
    [dq, d_w_q, d_b_q] = call(
        query_back_kernel, [row_shape, shape((columns, features), BF16), shape((16, features), F32)],
        *scalars, slopes, *keys, *values, da_own, q_raw, tokens,
        grid=(steps,), scalars=4,
        in_specs=[tile_spec, *placed, *v_placed, None, None, None],
        flops=3 * pair_flops, scratch=[sums],
    )
    for mask in masks[1:-1]:
        da_got = flipped(da_cells, "seq", mask)
        da_got, dq, k_own, da_cells, early_got, context_rims = joined(
            da_got, dq, k_own, da_cells, early_got, context_rims
        )
        da_cells = stacked(da_cells, da_got)
    da_got = flipped(da_cells, "seq", masks[-1])
    early = Chain(added(early_kept, early_got), "seq", masks_of("seq")[-2::-1])
    early.start()
    k_own = after(k_own, da_cells, early.cells)
    queries = (q_cells, q_got)
    context_rims = after(context_rims, early.cells, da_cells)
    context_rim = jnp.concatenate([context_rims[0], d_context_turned, context_rims[1]], axis=1)
    dv_conv, d_taps_wide = call(
        conv_back_kernel, [heads_wide, shape((heads, BAND), F32)],
        scalars[1], scalars[3], mirrored, v_rim, d_context, context_rim,
        grid=(1,), scalars=2,
        flops=2 * rows * BAND * columns,
    )
    k_own = after(k_own, dv_conv)
    weights_back, slopes_back = call(
        weights_kernel, [tiles, tiles], *scalars, k_own, *queries,
        grid=(steps,), scalars=4,
        in_specs=[None, *placed],
        out_specs=[tile_spec, tile_spec],
        flops=8 * pair_flops, scratch=[pltpu.VMEM((rows, 1), jnp.int32)],
    )
    da_got, weights_back, dv_conv, da_cells = round_end([early], da_got, weights_back, dv_conv, da_cells)
    early.start()
    d_attended = (after(da_cells, early.cells), da_got)
    dk, dv, late = call(
        key_back_kernel, [row_shape, row_shape, shape((3 * columns + 64, features), BF16)],
        *scalars, weights_back, slopes_back, *queries, *d_attended, v_own, k_raw, dv_conv, d_taps_wide, d_b_q, d_w_q, tokens,
        grid=(steps,), scalars=4,
        in_specs=[tile_spec, tile_spec, *placed, *placed] + [None] * 7,
        flops=4 * pair_flops, scratch=[sums, sums],
    )
    late = Chain(late, "seq")
    d_tokens_part = sum(
        jnp.dot(part, w_turned[i], preferred_element_type=F32) for i, part in enumerate((dq, dk, dv))
    )
    token = Chain(d_tokens_part.astype(BF16), "mp")
    late.start()
    token.start()
    round_end([late, token, early])
    while early.left > 1:
        early.start()
        round_end([early])
    early.start()
    [late.cells] = round_end([early], late.cells)
    early_got = flipped(early.cells, "seq", masks[-1])
    late.start()
    token.start()
    while late.left > 1:
        ending = [chain for chain in (late, token) if chain.left]
        if late.left == 2:
            early_got, early.cells = round_end(ending, early_got, early.cells)
        else:
            round_end(ending)
        late.start()
        if token.left:
            token.start()
    d_tokens = (d_first + token.cells.astype(F32)).astype(BF16)
    upper = ((index & masks[-1]) != 0).astype(jnp.int32)[None]
    d_w_out, vectors, d_w_up, d_w_down = call(
        results_kernel,
        [shape(w_out.shape, F32), shape((16, features), F32), shape(w_up.shape, F32), shape(w_down.shape, F32)],
        upper, early.cells, early_got,
        grid=(1,), scalars=1,
    )
    d_w_qkv, d_b_qv, d_taps = call(
        late_results_kernel,
        [shape((3, columns, features), F32), shape((2, columns), F32), shape((heads, kernel), F32)],
        upper, late.cells, after(late.got, d_w_up),
        grid=(1,), scalars=1,
    )
    d_ln2_gain, d_ln2_bias, d_b_down, d_ln1_gain, d_ln1_bias, d_b_out, d_b_up = [vectors[i] for i in range(7)]
    return (
        layer_output, d_tokens, jnp.swapaxes(d_w_qkv, 1, 2), d_b_qv, d_taps, d_w_out, d_b_out, d_ln1_gain,
        d_ln1_bias, d_w_up, d_b_up, d_w_down, d_b_down, d_ln2_gain, d_ln2_bias,
    )


def solution(mesh):
    placed = (
        P("seq", None), P(), P(None, None, "mp"), P(None, "mp"), P("mp", None), P("mp", None), P(), P(), P(),
        P(None, "mp"), P("mp"), P("mp", None), P(), P(), P(), P("seq", None),
    )
    given = (
        P("seq", None), P("seq", None), P(None, None, "mp"), P(None, "mp"), P("mp", None), P("mp", None), P(),
        P(), P(), P(None, "mp"), P("mp"), P("mp", None), P(), P(), P(),
    )
    return jax.shard_map(per_device, mesh=mesh, in_specs=placed, out_specs=given, check_vma=False)
```
